32 devices in a mesh: grp: 2 (over y), seq: 4 (over x, core), head: 4 (over z).
Axes of the slice: x: 2, y: 2, z: 4, core: 2. Of those that a mesh axis runs over, the one named last changes fastest.
Arguments:
- queries: bfloat16 [2048, 8192], P(('grp', 'seq'), 'head'), parts along dimension 0, may hold values from -6 to 6
- key_vecs: bfloat16 [2048, 1024], P(('grp', 'seq'), 'head'), parts along dimension 0, may hold values from -6 to 6
- value_vecs: bfloat16 [2048, 1024], P(('grp', 'seq'), 'head'), parts along dimension 0, may hold values from -4.5 to 4.5
- teacher_out: bfloat16 [2048, 8192], P(('grp', 'seq'), 'head'), parts along dimension 0, may hold values from -4.5 to 4.5
- map_query: bfloat16 [128, 128], replicated, may hold values from -25 to 25
- map_key: bfloat16 [128, 128], replicated, may hold values from -25 to 25
Outputs:
- grad_query: bfloat16 [2048, 8192], P(('grp', 'seq'), 'head'), parts along dimension 0
- grad_key: bfloat16 [2048, 1024], P(('grp', 'seq'), 'head'), parts along dimension 0
- grad_value: bfloat16 [2048, 1024], P(('grp', 'seq'), 'head'), parts along dimension 0
- grad_map_query: float32 [256, 128], P('grp'), parts along dimension 0
- grad_map_key: float32 [256, 128], P('grp'), parts along dimension 0
The draws below stay inside these ranges and needn't reach their ends.
There are 2 independent parts, one for each index of `grp`. The reference program is written for one: setup_inputs(seed, part) draws one part's arguments, and reference() takes and returns one part's arrays. A program takes and returns all parts, laid end to end along the dimension named above; an argument that names none is the same for every part. Nothing has to cross between parts.
All inputs are finite; a program needn't handle non-finite values.
Results may differ from the reference program's by a relative error of at most 0.006.
Values may be sent and summed in bfloat16 or wider, within the bound.
A program may use at most 128 MiB of HBM per device.

```python
import math
import jax
import jax.numpy as jnp
from jax import lax

QH = 64
KVH = 8
DH = 128
HALF = 128
WIN = 64
TOK_DEV = 256
TOKENS = 1024


def draw_queries(key, part):
    base_draw = jnp.clip(jax.random.normal(jax.random.fold_in(key, 1), (TOKENS, QH * DH), jnp.float32), -5.0, 5.0)
    return base_draw.astype(jnp.bfloat16)


def draw_key_vecs(key, part):
    base_draw = jnp.clip(jax.random.normal(jax.random.fold_in(key, 2), (TOKENS, KVH * DH), jnp.float32), -5.0, 5.0)
    return base_draw.astype(jnp.bfloat16)


def region_draw(key, salt, columns):
    span = TOK_DEV // 4
    offsets = jax.random.uniform(jax.random.fold_in(key, salt), (TOKENS // span, columns), jnp.float32, -1.5, 1.5)
    noise = jnp.clip(jax.random.normal(jax.random.fold_in(key, salt + 1), (TOKENS, columns), jnp.float32), -3.0, 3.0)
    return (noise + jnp.repeat(offsets, span, axis=0)).astype(jnp.bfloat16)


def draw_value_vecs(key, part):
    return region_draw(key, 21, KVH * DH)


def draw_teacher_out(key, part):
    return region_draw(key, 31, QH * DH)


def map_draw(key, salt):
    low_end, high_end = (0.03, 0.3)
    column_scale = jnp.exp(jax.random.uniform(jax.random.fold_in(key, salt), (1, HALF), jnp.float32, math.log(low_end), math.log(high_end)))
    entries = jnp.clip(jax.random.normal(jax.random.fold_in(key, salt + 1), (DH, HALF), jnp.float32), -4.0, 4.0)
    return (entries * column_scale).astype(jnp.bfloat16)


def draw_map_query(key, part):
    return map_draw(key, 41)


def draw_map_key(key, part):
    return map_draw(key, 51)


def setup_inputs(seed: int = 0, part: int = 0) -> dict:
    arg_keys = jax.random.split(jax.random.key(seed), 7)
    part_keys = jax.random.split(jax.random.fold_in(arg_keys[6], part), 7)
    queries = draw_queries(jax.random.fold_in(jax.random.fold_in(arg_keys[6], part), 71), part)
    key_vecs = draw_key_vecs(jax.random.fold_in(jax.random.fold_in(arg_keys[6], part), 71), part)
    value_vecs = draw_value_vecs(jax.random.fold_in(jax.random.fold_in(arg_keys[6], part), 71), part)
    teacher_out = draw_teacher_out(jax.random.fold_in(jax.random.fold_in(arg_keys[6], part), 71), part)
    map_query = draw_map_query(jax.random.fold_in(arg_keys[6], 71), part)
    map_key = draw_map_key(jax.random.fold_in(arg_keys[6], 71), part)
    return {"queries": queries, "key_vecs": key_vecs, "value_vecs": value_vecs, "teacher_out": teacher_out, "map_query": map_query, "map_key": map_key}


block_rows = 128
highest = lax.Precision.HIGHEST

def to_wide(source):
    return source.astype(jnp.float32)

def feature_map(inputs, weight):
    logits = jnp.einsum('...d,df->...f', to_wide(inputs), to_wide(weight))
    features = jnp.concatenate([jax.nn.softmax(logits, axis=-1), jax.nn.softmax(-logits, axis=-1)], axis=-1)
    return (logits, features)

def feature_grad(logits, grad_features):
    half_size = logits.shape[-1]
    upper_soft = jax.nn.softmax(logits, axis=-1)
    lower_soft = jax.nn.softmax(-logits, axis=-1)
    grad_upper = grad_features[..., :half_size]
    grad_lower = grad_features[..., half_size:]
    part_upper = upper_soft * (grad_upper - lax.optimization_barrier(jnp.sum(upper_soft * grad_upper, axis=-1, keepdims=True)))
    part_lower = lower_soft * (grad_lower - lax.optimization_barrier(jnp.sum(lower_soft * grad_lower, axis=-1, keepdims=True)))
    return (part_upper - part_lower).astype(jnp.bfloat16)

def window_blocks(source):
    block_count = (source.shape[0] - WIN) // WIN
    earlier = source[:-WIN].reshape((block_count, WIN) + source.shape[1:])
    current = source[WIN:].reshape((block_count, WIN) + source.shape[1:])
    return jnp.concatenate([earlier, current], axis=1)

def window_unblock(blocks):
    block_count = blocks.shape[0]
    earlier = blocks[:, :WIN].reshape((block_count * WIN,) + blocks.shape[2:])
    current = blocks[:, WIN:].reshape((block_count * WIN,) + blocks.shape[2:])
    pad_rows = jnp.zeros((WIN,) + blocks.shape[2:], blocks.dtype)
    return jnp.concatenate([earlier, pad_rows], axis=0) + jnp.concatenate([pad_rows, current], axis=0)

def window_allowed(key_valid):
    valid_blocks = window_blocks(key_valid)
    offset_query = jnp.arange(WIN)[:, None]
    offset_key = jnp.arange(2 * WIN)[None, :]
    inside = (offset_key > offset_query) & (offset_key <= offset_query + WIN)
    return inside[None, None, None] & valid_blocks[:, None, None, None, :]

def window_forward(queries, keys_ext, values_ext, key_valid):
    block_count = queries.shape[0] // WIN
    query_blocks = queries.reshape((block_count, WIN) + queries.shape[1:])
    key_blocks = window_blocks(keys_ext)
    value_blocks = window_blocks(values_ext)
    score_scale = queries.shape[-1] ** (-0.5)
    scores = jnp.einsum('bahgd,behd->bhgae', to_wide(query_blocks), to_wide(key_blocks)) * score_scale
    scores = jnp.where(window_allowed(key_valid), scores, -jnp.inf)
    row_max = lax.optimization_barrier(jnp.max(scores, axis=-1, keepdims=True))
    weights = jnp.exp(scores - row_max)
    probabilities = weights / lax.optimization_barrier(jnp.sum(weights, axis=-1, keepdims=True))
    probs_low = probabilities.astype(jnp.bfloat16)
    window_mix = jnp.einsum('bhgae,behd->bahgd', to_wide(probs_low), to_wide(value_blocks))
    return (window_mix.reshape(queries.shape), probabilities)

def window_backward(queries, keys_ext, values_ext, probabilities, grad_out):
    block_count = queries.shape[0] // WIN
    query_blocks = queries.reshape((block_count, WIN) + queries.shape[1:])
    grad_blocks = grad_out.reshape((block_count, WIN) + grad_out.shape[1:])
    key_blocks = window_blocks(keys_ext)
    value_blocks = window_blocks(values_ext)
    score_scale = queries.shape[-1] ** (-0.5)
    probs_low = probabilities.astype(jnp.bfloat16)
    grad_values = jnp.einsum('bhgae,bahgd->behd', to_wide(probs_low), to_wide(grad_blocks))
    grad_probs = jnp.einsum('bahgd,behd->bhgae', to_wide(grad_blocks), to_wide(value_blocks))
    grad_scores = probabilities * (grad_probs - lax.optimization_barrier(jnp.sum(probabilities * grad_probs, axis=-1, keepdims=True))) * score_scale
    scores_low = grad_scores.astype(jnp.bfloat16)
    grad_queries = jnp.einsum('bhgae,behd->bahgd', to_wide(scores_low), to_wide(key_blocks))
    grad_keys = jnp.einsum('bhgae,bahgd->behd', to_wide(scores_low), to_wide(query_blocks))
    return (grad_queries.reshape(queries.shape), window_unblock(grad_keys), window_unblock(grad_values))

def split_blocks(source):
    block_count = source.shape[0] // block_rows
    return source.reshape((block_count, block_rows) + source.shape[1:])

def lower_mask():
    index_rows = jnp.arange(block_rows)
    return index_rows[:, None] >= index_rows[None, :]

def prefix_before(totals):
    running = jnp.cumsum(totals, axis=0)
    return jnp.concatenate([jnp.zeros_like(totals[:1]), running[:-1]], axis=0)

def suffix_after(totals):
    running = jnp.cumsum(totals[::-1], axis=0)[::-1]
    return jnp.concatenate([running[1:], jnp.zeros_like(totals[:1])], axis=0)

def linear_totals(features_key, values_lag):
    fk_blocks = split_blocks(features_key)
    val_blocks = split_blocks(to_wide(values_lag))
    state_blocks = jnp.einsum('behf,behd->bhfd', fk_blocks, val_blocks, precision=highest)
    norm_blocks = lax.optimization_barrier(jnp.sum(fk_blocks, axis=1))
    return (state_blocks, norm_blocks)

def linear_forward(features_query, features_key, values_lag, state_blocks, norm_blocks, state_in, norm_in):
    fq_blocks = split_blocks(features_query)
    fk_blocks = split_blocks(features_key)
    val_blocks = split_blocks(to_wide(values_lag))
    state_start = state_in[None] + prefix_before(state_blocks)
    norm_start = norm_in[None] + prefix_before(norm_blocks)
    causal = lower_mask()

    def one_block(pieces):
        fq_piece, fk_piece, val_piece, state_piece, norm_piece = pieces
        kernel = jnp.einsum('ahgf,ehf->hgae', fq_piece, fk_piece, precision=highest)
        kernel = jnp.where(causal, kernel, 0.0)
        numerator = jnp.einsum('ahgf,hfd->ahgd', fq_piece, state_piece, precision=highest)
        numerator = numerator + jnp.einsum('hgae,ehd->ahgd', kernel, val_piece, precision=highest)
        denominator = jnp.einsum('ahgf,hf->ahg', fq_piece, norm_piece, precision=highest)
        denominator = denominator + jnp.transpose(lax.optimization_barrier(jnp.sum(kernel, axis=-1)), (2, 0, 1))
        return (numerator, denominator)
    numerator, denominator = lax.map(one_block, (fq_blocks, fk_blocks, val_blocks, state_start, norm_start))
    numerator = numerator.reshape(features_query.shape[:-1] + (values_lag.shape[-1],))
    denominator = denominator.reshape(features_query.shape[:-1])
    return (numerator, denominator, state_start, norm_start)

def back_totals(features_query, grad_numer, grad_denom):
    fq_blocks = split_blocks(features_query)
    gn_blocks = split_blocks(grad_numer)
    gd_blocks = split_blocks(grad_denom)
    back_state = jnp.einsum('bahgf,bahgd->bhfd', fq_blocks, gn_blocks, precision=highest)
    back_norm = jnp.einsum('bahgf,bahg->bhf', fq_blocks, gd_blocks, precision=highest)
    return (back_state, back_norm)

def linear_backward(features_query, features_key, values_lag, state_start, norm_start, grad_numer, grad_denom, back_state, back_norm, after_in, after_norm_in):
    fq_blocks = split_blocks(features_query)
    fk_blocks = split_blocks(features_key)
    val_blocks = split_blocks(to_wide(values_lag))
    gn_blocks = split_blocks(grad_numer)
    gd_blocks = split_blocks(grad_denom)
    after_state = after_in[None] + suffix_after(back_state)
    after_norm = after_norm_in[None] + suffix_after(back_norm)
    causal = lower_mask()

    def one_block(pieces):
        fq_piece, fk_piece, val_piece, state_piece, norm_piece, gn_piece, gd_piece, after_piece, after_sum = pieces
        kernel = jnp.where(causal, jnp.einsum('ahgf,ehf->hgae', fq_piece, fk_piece, precision=highest), 0.0)
        grad_kernel = jnp.einsum('ahgd,ehd->hgae', gn_piece, val_piece, precision=highest)
        grad_kernel = jnp.where(causal, grad_kernel + jnp.transpose(gd_piece, (1, 2, 0))[..., None], 0.0)
        grad_fq = jnp.einsum('hfd,ahgd->ahgf', state_piece, gn_piece, precision=highest)
        grad_fq = grad_fq + norm_piece[None, :, None, :] * gd_piece[..., None]
        grad_fq = grad_fq + jnp.einsum('hgae,ehf->ahgf', grad_kernel, fk_piece, precision=highest)
        grad_fk = jnp.einsum('hfd,ehd->ehf', after_piece, val_piece, precision=highest) + after_sum[None]
        grad_fk = grad_fk + jnp.einsum('hgae,ahgf->ehf', grad_kernel, fq_piece, precision=highest)
        grad_val = jnp.einsum('hfd,ehf->ehd', after_piece, fk_piece, precision=highest)
        grad_val = grad_val + jnp.einsum('hgae,ahgd->ehd', kernel, gn_piece, precision=highest)
        return (grad_fq, grad_fk, grad_val)
    grad_fq, grad_fk, grad_val = lax.map(one_block, (fq_blocks, fk_blocks, val_blocks, state_start, norm_start, gn_blocks, gd_blocks, after_state, after_norm))
    return (grad_fq.reshape(features_query.shape), grad_fk.reshape(features_key.shape), grad_val.reshape(values_lag.shape))

def group_grads(queries, keys_in, values_in, teacher, map_query, map_key):
    local_rows = queries.shape[0]
    pad_rows = jnp.zeros((WIN,) + keys_in.shape[1:], keys_in.dtype)
    keys_ext = jnp.concatenate([pad_rows, keys_in], axis=0)
    values_ext = jnp.concatenate([pad_rows, values_in], axis=0)
    key_valid = jnp.arange(local_rows + WIN) >= WIN
    lag_valid = key_valid[:local_rows]
    lag_keys = keys_ext[:local_rows]
    lag_values = values_ext[:local_rows]
    window_mix, probabilities = window_forward(queries, keys_ext, values_ext, key_valid)
    query_logits, features_query = feature_map(queries, map_query)
    key_logits, features_key = feature_map(lag_keys, map_key)
    features_key = jnp.where(lag_valid[:, None, None], features_key, 0.0)
    state_blocks, norm_blocks = linear_totals(features_key, lag_values)
    zero_state = jnp.zeros(state_blocks.shape[1:], jnp.float32)
    zero_norm = jnp.zeros(norm_blocks.shape[1:], jnp.float32)
    numerator, denominator, state_start, norm_start = linear_forward(features_query, features_key, lag_values, state_blocks, norm_blocks, zero_state, zero_norm)
    floored = jnp.where(denominator > 1.0, denominator, 1.0)
    linear_mix = numerator / floored[..., None]
    grad_out = (window_mix + linear_mix - to_wide(teacher)).astype(jnp.bfloat16)
    grad_wide = to_wide(grad_out)
    grad_numer = grad_wide / floored[..., None]
    grad_denom = jnp.where(denominator > 1.0, -lax.optimization_barrier(jnp.sum(grad_wide * linear_mix, axis=-1)) / floored, 0.0)
    back_state, back_norm = back_totals(features_query, grad_numer, grad_denom)
    grad_fq, grad_fk, grad_lag_values = linear_backward(features_query, features_key, lag_values, state_start, norm_start, grad_numer, grad_denom, back_state, back_norm, zero_state, zero_norm)
    grad_fk = jnp.where(lag_valid[:, None, None], grad_fk, 0.0)
    win_queries, win_keys, win_values = window_backward(queries, keys_ext, values_ext, probabilities, grad_out)
    query_logit_grad = feature_grad(query_logits, grad_fq)
    key_logit_grad = feature_grad(key_logits, grad_fk)
    map_part = jnp.einsum('...f,df->...d', to_wide(query_logit_grad), to_wide(map_query))
    lag_key_grad = jnp.einsum('...f,df->...d', to_wide(key_logit_grad), to_wide(map_key))
    grad_map_q = jnp.einsum('ahgd,ahgf->df', to_wide(queries), to_wide(query_logit_grad))
    grad_map_k = jnp.einsum('ahd,ahf->df', to_wide(lag_keys), to_wide(key_logit_grad))
    tail_zero = jnp.zeros((WIN,) + keys_in.shape[1:], jnp.float32)
    grad_queries = (win_queries + map_part).astype(jnp.bfloat16)
    grad_keys = (win_keys[WIN:] + jnp.concatenate([lag_key_grad[WIN:], tail_zero], axis=0)).astype(jnp.bfloat16)
    grad_values = (win_values[WIN:] + jnp.concatenate([grad_lag_values[WIN:], tail_zero], axis=0)).astype(jnp.bfloat16)
    return (grad_queries, grad_keys, grad_values, grad_map_q, grad_map_k)

def reference(queries, key_vecs, value_vecs, teacher_out, map_query, map_key):
    per_group = QH // KVH
    query_heads = jnp.moveaxis(queries.reshape(TOKENS, KVH, 1, per_group, DH), 1, 0)
    key_heads = jnp.moveaxis(key_vecs.reshape(TOKENS, KVH, 1, DH), 1, 0)
    value_heads = jnp.moveaxis(value_vecs.reshape(TOKENS, KVH, 1, DH), 1, 0)
    teacher_heads = jnp.moveaxis(teacher_out.reshape(TOKENS, KVH, 1, per_group, DH), 1, 0)

    def one_group(pieces):
        return group_grads(pieces[0], pieces[1], pieces[2], pieces[3], map_query, map_key)
    grad_q, grad_k, grad_v, grad_mq, grad_mk = lax.map(one_group, (query_heads, key_heads, value_heads, teacher_heads))
    grad_query = jnp.moveaxis(grad_q, 0, 1).reshape(TOKENS, QH * DH)
    grad_key = jnp.moveaxis(grad_k, 0, 1).reshape(TOKENS, KVH * DH)
    grad_value = jnp.moveaxis(grad_v, 0, 1).reshape(TOKENS, KVH * DH)
    return (grad_query, grad_key, grad_value, lax.optimization_barrier(jnp.sum(grad_mq, axis=0)), lax.optimization_barrier(jnp.sum(grad_mk, axis=0)))
```

```python
import functools

import jax
import jax.numpy as jnp
from jax import lax
from jax.experimental import pallas as pl
from jax.experimental.pallas import tpu as pltpu
from jax.sharding import PartitionSpec as P

QH = 64
KVH = 8
DH = 128
WIN = 64
FEAT = 256

f32 = jnp.float32
bf16 = jnp.bfloat16
MESH = pl.DeviceIdType.MESH


def mm(a, b, ca=1, cb=0, precision=None):
    return lax.dot_general(
        a, b, (((ca,), (cb,)), ((), ())), preferred_element_type=f32, precision=precision
    )


def soft_pair(logits):
    top = jnp.max(logits, axis=-1, keepdims=True)
    low = jnp.min(logits, axis=-1, keepdims=True)
    up = jnp.exp(logits - top)
    down = jnp.exp(low - logits)
    up = up * (1.0 / jnp.sum(up, axis=-1, keepdims=True))
    down = down * (1.0 / jnp.sum(down, axis=-1, keepdims=True))
    return up, down


def soft_pair_grad(up, down, ga, gb):
    part_up = up * (ga - jnp.sum(up * ga, axis=-1, keepdims=True))
    part_down = down * (gb - jnp.sum(down * gb, axis=-1, keepdims=True))
    return (part_up - part_down).astype(bf16)


def kernel(
    nseq, nhead, rows, kvl, per,
    q_hbm, k_hbm, v_hbm, t_hbm, mq_hbm, mk_hbm,
    gq_ref, gk_ref, gv_ref, gm_ref,
    q_ref, k_ref, v_ref, t_ref, mq_ref, mk_ref, in_s,
    kx, vx, fkx, fkb, cum, stl, stb, p_scr, fq_scr,
    gfk_acc, dv_acc, dk_acc, bt_acc, bn_acc, gmq_acc, gmk_acc,
    halo_out, halo_in, st_out, st_in, nm_out, nm_in,
    bt_out, bt_in, bn_out, bn_in, hr_out, hr_in, mg, mr, tot,
    halo_s, halo_r, st_s, st_r, nm_s, nm_r, bt_s, bt_r, bn_s, bn_r, hr_s, hr_r,
    mg_s, mr_s, tot_s, tot_r,
):
    nb = rows // WIN
    head_rows = per * WIN
    tail = rows - WIN
    chunks, _, _ = mg.shape
    crows = 2 * DH // chunks
    place = lax.axis_index("seq")
    mine = place * nhead + lax.axis_index("head")
    team = nseq * nhead
    scale = DH ** (-0.5)

    def remote(src, dst, send, recv, device):
        return pltpu.make_async_remote_copy(
            src_ref=src, dst_ref=dst, send_sem=send, recv_sem=recv,
            device_id=device, device_id_type=MESH,
        )

    barrier = pltpu.get_barrier_semaphore()

    def peer(n):
        return {"seq": n // nhead, "head": n % nhead}

    def hail(d, carry):
        pl.semaphore_signal(barrier, inc=1, device_id=peer((mine + d) % team), device_id_type=MESH)
        return carry

    lax.fori_loop(1, team, hail, 0)

    loads = [
        pltpu.make_async_copy(source, held, in_s.at[n])
        for n, (source, held) in enumerate(
            [(k_hbm, k_ref), (v_hbm, v_ref), (mk_hbm, mk_ref), (q_hbm, q_ref), (mq_hbm, mq_ref), (t_hbm, t_ref)]
        )
    ]
    for load in loads:
        load.start()
    for load in loads[:3]:
        load.wait()

    for g in range(kvl):
        cols = slice(g * DH, (g + 1) * DH)
        kx[g, WIN:] = k_ref[:, cols]
        vx[g, WIN:] = v_ref[:, cols]
        halo_out[g] = k_ref[tail:, cols]
        halo_out[kvl + g] = v_ref[tail:, cols]

    pl.semaphore_wait(barrier, team - 1)

    def halo_copy(target):
        return remote(halo_out, halo_in, halo_s, halo_r, {"seq": target})

    @pl.when(place < nseq - 1)
    def _():
        halo_copy(place + 1).start()

    mk = mk_ref[...]
    for g in range(kvl):
        up, down = soft_pair(mm(kx[g, WIN:], mk))
        fk = jnp.concatenate([up, down], axis=-1)
        fkx[g, WIN:] = fk
        fkl = fk.astype(bf16)
        fkb[g, WIN:] = fkl
        early = mm(vx[g, WIN:rows], fkl[:tail], 0, 0)
        late = mm(vx[g, rows:], fkl[tail:], 0, 0)
        st_out[0, g] = early.astype(bf16)
        st_out[1, g] = (early + late).astype(bf16)
        n_early = jnp.sum(fk[:tail].reshape(tail // 8, 8, FEAT), axis=0)
        n_late = jnp.sum(fk[tail:].reshape(WIN // 8, 8, FEAT), axis=0)
        nm_out[0, g] = n_early
        nm_out[1, g] = n_early + n_late

    def state_copies(slot, source, target):
        return (
            remote(st_out.at[slot], st_in.at[source], st_s.at[target], st_r.at[source],
                   {"seq": target}),
            remote(nm_out.at[slot], nm_in.at[source], nm_s.at[target], nm_r.at[source],
                   {"seq": target}),
        )

    @pl.when(place < nseq - 1)
    def _():
        for copy in state_copies(0, place, place + 1):
            copy.start()

    def send_far(target, carry):
        for copy in state_copies(1, place, target):
            copy.start()
        return carry

    lax.fori_loop(place + 2, nseq, send_far, 0)

    @pl.when(place > 0)
    def _():
        halo_copy(place - 1).wait_recv()

    @pl.when(place == 0)
    def _():
        halo_in[...] = jnp.zeros_like(halo_in)

    has_before = (place > 0).astype(f32)
    for g in range(kvl):
        kx[g, :WIN] = halo_in[g]
        vx[g, :WIN] = halo_in[kvl + g]
        up, down = soft_pair(mm(halo_in[g], mk))
        fk = jnp.concatenate([up, down], axis=-1) * has_before
        fkx[g, :WIN] = fk
        fkb[g, :WIN] = fk.astype(bf16)

    ia = lax.broadcasted_iota(jnp.int32, (WIN, 2 * WIN), 0)
    ie = lax.broadcasted_iota(jnp.int32, (WIN, 2 * WIN), 1)
    lag_mask = (ie <= ia)[None]

    def stacked(ref, g, b):
        return jnp.concatenate(
            [
                ref[pl.ds(b * WIN, WIN), pl.ds(pl.multiple_of((g * per + h) * DH, DH), DH)]
                for h in range(per)
            ],
            axis=0,
        )

    def cube(x):
        return x.reshape(per, WIN, x.shape[-1])

    def plain(x):
        return x.reshape(head_rows, x.shape[-1])

    def forward(unit, carry):
        g = unit // nb
        b = unit % nb
        qs = stacked(q_ref, g, b)
        up, down = soft_pair(mm(qs, mq_ref[...]))
        fq_scr[unit, :, :DH] = up
        fq_scr[unit, :, DH:] = down
        kw = kx[g, pl.ds(b * WIN, 2 * WIN)]
        first_key = jnp.where(place > 0, 0, WIN) - b * WIN
        seen = ((ie > ia) & (ie <= ia + WIN) & (ie >= first_key))[None]
        scores = jnp.where(seen, cube(mm(qs, kw, 1, 1)) * scale, -jnp.inf)
        weights = jnp.exp(scores - jnp.max(scores, axis=-1, keepdims=True))
        probs = weights * (1.0 / jnp.sum(weights, axis=-1, keepdims=True))
        p_scr[unit] = plain(probs)
        return carry

    loads[3].wait()
    loads[4].wait()
    lax.fori_loop(0, kvl * nb, forward, 0)

    ra = lax.broadcasted_iota(jnp.int32, (rows, rows), 0)
    re = lax.broadcasted_iota(jnp.int32, (rows, rows), 1)
    lower = (re <= ra).astype(f32)
    for g in range(kvl):
        cum[g] = mm(lower, fkx[g, :rows], precision=lax.Precision.HIGHEST)
        running = jnp.zeros((DH, FEAT), f32)
        for b in range(nb):
            stl[g, b] = running
            if b < nb - 1:
                part = slice(b * WIN, (b + 1) * WIN)
                running = running + mm(vx[g, part], fkb[g, part], 0, 0)

    def take_state(source, carry):
        for copy in state_copies(0, source, source):
            copy.wait_recv()
        for g in range(kvl):
            norm = jnp.sum(nm_in[source, g], axis=0, keepdims=True)
            cum[g] = cum[g] + norm
            state = st_in[source, g].astype(f32)
            for b in range(nb):
                stl[g, b] = stl[g, b] + state
        return carry

    lax.fori_loop(0, place, take_state, 0)
    for g in range(kvl):
        for b in range(nb):
            stb[g, b] = stl[g, b].astype(bf16)

    gmq_acc[...] = jnp.zeros_like(gmq_acc)
    dv_acc[...] = jnp.zeros_like(dv_acc)
    dk_acc[...] = jnp.zeros_like(dk_acc)

    def back_copies(g, source, target):
        return (
            remote(bt_out.at[g], bt_in.at[source, g], bt_s.at[g, target], bt_r.at[g, source],
                   {"seq": target}),
            remote(bn_out.at[g], bn_in.at[source, g], bn_s.at[g, target], bn_r.at[g, source],
                   {"seq": target}),
        )

    def return_copy(g, target):
        return remote(hr_out.at[g], hr_in.at[g], hr_s.at[g], hr_r.at[g], {"seq": target})

    def group(g, carry):
        bt_acc[...] = jnp.zeros_like(bt_acc)
        bn_acc[...] = jnp.zeros_like(bn_acc)

        def block(lap, inner):
            b = nb - 1 - lap
            unit = g * nb + b
            here = pl.ds(b * WIN, WIN)
            span = pl.ds(b * WIN, 2 * WIN)
            qs = stacked(q_ref, g, b)
            fq = fq_scr[unit]
            probs = cube(p_scr[unit])
            cumb = cum[g, here][None]
            kw = kx[g, span]
            vw = vx[g, span]
            fkw = fkb[g, span]
            state = stb[g, b]
            den = jnp.sum(cube(fq) * cumb, axis=-1, keepdims=True)
            above = den > 1.0
            inv = 1.0 / jnp.where(above, den, 1.0)
            fqb = fq.astype(bf16)
            kin = cube(mm(fqb, fkw, 1, 1))
            mixer = plain(jnp.where(lag_mask, kin * inv, probs)).astype(bf16)
            mix = cube(mm(mixer, vw)) + cube(mm(fqb, state, 1, 1)) * inv
            go = plain(mix - cube(stacked(t_ref, g, b).astype(f32))).astype(bf16)
            gp = cube(mm(go, vw, 1, 1))
            ds = probs * (gp - jnp.sum(probs * gp, axis=-1, keepdims=True)) * scale
            ds = plain(ds).astype(bf16)
            gin = plain(jnp.where(lag_mask, gp, 0.0)).astype(bf16)
            gfq = cube(mm(go, state) + mm(gin, fkw)) * inv
            gd = jnp.where(above, -jnp.sum(cube(fq) * gfq, axis=-1, keepdims=True) * inv, 0.0)
            gfq = gfq + gd * cumb
            gker = plain(jnp.where(lag_mask, gp * inv + gd, 0.0)).astype(bf16)
            gfq = plain(gfq)
            dl = soft_pair_grad(fq[:, :DH], fq[:, DH:], gfq[:, :DH], gfq[:, DH:])
            gq = mm(ds, kw) + mm(dl, mq_ref[...], 1, 1)
            gq = gq.astype(bf16)
            for h in range(per):
                gq_ref[here, pl.ds(pl.multiple_of((g * per + h) * DH, DH), DH)] = gq[
                    h * WIN : (h + 1) * WIN
                ]
            qt = mm(qs, jnp.concatenate([dl, ds], axis=-1), 0, 0)
            gmq_acc[...] += qt[:, :DH]
            dk_acc[g, span] += qt[:, DH:].T
            fqn = plain(cube(fq) * inv).astype(bf16)
            gt = mm(go, jnp.concatenate([fqn, mixer], axis=-1), 0, 0)
            dv_acc[g, span] += gt[:, FEAT:].T
            later = bt_acc[...].astype(bf16)
            gfk = mm(gker, fqb, 0, 0)[:WIN] + mm(vw[:WIN], later)
            gfk_acc[g, here] = gfk + jnp.sum(bn_acc[...], axis=0, keepdims=True)
            dv_acc[g, here] += mm(fkw[:WIN], later, 1, 1)
            bt_acc[...] += gt[:, :FEAT]
            bn_acc[...] += jnp.sum(
                plain(cube(fq) * gd).reshape(head_rows // 8, 8, FEAT), axis=0
            )
            return inner

        lax.fori_loop(0, nb, block, 0)
        bt_out[g] = bt_acc[...].astype(bf16)
        bn_out[g] = bn_acc[...]
        hr_out[g, :, :FEAT] = gfk_acc[g, :WIN].astype(bf16)
        hr_out[g, :, FEAT : FEAT + DH] = dv_acc[g, :WIN].astype(bf16)
        hr_out[g, :, FEAT + DH :] = dk_acc[g, :WIN].astype(bf16)

        @pl.when(place > 0)
        def _():
            return_copy(g, place - 1).start()

        def send_back(lap, inner):
            for copy in back_copies(g, place, place - 1 - lap):
                copy.start()
            return inner

        lax.fori_loop(0, place, send_back, 0)
        return carry

    loads[5].wait()
    lax.fori_loop(0, kvl, group, 0)

    def each_peer(visit):
        def one(d, carry):
            visit((mine + d) % team)
            return carry

        lax.fori_loop(1, team, one, 0)

    def each_owner(first, last, visit):
        def one(c, carry):
            @pl.when(c != mine)
            def _():
                visit(c)

            return carry

        lax.fori_loop(first, last, one, 0)

    def part_copy(chunk, source):
        return remote(mg.at[chunk], mr.at[source], mg_s.at[chunk], mr_s.at[source], peer(chunk))

    def total_copy(chunk, target):
        return remote(tot.at[chunk], tot.at[chunk], tot_s.at[target], tot_r.at[chunk], peer(target))

    def scatter(which, part):
        half = chunks // 2
        for c in range(half):
            mg[which * half + c] = part[c * crows : (c + 1) * crows].astype(bf16)
        each_owner(which * half, which * half + half, lambda c: part_copy(c, mine).start())

    scatter(0, gmq_acc[...])

    @pl.when(place == nseq - 1)
    def _():
        hr_in[...] = jnp.zeros_like(hr_in)

    gmk_acc[...] = jnp.zeros_like(gmk_acc)
    for g in range(kvl):
        bt_acc[...] = jnp.zeros_like(bt_acc)
        bn_acc[...] = jnp.zeros_like(bn_acc)

        def take_back(source, carry):
            for copy in back_copies(g, source, source):
                copy.wait_recv()
            bt_acc[...] += bt_in[source, g].astype(f32)
            bn_acc[...] += bn_in[source, g]
            return carry

        lax.fori_loop(place + 2, nseq, take_back, 0)
        far = bt_acc[...].astype(bf16)
        far_norm = jnp.sum(bn_acc[...], axis=0, keepdims=True)

        @pl.when(place < nseq - 1)
        def _():
            take_back(place + 1, 0)
            return_copy(g, place + 1).wait_recv()

        near = bt_acc[...].astype(bf16)
        near_norm = jnp.sum(bn_acc[...], axis=0, keepdims=True)
        gfk = jnp.concatenate(
            [
                gfk_acc[g, WIN:] + mm(vx[g, WIN:rows], near) + near_norm,
                hr_in[g, :, :FEAT].astype(f32) + mm(vx[g, rows:], far) + far_norm,
            ],
            axis=0,
        )
        gv = jnp.concatenate(
            [
                dv_acc[g, WIN:rows] + mm(fkb[g, WIN:rows], near, 1, 1),
                dv_acc[g, rows:]
                + hr_in[g, :, FEAT : FEAT + DH].astype(f32)
                + mm(fkb[g, rows:], far, 1, 1),
            ],
            axis=0,
        )
        dk = jnp.concatenate(
            [dk_acc[g, WIN:rows], dk_acc[g, rows:] + hr_in[g, :, FEAT + DH :].astype(f32)], axis=0
        )
        dl = soft_pair_grad(
            fkx[g, WIN:, :DH], fkx[g, WIN:, DH:], gfk[:, :DH], gfk[:, DH:]
        )
        cols = slice(g * DH, (g + 1) * DH)
        gk_ref[:, cols] = (dk + mm(dl, mk, 1, 1)).astype(bf16)
        gv_ref[:, cols] = gv.astype(bf16)
        gmk_acc[...] += mm(kx[g, WIN:], dl, 0, 0)

    scatter(1, gmk_acc[...])

    @pl.when(mine < chunks)
    def _():
        each_peer(lambda d: part_copy(mine, d).wait_recv())
        mr[mine] = mg[mine]
        part = mr[0].astype(f32)
        for d in range(1, team):
            part = part + mr[d].astype(f32)
        tot[mine] = part.astype(bf16)
        each_peer(lambda d: total_copy(mine, d).start())

    each_owner(0, chunks, lambda c: total_copy(c, mine).wait_recv())
    for c in range(chunks):
        gm_ref[c * crows : (c + 1) * crows] = tot[c].astype(f32)

    @pl.when(place < nseq - 1)
    def _():
        halo_copy(place + 1).wait_send()
        for copy in state_copies(0, place, place + 1):
            copy.wait_send()

    def far_sent(target, carry):
        for copy in state_copies(1, place, target):
            copy.wait_send()
        return carry

    lax.fori_loop(place + 2, nseq, far_sent, 0)

    for g in range(kvl):

        @pl.when(place > 0)
        def _():
            return_copy(g, place - 1).wait_send()

        def back_sent(lap, carry):
            for copy in back_copies(g, place, place - 1 - lap):
                copy.wait_send()
            return carry

        lax.fori_loop(0, place, back_sent, 0)

    each_owner(0, chunks, lambda c: part_copy(c, mine).wait_send())

    @pl.when(mine < chunks)
    def _():
        each_peer(lambda d: total_copy(mine, d).wait_send())


def hand_over(gq, gk, gv, gm, gq_out, gk_out, gv_out, gmq_out, gmk_out, put):
    writes = []
    for held, target in [(gq, gq_out), (gk, gk_out), (gv, gv_out), (gm.at[:DH], gmq_out), (gm.at[DH:], gmk_out)]:
        write = pltpu.make_async_copy(held, target, put.at[len(writes)])
        write.start()
        writes.append(write)
    for write in writes:
        write.wait()


def shards(nseq, nhead, queries, key_vecs, value_vecs, teacher_out, map_query, map_key):
    rows = queries.shape[0]
    kvl = key_vecs.shape[1] // DH
    per = QH // KVH
    nb = rows // WIN
    units = kvl * nb
    team = nseq * nhead
    chunks = min(team, 2 * DH // 16)
    crows = 2 * DH // chunks
    vm = pltpu.VMEM
    dma = pltpu.SemaphoreType.DMA
    scratch = [
        vm(queries.shape, bf16),
        vm(key_vecs.shape, bf16),
        vm(value_vecs.shape, bf16),
        vm(queries.shape, bf16),
        vm(map_query.shape, bf16),
        vm(map_key.shape, bf16),
        dma((6,)),
        vm((kvl, rows + WIN, DH), bf16),
        vm((kvl, rows + WIN, DH), bf16),
        vm((kvl, rows + WIN, FEAT), f32),
        vm((kvl, rows + WIN, FEAT), bf16),
        vm((kvl, rows, FEAT), f32),
        vm((kvl, nb, DH, FEAT), f32),
        vm((kvl, nb, DH, FEAT), bf16),
        vm((units, per * WIN, 2 * WIN), f32),
        vm((units, per * WIN, FEAT), f32),
        vm((kvl, rows, FEAT), f32),
        vm((kvl, rows + WIN, DH), f32),
        vm((kvl, rows + WIN, DH), f32),
        vm((DH, FEAT), f32),
        vm((8, FEAT), f32),
        vm((DH, DH), f32),
        vm((DH, DH), f32),
        vm((2 * kvl, WIN, DH), bf16),
        vm((2 * kvl, WIN, DH), bf16),
        vm((2, kvl, DH, FEAT), bf16),
        vm((nseq, kvl, DH, FEAT), bf16),
        vm((2, kvl, 8, FEAT), f32),
        vm((nseq, kvl, 8, FEAT), f32),
        vm((kvl, DH, FEAT), bf16),
        vm((nseq, kvl, DH, FEAT), bf16),
        vm((kvl, 8, FEAT), f32),
        vm((nseq, kvl, 8, FEAT), f32),
        vm((kvl, WIN, FEAT + 2 * DH), bf16),
        vm((kvl, WIN, FEAT + 2 * DH), bf16),
        vm((chunks, crows, DH), bf16),
        vm((team, crows, DH), bf16),
        vm((chunks, crows, DH), bf16),
        dma, dma,
        dma((nseq,)), dma((nseq,)), dma((nseq,)), dma((nseq,)),
        dma((kvl, nseq)), dma((kvl, nseq)), dma((kvl, nseq)), dma((kvl, nseq)),
        dma((kvl,)), dma((kvl,)),
        dma((chunks,)), dma((team,)), dma((team,)), dma((chunks,)),
    ]
    whole = pl.BlockSpec(memory_space=pltpu.VMEM)
    anywhere = pl.BlockSpec(memory_space=pl.ANY)
    queries, key_vecs, value_vecs, teacher_out, map_query, map_key = (
        pltpu.with_memory_space_constraint(x, pltpu.HBM)
        for x in (queries, key_vecs, value_vecs, teacher_out, map_query, map_key)
    )
    results = pl.pallas_call(
        functools.partial(kernel, nseq, nhead, rows, kvl, per),
        out_shape=(
            vm(queries.shape, bf16),
            vm(key_vecs.shape, bf16),
            vm(value_vecs.shape, bf16),
            vm((2 * DH, DH), f32),
        ),
        in_specs=[anywhere] * 6,
        out_specs=[whole, whole, whole, whole],
        scratch_shapes=scratch,
        compiler_params=pltpu.CompilerParams(
            collective_id=0, has_side_effects=True, vmem_limit_bytes=32 * 1024 * 1024
        ),
        name="transfer_step",
    )(queries, key_vecs, value_vecs, teacher_out, map_query, map_key)
    return pl.pallas_call(
        hand_over,
        out_shape=(
            jax.ShapeDtypeStruct(queries.shape, bf16),
            jax.ShapeDtypeStruct(key_vecs.shape, bf16),
            jax.ShapeDtypeStruct(value_vecs.shape, bf16),
            jax.ShapeDtypeStruct((DH, DH), f32),
            jax.ShapeDtypeStruct((DH, DH), f32),
        ),
        in_specs=[whole] * 4,
        out_specs=[anywhere] * 5,
        scratch_shapes=[dma((5,))],
        compiler_params=pltpu.CompilerParams(vmem_limit_bytes=1024 * 1024),
        name="hand_over",
    )(*results)


def solution(mesh):
    in_specs = (
        P(("grp", "seq"), "head"),
        P(("grp", "seq"), "head"),
        P(("grp", "seq"), "head"),
        P(("grp", "seq"), "head"),
        P(),
        P(),
    )
    out_specs = (
        P(("grp", "seq"), "head"),
        P(("grp", "seq"), "head"),
        P(("grp", "seq"), "head"),
        P("grp", None),
        P("grp", None),
    )
    body = functools.partial(shards, mesh.shape["seq"], mesh.shape["head"])
    return jax.shard_map(body, mesh=mesh, in_specs=in_specs, out_specs=out_specs, check_vma=False)
```

```python
import functools

import jax
import jax.numpy as jnp
from jax import lax
from jax.experimental import pallas as pl
from jax.experimental.pallas import tpu as pltpu
from jax.sharding import PartitionSpec as P

QH = 64
KVH = 8
DH = 128
WIN = 64
FEAT = 256

f32 = jnp.float32
bf16 = jnp.bfloat16
MESH = pl.DeviceIdType.MESH


def mm(a, b, ca=1, cb=0, precision=None):
    return lax.dot_general(
        a, b, (((ca,), (cb,)), ((), ())), preferred_element_type=f32, precision=precision
    )


def soft_pair(logits):
    top = jnp.max(logits, axis=-1, keepdims=True)
    low = jnp.min(logits, axis=-1, keepdims=True)
    up = jnp.exp(logits - top)
    down = jnp.exp(low - logits)
    up = up * (1.0 / jnp.sum(up, axis=-1, keepdims=True))
    down = down * (1.0 / jnp.sum(down, axis=-1, keepdims=True))
    return up, down


def soft_pair_grad(up, down, ga, gb):
    part_up = up * (ga - jnp.sum(up * ga, axis=-1, keepdims=True))
    part_down = down * (gb - jnp.sum(down * gb, axis=-1, keepdims=True))
    return (part_up - part_down).astype(bf16)


def kernel(
    nseq, nhead, rows, kvl, per,
    q_hbm, k_hbm, v_hbm, t_hbm, mq_hbm, mk_hbm,
    gq_ref, gk_ref, gv_ref, gm_ref,
    q_ref, k_ref, v_ref, t_ref, mq_ref, mk_ref, in_s,
    kx, vx, fkx, fkb, cum, pre, stb, kq, p_scr, fq_scr, gp_scr, gf_scr, dl_scr,
    gfk_acc, dv_acc, dk_acc, gk_acc, bt_acc, bn_acc, gmq_acc, gmk_acc,
    halo_out, halo_in, st_out, st_in, nm_out, nm_in,
    bt_out, bt_in, bn_out, bn_in, hr_out, hr_in, hk_out, hk_in, mg, mr, tot,
    halo_s, halo_r, st_s, st_r, nm_s, nm_r, bt_s, bt_r, bn_s, bn_r, hr_s, hr_r, hk_s, hk_r,
    mg_s, mr_s, tot_s, tot_r,
):
    nb = rows // WIN
    head_rows = per * WIN
    tail = rows - WIN
    chunks, _, _ = mg.shape
    crows = 2 * DH // chunks
    place = lax.axis_index("seq")
    mine = place * nhead + lax.axis_index("head")
    team = nseq * nhead
    scale = DH ** (-0.5)

    def remote(src, dst, send, recv, device):
        return pltpu.make_async_remote_copy(
            src_ref=src, dst_ref=dst, send_sem=send, recv_sem=recv,
            device_id=device, device_id_type=MESH,
        )

    barrier = pltpu.get_barrier_semaphore()

    def peer(n):
        return {"seq": n // nhead, "head": n % nhead}

    def hail(d, carry):
        pl.semaphore_signal(barrier, inc=1, device_id=peer((mine + d) % team), device_id_type=MESH)
        return carry

    lax.fori_loop(1, team, hail, 0)

    loads = [
        pltpu.make_async_copy(source, held, in_s.at[n])
        for n, (source, held) in enumerate(
            [(k_hbm, k_ref), (v_hbm, v_ref), (mk_hbm, mk_ref), (q_hbm, q_ref), (mq_hbm, mq_ref), (t_hbm, t_ref)]
        )
    ]
    for load in loads:
        load.start()
    for load in loads[:3]:
        load.wait()

    for g in range(kvl):
        cols = slice(g * DH, (g + 1) * DH)
        kx[g, WIN:] = k_ref[:, cols]
        vx[g, WIN:] = v_ref[:, cols]
        halo_out[g] = k_ref[tail:, cols]
        halo_out[kvl + g] = v_ref[tail:, cols]

    def halo_copy(target):
        return remote(halo_out, halo_in, halo_s, halo_r, {"seq": target})

    def state_copies(slot, g, source, target):
        return (
            remote(st_out.at[slot, g], st_in.at[source, g], st_s.at[g, target], st_r.at[g, source],
                   {"seq": target}),
            remote(nm_out.at[slot, g], nm_in.at[source, g], nm_s.at[g, target], nm_r.at[g, source],
                   {"seq": target}),
        )

    mk = mk_ref[...]
    for g in range(kvl):
        up, down = soft_pair(mm(kx[g, WIN:], mk))
        fk = jnp.concatenate([up, down], axis=-1)
        fkx[g, WIN:] = fk
        fkl = fk.astype(bf16)
        fkb[g, WIN:] = fkl
        early = mm(vx[g, WIN:rows], fkl[:tail], 0, 0)
        late = mm(vx[g, rows:], fkl[tail:], 0, 0)
        st_out[0, g] = early.astype(bf16)
        st_out[1, g] = (early + late).astype(bf16)
        n_early = jnp.sum(fk[:tail].reshape(tail // 8, 8, FEAT), axis=0)
        n_late = jnp.sum(fk[tail:].reshape(WIN // 8, 8, FEAT), axis=0)
        nm_out[0, g] = n_early
        nm_out[1, g] = n_early + n_late

    pl.semaphore_wait(barrier, team - 1)

    @pl.when(place < nseq - 1)
    def _():
        halo_copy(place + 1).start()

    for g in range(kvl):

        @pl.when(place < nseq - 1)
        def _():
            for copy in state_copies(0, g, place, place + 1):
                copy.start()

        def send_far(target, carry):
            for copy in state_copies(1, g, place, target):
                copy.start()
            return carry

        lax.fori_loop(place + 2, nseq, send_far, 0)

    ia = lax.broadcasted_iota(jnp.int32, (WIN, 2 * WIN), 0)
    ie = lax.broadcasted_iota(jnp.int32, (WIN, 2 * WIN), 1)
    lag_mask = (ie <= ia)[None]

    def stacked(ref, g, b):
        return jnp.concatenate(
            [
                ref[pl.ds(b * WIN, WIN), pl.ds(pl.multiple_of((g * per + h) * DH, DH), DH)]
                for h in range(per)
            ],
            axis=0,
        )

    def cube(x):
        return x.reshape(per, WIN, x.shape[-1])

    def plain(x):
        return x.reshape(head_rows, x.shape[-1])

    def forward(lap, carry):
        b = (lap // kvl + 1) % nb
        g = lap % kvl
        unit = g * nb + b
        qs = stacked(q_ref, g, b)
        up, down = soft_pair(mm(qs, mq_ref[...]))
        fq_scr[unit, :, :DH] = up
        fq_scr[unit, :, DH:] = down
        kw = kx[g, pl.ds(b * WIN, 2 * WIN)]
        first_key = jnp.where(place > 0, 0, WIN) - b * WIN
        seen = ((ie > ia) & (ie <= ia + WIN) & (ie >= first_key))[None]
        scores = jnp.where(seen, cube(mm(qs, kw, 1, 1)) * scale, -jnp.inf)
        weights = jnp.exp(scores - jnp.max(scores, axis=-1, keepdims=True))
        probs = weights * (1.0 / jnp.sum(weights, axis=-1, keepdims=True))
        p_scr[unit] = plain(probs)
        return carry

    loads[3].wait()
    loads[4].wait()
    lax.fori_loop(0, kvl * (nb - 1), forward, 0)

    @pl.when(place > 0)
    def _():
        halo_copy(place - 1).wait_recv()

    @pl.when(place == 0)
    def _():
        halo_in[...] = jnp.zeros_like(halo_in)

    has_before = (place > 0).astype(f32)
    for g in range(kvl):
        kx[g, :WIN] = halo_in[g]
        vx[g, :WIN] = halo_in[kvl + g]
        up, down = soft_pair(mm(halo_in[g], mk))
        fk = jnp.concatenate([up, down], axis=-1) * has_before
        fkx[g, :WIN] = fk
        fkb[g, :WIN] = fk.astype(bf16)

    lax.fori_loop(kvl * (nb - 1), kvl * nb, forward, 0)

    ra = lax.broadcasted_iota(jnp.int32, (rows, rows), 0)
    re = lax.broadcasted_iota(jnp.int32, (rows, rows), 1)
    lower = (re <= ra).astype(bf16)
    for g in range(kvl):
        high = fkb[g, :rows]
        rest = (fkx[g, :rows] - high.astype(f32)).astype(bf16)
        cum[g] = mm(lower, high) + mm(lower, rest)
        for b in range(nb - 1):
            part = slice(b * WIN, (b + 1) * WIN)
            pre[g, b] = mm(vx[g, part], fkb[g, part], 0, 0)
    kq[:DH] = mq_ref[...].T

    gmq_acc[...] = jnp.zeros_like(gmq_acc)
    dv_acc[...] = jnp.zeros_like(dv_acc)
    dk_acc[...] = jnp.zeros_like(dk_acc)

    def back_copies(g, source, target):
        return (
            remote(bt_out.at[g], bt_in.at[source, g], bt_s.at[g, target], bt_r.at[g, source],
                   {"seq": target}),
            remote(bn_out.at[g], bn_in.at[source, g], bn_s.at[g, target], bn_r.at[g, source],
                   {"seq": target}),
        )

    def return_copy(g, target):
        return remote(hr_out.at[g], hr_in.at[g], hr_s.at[g], hr_r.at[g], {"seq": target})

    def key_copy(g, target):
        return remote(hk_out.at[g], hk_in.at[g], hk_s.at[g], hk_r.at[g], {"seq": target})

    def group(g, carry):
        bt_acc[...] = jnp.zeros_like(bt_acc)
        bn_acc[...] = jnp.zeros_like(bn_acc)

        def take_state(source, inner):
            for copy in state_copies(0, g, source, source):
                copy.wait_recv()
            bt_acc[...] += st_in[source, g].astype(f32)
            bn_acc[...] += nm_in[source, g]
            return inner

        lax.fori_loop(0, place, take_state, 0)
        cum[g] = cum[g] + jnp.sum(bn_acc[...], axis=0, keepdims=True)
        running = bt_acc[...]
        for b in range(nb):
            stb[g, b] = running.astype(bf16)
            if b < nb - 1:
                running = running + pre[g, b]
        bt_acc[...] = jnp.zeros_like(bt_acc)
        bn_acc[...] = jnp.zeros_like(bn_acc)

        def block(lap, inner):
            b = nb - 1 - lap
            unit = g * nb + b
            here = pl.ds(b * WIN, WIN)
            span = pl.ds(b * WIN, 2 * WIN)
            fq = cube(fq_scr[unit])
            probs = cube(p_scr[unit])
            cumb = cum[g, here][None]
            vw = vx[g, span]
            fkw = fkb[g, span]
            state = stb[g, b]
            den = jnp.sum(fq * cumb, axis=-1, keepdims=True)
            above = den > 1.0
            inv = 1.0 / jnp.where(above, den, 1.0)
            fqn = fq * inv
            fqb = plain(fqn).astype(bf16)
            kin = cube(mm(fqb, fkw, 1, 1))
            mixer = plain(jnp.where(lag_mask, kin, probs)).astype(bf16)
            mix = mm(mixer, vw) + mm(fqb, state, 1, 1)
            go = (mix - stacked(t_ref, g, b).astype(f32)).astype(bf16)
            gp = mm(go, vw, 1, 1)
            gp_scr[unit] = gp
            gp = cube(gp)
            gin = plain(jnp.where(lag_mask, gp, 0.0)).astype(bf16)
            gf = cube(
                mm(jnp.concatenate([go, gin], axis=-1), jnp.concatenate([state, fkw], axis=0))
            )
            slope = jnp.where(above, -jnp.sum(fqn * gf, axis=-1, keepdims=True), 0.0)
            gf_scr[unit] = plain((gf + slope * cumb) * inv)
            gker = plain(jnp.where(lag_mask, gp + slope, 0.0)).astype(bf16)
            gt = mm(go, jnp.concatenate([fqb, mixer], axis=-1), 0, 0)
            dv_acc[g, span] += gt[:, FEAT:].T
            later = bt_acc[...].astype(bf16)
            gfk = mm(gker, fqb, 0, 0)[:WIN] + mm(vw[:WIN], later)
            gfk_acc[g, here] = gfk + jnp.sum(bn_acc[...], axis=0, keepdims=True)
            dv_acc[g, here] += mm(fkw[:WIN], later, 1, 1)
            bt_acc[...] += gt[:, :FEAT]
            bn_acc[...] += jnp.sum(
                plain(fqn * slope).reshape(head_rows // 8, 8, FEAT), axis=0
            )
            return inner

        lax.fori_loop(0, nb, block, 0)
        bt_out[g] = bt_acc[...].astype(bf16)
        bn_out[g] = bn_acc[...]
        hr_out[g, :, :FEAT] = gfk_acc[g, :WIN].astype(bf16)
        hr_out[g, :, FEAT:] = dv_acc[g, :WIN].astype(bf16)

        def send_back(lap, inner):
            for copy in back_copies(g, place, place - 1 - lap):
                copy.start()
            return inner

        lax.fori_loop(0, place, send_back, 0)

        @pl.when(place > 0)
        def _():
            return_copy(g, place - 1).start()

        return carry

    loads[5].wait()
    lax.fori_loop(0, kvl, group, 0)

    def logit_grads(unit, carry):
        fq = fq_scr[unit]
        gf = gf_scr[unit]
        dl = soft_pair_grad(fq[:, :DH], fq[:, DH:], gf[:, :DH], gf[:, DH:])
        dl_scr[unit] = dl
        gmq_acc[...] += mm(stacked(q_ref, unit // nb, unit % nb), dl, 0, 0)
        return carry

    lax.fori_loop(0, kvl * nb, logit_grads, 0)

    def each_peer(visit):
        def one(d, carry):
            visit((mine + d) % team)
            return carry

        lax.fori_loop(1, team, one, 0)

    def each_owner(first, last, visit):
        def one(c, carry):
            @pl.when(c != mine)
            def _():
                visit(c)

            return carry

        lax.fori_loop(first, last, one, 0)

    def part_copy(chunk, source):
        return remote(mg.at[chunk], mr.at[source], mg_s.at[chunk], mr_s.at[source], peer(chunk))

    def total_copy(chunk, target):
        return remote(tot.at[chunk], tot.at[chunk], tot_s.at[target], tot_r.at[chunk], peer(target))

    def scatter(which, part):
        half = chunks // 2
        for c in range(half):
            mg[which * half + c] = part[c * crows : (c + 1) * crows].astype(bf16)
        each_owner(which * half, which * half + half, lambda c: part_copy(c, mine).start())

    scatter(0, gmq_acc[...])

    def query_grads(lap, carry):
        b = lap // kvl
        g = lap % kvl
        unit = g * nb + b
        here = pl.ds(b * WIN, WIN)
        span = pl.ds(b * WIN, 2 * WIN)
        probs = p_scr[unit]
        gp = gp_scr[unit]
        ds = (probs * (gp - jnp.sum(probs * gp, axis=-1, keepdims=True)) * scale).astype(bf16)
        gq = mm(
            jnp.concatenate([dl_scr[unit], ds], axis=-1),
            jnp.concatenate([kq[:DH], kx[g, span]], axis=0),
        ).astype(bf16)
        for h in range(per):
            gq_ref[here, pl.ds(pl.multiple_of((g * per + h) * DH, DH), DH)] = gq[
                h * WIN : (h + 1) * WIN
            ]
        dk_acc[g, span] += mm(ds, stacked(q_ref, g, b), 0, 0)
        return carry

    lax.fori_loop(0, kvl, query_grads, 0)
    for g in range(kvl):
        hk_out[g] = dk_acc[g, :WIN].astype(bf16)

        @pl.when(place > 0)
        def _():
            key_copy(g, place - 1).start()

    half_way = kvl * nb // 2
    lax.fori_loop(kvl, half_way, query_grads, 0)

    @pl.when(place == nseq - 1)
    def _():
        hr_in[...] = jnp.zeros_like(hr_in)
        hk_in[...] = jnp.zeros_like(hk_in)

    gmk_acc[...] = jnp.zeros_like(gmk_acc)
    for g in range(kvl):
        bt_acc[...] = jnp.zeros_like(bt_acc)
        bn_acc[...] = jnp.zeros_like(bn_acc)

        def take_back(source, carry):
            for copy in back_copies(g, source, source):
                copy.wait_recv()
            bt_acc[...] += bt_in[source, g].astype(f32)
            bn_acc[...] += bn_in[source, g]
            return carry

        lax.fori_loop(place + 2, nseq, take_back, 0)
        far = bt_acc[...].astype(bf16)
        far_norm = jnp.sum(bn_acc[...], axis=0, keepdims=True)

        @pl.when(place < nseq - 1)
        def _():
            take_back(place + 1, 0)
            return_copy(g, place + 1).wait_recv()

        near = bt_acc[...].astype(bf16)
        near_norm = jnp.sum(bn_acc[...], axis=0, keepdims=True)
        gfk = jnp.concatenate(
            [
                gfk_acc[g, WIN:] + mm(vx[g, WIN:rows], near) + near_norm,
                hr_in[g, :, :FEAT].astype(f32) + mm(vx[g, rows:], far) + far_norm,
            ],
            axis=0,
        )
        gv = jnp.concatenate(
            [
                dv_acc[g, WIN:rows] + mm(fkb[g, WIN:rows], near, 1, 1),
                dv_acc[g, rows:]
                + hr_in[g, :, FEAT:].astype(f32)
                + mm(fkb[g, rows:], far, 1, 1),
            ],
            axis=0,
        )
        dl = soft_pair_grad(
            fkx[g, WIN:, :DH], fkx[g, WIN:, DH:], gfk[:, :DH], gfk[:, DH:]
        )
        gk_acc[g] = mm(dl, mk, 1, 1)
        gv_ref[:, g * DH : (g + 1) * DH] = gv.astype(bf16)
        gmk_acc[...] += mm(kx[g, WIN:], dl, 0, 0)

    scatter(1, gmk_acc[...])
    lax.fori_loop(half_way, kvl * nb, query_grads, 0)

    for g in range(kvl):

        @pl.when(place < nseq - 1)
        def _():
            key_copy(g, place + 1).wait_recv()

        cols = slice(g * DH, (g + 1) * DH)
        gk_ref[:tail, cols] = (dk_acc[g, WIN:rows] + gk_acc[g, :tail]).astype(bf16)
        gk_ref[tail:, cols] = (
            dk_acc[g, rows:] + gk_acc[g, tail:] + hk_in[g].astype(f32)
        ).astype(bf16)

    @pl.when(mine < chunks)
    def _():
        each_peer(lambda d: part_copy(mine, d).wait_recv())
        mr[mine] = mg[mine]
        part = mr[0].astype(f32)
        for d in range(1, team):
            part = part + mr[d].astype(f32)
        tot[mine] = part.astype(bf16)
        each_peer(lambda d: total_copy(mine, d).start())

    each_owner(0, chunks, lambda c: total_copy(c, mine).wait_recv())
    for c in range(chunks):
        gm_ref[c * crows : (c + 1) * crows] = tot[c].astype(f32)

    @pl.when(place < nseq - 1)
    def _():
        halo_copy(place + 1).wait_send()

    for g in range(kvl):

        @pl.when(place < nseq - 1)
        def _():
            for copy in state_copies(0, g, place, place + 1):
                copy.wait_send()

        def far_sent(target, carry):
            for copy in state_copies(1, g, place, target):
                copy.wait_send()
            return carry

        lax.fori_loop(place + 2, nseq, far_sent, 0)

        @pl.when(place > 0)
        def _():
            return_copy(g, place - 1).wait_send()
            key_copy(g, place - 1).wait_send()

        def back_sent(lap, carry):
            for copy in back_copies(g, place, place - 1 - lap):
                copy.wait_send()
            return carry

        lax.fori_loop(0, place, back_sent, 0)

    each_owner(0, chunks, lambda c: part_copy(c, mine).wait_send())

    @pl.when(mine < chunks)
    def _():
        each_peer(lambda d: total_copy(mine, d).wait_send())


def hand_over(gq, gk, gv, gm, gq_out, gk_out, gv_out, gmq_out, gmk_out, put):
    writes = []
    for held, target in [(gq, gq_out), (gk, gk_out), (gv, gv_out), (gm.at[:DH], gmq_out), (gm.at[DH:], gmk_out)]:
        write = pltpu.make_async_copy(held, target, put.at[len(writes)])
        write.start()
        writes.append(write)
    for write in writes:
        write.wait()


def shards(nseq, nhead, queries, key_vecs, value_vecs, teacher_out, map_query, map_key):
    rows = queries.shape[0]
    kvl = key_vecs.shape[1] // DH
    per = QH // KVH
    nb = rows // WIN
    units = kvl * nb
    team = nseq * nhead
    chunks = min(team, 2 * DH // 16)
    crows = 2 * DH // chunks
    vm = pltpu.VMEM
    dma = pltpu.SemaphoreType.DMA
    scratch = [
        vm(queries.shape, bf16),
        vm(key_vecs.shape, bf16),
        vm(value_vecs.shape, bf16),
        vm(queries.shape, bf16),
        vm(map_query.shape, bf16),
        vm(map_key.shape, bf16),
        dma((6,)),
        vm((kvl, rows + WIN, DH), bf16),
        vm((kvl, rows + WIN, DH), bf16),
        vm((kvl, rows + WIN, FEAT), f32),
        vm((kvl, rows + WIN, FEAT), bf16),
        vm((kvl, rows, FEAT), f32),
        vm((kvl, nb - 1, DH, FEAT), f32),
        vm((kvl, nb, DH, FEAT), bf16),
        vm((DH, DH), bf16),
        vm((units, per * WIN, 2 * WIN), f32),
        vm((units, per * WIN, FEAT), f32),
        vm((units, per * WIN, 2 * WIN), f32),
        vm((units, per * WIN, FEAT), f32),
        vm((units, per * WIN, DH), bf16),
        vm((kvl, rows, FEAT), f32),
        vm((kvl, rows + WIN, DH), f32),
        vm((kvl, rows + WIN, DH), f32),
        vm((kvl, rows, DH), f32),
        vm((DH, FEAT), f32),
        vm((8, FEAT), f32),
        vm((DH, DH), f32),
        vm((DH, DH), f32),
        vm((2 * kvl, WIN, DH), bf16),
        vm((2 * kvl, WIN, DH), bf16),
        vm((2, kvl, DH, FEAT), bf16),
        vm((nseq, kvl, DH, FEAT), bf16),
        vm((2, kvl, 8, FEAT), f32),
        vm((nseq, kvl, 8, FEAT), f32),
        vm((kvl, DH, FEAT), bf16),
        vm((nseq, kvl, DH, FEAT), bf16),
        vm((kvl, 8, FEAT), f32),
        vm((nseq, kvl, 8, FEAT), f32),
        vm((kvl, WIN, FEAT + DH), bf16),
        vm((kvl, WIN, FEAT + DH), bf16),
        vm((kvl, WIN, DH), bf16),
        vm((kvl, WIN, DH), bf16),
        vm((chunks, crows, DH), bf16),
        vm((team, crows, DH), bf16),
        vm((chunks, crows, DH), bf16),
        dma, dma,
        dma((kvl, nseq)), dma((kvl, nseq)), dma((kvl, nseq)), dma((kvl, nseq)),
        dma((kvl, nseq)), dma((kvl, nseq)), dma((kvl, nseq)), dma((kvl, nseq)),
        dma((kvl,)), dma((kvl,)), dma((kvl,)), dma((kvl,)),
        dma((chunks,)), dma((team,)), dma((team,)), dma((chunks,)),
    ]
    whole = pl.BlockSpec(memory_space=pltpu.VMEM)
    anywhere = pl.BlockSpec(memory_space=pl.ANY)
    queries, key_vecs, value_vecs, teacher_out, map_query, map_key = (
        pltpu.with_memory_space_constraint(x, pltpu.HBM)
        for x in (queries, key_vecs, value_vecs, teacher_out, map_query, map_key)
    )
    results = pl.pallas_call(
        functools.partial(kernel, nseq, nhead, rows, kvl, per),
        out_shape=(
            vm(queries.shape, bf16),
            vm(key_vecs.shape, bf16),
            vm(value_vecs.shape, bf16),
            vm((2 * DH, DH), f32),
        ),
        in_specs=[anywhere] * 6,
        out_specs=[whole, whole, whole, whole],
        scratch_shapes=scratch,
        compiler_params=pltpu.CompilerParams(
            collective_id=0, has_side_effects=True, vmem_limit_bytes=40 * 1024 * 1024
        ),
        name="transfer_step",
    )(queries, key_vecs, value_vecs, teacher_out, map_query, map_key)
    return pl.pallas_call(
        hand_over,
        out_shape=(
            jax.ShapeDtypeStruct(queries.shape, bf16),
            jax.ShapeDtypeStruct(key_vecs.shape, bf16),
            jax.ShapeDtypeStruct(value_vecs.shape, bf16),
            jax.ShapeDtypeStruct((DH, DH), f32),
            jax.ShapeDtypeStruct((DH, DH), f32),
        ),
        in_specs=[whole] * 4,
        out_specs=[anywhere] * 5,
        scratch_shapes=[dma((5,))],
        compiler_params=pltpu.CompilerParams(vmem_limit_bytes=1024 * 1024),
        name="hand_over",
    )(*results)


def solution(mesh):
    in_specs = (
        P(("grp", "seq"), "head"),
        P(("grp", "seq"), "head"),
        P(("grp", "seq"), "head"),
        P(("grp", "seq"), "head"),
        P(),
        P(),
    )
    out_specs = (
        P(("grp", "seq"), "head"),
        P(("grp", "seq"), "head"),
        P(("grp", "seq"), "head"),
        P("grp", None),
        P("grp", None),
    )
    body = functools.partial(shards, mesh.shape["seq"], mesh.shape["head"])
    return jax.shard_map(body, mesh=mesh, in_specs=in_specs, out_specs=out_specs, check_vma=False)
```

```python
import functools

import jax
import jax.numpy as jnp
from jax import lax
from jax.experimental import pallas as pl
from jax.experimental.pallas import tpu as pltpu
from jax.sharding import PartitionSpec as P

QH = 64
KVH = 8
DH = 128
WIN = 64
FEAT = 256

f32 = jnp.float32
bf16 = jnp.bfloat16
MESH = pl.DeviceIdType.MESH


def mm(a, b, ca=1, cb=0, precision=None):
    return lax.dot_general(
        a, b, (((ca,), (cb,)), ((), ())), preferred_element_type=f32, precision=precision
    )


def soft_pair(logits):
    top = jnp.max(logits, axis=-1, keepdims=True)
    low = jnp.min(logits, axis=-1, keepdims=True)
    up = jnp.exp(logits - top)
    down = jnp.exp(low - logits)
    up = up * (1.0 / jnp.sum(up, axis=-1, keepdims=True))
    down = down * (1.0 / jnp.sum(down, axis=-1, keepdims=True))
    return up, down


def spread_sum(x, ones):
    high = x.astype(bf16)
    rest = (x - high.astype(f32)).astype(bf16)
    return mm(jnp.concatenate([high, rest], axis=-1), ones)


def soft_pair_grad(up, down, ga, gb):
    part_up = up * (ga - jnp.sum(up * ga, axis=-1, keepdims=True))
    part_down = down * (gb - jnp.sum(down * gb, axis=-1, keepdims=True))
    return (part_up - part_down).astype(bf16)


def kernel(
    nseq, nhead, rows, kvl, per,
    q_hbm, k_hbm, v_hbm, t_hbm, mq_hbm, mk_hbm,
    gq_ref, gk_ref, gv_ref, gm_ref,
    q_ref, k_ref, v_ref, t_ref, mq_ref, mk_ref, in_s,
    kx, vx, fkx, fkb, cum, pre, stb, kq, p_scr, fq_scr, gp_scr, gf_scr, dl_scr,
    gfk_acc, dv_acc, dk_acc, gk_acc, bt_acc, bn_acc, gmq_acc, gmk_acc,
    halo_out, halo_in, st_out, st_in, nm_out, nm_in,
    bt_out, bt_in, bn_out, bn_in, hr_out, hr_in, hk_out, hk_in, mg, mr, tot,
    halo_s, halo_r, st_s, st_r, nm_s, nm_r, bt_s, bt_r, bn_s, bn_r, hr_s, hr_r, hk_s, hk_r,
    mg_s, mg_r, tot_s, tot_r,
):
    nb = rows // WIN
    head_rows = per * WIN
    tail = rows - WIN
    chunks, _, _ = mg.shape
    crows = 2 * DH // chunks
    place = lax.axis_index("seq")
    mine = place * nhead + lax.axis_index("head")
    team = nseq * nhead
    scale = DH ** (-0.5)

    def remote(src, dst, send, recv, device):
        return pltpu.make_async_remote_copy(
            src_ref=src, dst_ref=dst, send_sem=send, recv_sem=recv,
            device_id=device, device_id_type=MESH,
        )

    barrier = pltpu.get_barrier_semaphore()

    def peer(n):
        return {"seq": n // nhead, "head": n % nhead}

    loads = [
        pltpu.make_async_copy(source, held, in_s.at[n])
        for n, (source, held) in enumerate(
            [(k_hbm, k_ref), (v_hbm, v_ref), (mk_hbm, mk_ref), (q_hbm, q_ref), (mq_hbm, mq_ref), (t_hbm, t_ref)]
        )
    ]
    for load in loads:
        load.start()
    def hail(d, carry):
        pl.semaphore_signal(barrier, inc=1, device_id=peer((mine + d) % team), device_id_type=MESH)
        return carry

    lax.fori_loop(1, team, hail, 0, unroll=min(team - 1, 15))

    for load in loads[:3]:
        load.wait()

    for g in range(kvl):
        cols = slice(g * DH, (g + 1) * DH)
        kx[g, WIN:] = k_ref[:, cols]
        vx[g, WIN:] = v_ref[:, cols]
        halo_out[g] = k_ref[tail:, cols]
        halo_out[kvl + g] = v_ref[tail:, cols]

    def halo_copy(target):
        return remote(halo_out, halo_in, halo_s, halo_r, {"seq": target})

    def state_copies(slot, g, source, target):
        return (
            remote(st_out.at[slot, g], st_in.at[source, g], st_s.at[g, target], st_r.at[g, source],
                   {"seq": target}),
            remote(nm_out.at[slot, g], nm_in.at[source, g], nm_s.at[g, target], nm_r.at[g, source],
                   {"seq": target}),
        )

    mk = mk_ref[...]
    for g in range(kvl):
        up, down = soft_pair(mm(kx[g, WIN:], mk))
        fk = jnp.concatenate([up, down], axis=-1)
        fkx[g, WIN:] = fk
        fkl = fk.astype(bf16)
        fkb[g, WIN:] = fkl
        early = mm(vx[g, WIN:rows], fkl[:tail], 0, 0)
        late = mm(vx[g, rows:], fkl[tail:], 0, 0)
        st_out[0, g] = early.astype(bf16)
        st_out[1, g] = (early + late).astype(bf16)
        n_early = jnp.sum(fk[:tail].reshape(tail // 8, 8, FEAT), axis=0)
        n_late = jnp.sum(fk[tail:].reshape(WIN // 8, 8, FEAT), axis=0)
        nm_out[0, g] = n_early
        nm_out[1, g] = n_early + n_late

    pl.semaphore_wait(barrier, team - 1)

    @pl.when(place < nseq - 1)
    def _():
        halo_copy(place + 1).start()

    for g in range(kvl):

        @pl.when(place < nseq - 1)
        def _():
            for copy in state_copies(0, g, place, place + 1):
                copy.start()

        def send_far(target, carry):
            for copy in state_copies(1, g, place, target):
                copy.start()
            return carry

        lax.fori_loop(place + 2, nseq, send_far, 0)

    ia = lax.broadcasted_iota(jnp.int32, (WIN, 2 * WIN), 0)
    ie = lax.broadcasted_iota(jnp.int32, (WIN, 2 * WIN), 1)
    lag_mask = (ie <= ia)[None]
    ones = jnp.ones((2 * DH, DH), bf16)

    def stacked(ref, g, b, h0, hs):
        return jnp.concatenate(
            [
                ref[pl.ds(b * WIN, WIN), pl.ds(pl.multiple_of((g * per + h) * DH, DH), DH)]
                for h in range(h0, h0 + hs)
            ],
            axis=0,
        )

    def cube(x):
        return x.reshape(x.shape[0] // WIN, WIN, x.shape[-1])

    def plain(x):
        return x.reshape(x.shape[0] * WIN, x.shape[-1])

    def forward(lap, carry):
        b = (lap // kvl + 1) % nb
        g = lap % kvl
        unit = g * nb + b
        kw = kx[g, pl.ds(b * WIN, 2 * WIN)]
        first_key = jnp.where(place > 0, 0, WIN) - b * WIN
        seen = ((ie > ia) & (ie <= ia + WIN) & (ie >= first_key))[None]
        for h0 in range(0, per, per):
            part = slice(h0 * WIN, (h0 + per) * WIN)
            qs = stacked(q_ref, g, b, h0, per)
            both = mm(qs, jnp.concatenate([kq[...], kw], axis=0), 1, 1)
            logits = both[:, :DH]
            up = jnp.exp(logits - jnp.max(logits, axis=-1, keepdims=True))
            down = jnp.exp(jnp.min(logits, axis=-1, keepdims=True) - logits)
            fq_scr[unit, part, :DH] = up * (1.0 / spread_sum(up, ones))
            fq_scr[unit, part, DH:] = down * (1.0 / spread_sum(down, ones))
            scores = jnp.where(seen, cube(both[:, DH:]) * scale, -jnp.inf)
            weights = plain(jnp.exp(scores - jnp.max(scores, axis=-1, keepdims=True)))
            p_scr[unit, part] = weights * (1.0 / spread_sum(weights, ones))
        return carry

    loads[3].wait()
    loads[4].wait()
    kq[...] = mq_ref[...].T
    lax.fori_loop(0, kvl * (nb - 1), forward, 0, unroll=2)

    @pl.when(place > 0)
    def _():
        halo_copy(place - 1).wait_recv()

    @pl.when(place == 0)
    def _():
        halo_in[...] = jnp.zeros_like(halo_in)

    has_before = (place > 0).astype(f32)
    for g in range(kvl):
        kx[g, :WIN] = halo_in[g]
        vx[g, :WIN] = halo_in[kvl + g]
        up, down = soft_pair(mm(halo_in[g], mk))
        fk = jnp.concatenate([up, down], axis=-1) * has_before
        fkx[g, :WIN] = fk
        fkb[g, :WIN] = fk.astype(bf16)

    lax.fori_loop(kvl * (nb - 1), kvl * nb, forward, 0, unroll=kvl)

    ra = lax.broadcasted_iota(jnp.int32, (rows, rows), 0)
    re = lax.broadcasted_iota(jnp.int32, (rows, rows), 1)
    lower = (re <= ra).astype(bf16)
    for g in range(kvl):
        high = fkb[g, :rows]
        rest = (fkx[g, :rows] - high.astype(f32)).astype(bf16)
        cum[g] = mm(lower, high) + mm(lower, rest)
        for b in range(nb - 1):
            part = slice(b * WIN, (b + 1) * WIN)
            pre[g, b] = mm(vx[g, part], fkb[g, part], 0, 0)

    gmq_acc[...] = jnp.zeros_like(gmq_acc)
    dv_acc[...] = jnp.zeros_like(dv_acc)
    dk_acc[...] = jnp.zeros_like(dk_acc)

    def back_copies(g, source, target):
        return (
            remote(bt_out.at[g], bt_in.at[source, g], bt_s.at[g, target], bt_r.at[g, source],
                   {"seq": target}),
            remote(bn_out.at[g], bn_in.at[source, g], bn_s.at[g, target], bn_r.at[g, source],
                   {"seq": target}),
        )

    def return_copy(g, target):
        return remote(hr_out.at[g], hr_in.at[g], hr_s.at[g], hr_r.at[g], {"seq": target})

    def key_copy(g, target):
        return remote(hk_out.at[g], hk_in.at[g], hk_s.at[g], hk_r.at[g], {"seq": target})

    def group(g, carry):
        bt_acc[...] = jnp.zeros_like(bt_acc)
        bn_acc[...] = jnp.zeros_like(bn_acc)

        def take_state(source, inner):
            for copy in state_copies(0, g, source, source):
                copy.wait_recv()
            bt_acc[...] += st_in[source, g].astype(f32)
            bn_acc[...] += nm_in[source, g]
            return inner

        lax.fori_loop(0, place, take_state, 0)
        cum[g] = cum[g] + jnp.sum(bn_acc[...], axis=0, keepdims=True)
        running = bt_acc[...]
        for b in range(nb):
            stb[g, b] = running.astype(bf16)
            if b < nb - 1:
                running = running + pre[g, b]
        bt_acc[...] = jnp.zeros_like(bt_acc)
        bn_acc[...] = jnp.zeros_like(bn_acc)

        def block(lap, inner):
            b = nb - 1 - lap
            unit = g * nb + b
            here = pl.ds(b * WIN, WIN)
            span = pl.ds(b * WIN, 2 * WIN)
            cumb = cum[g, here][None]
            vw = vx[g, span]
            fkw = fkb[g, span]
            state = stb[g, b]
            back = jnp.concatenate([state, fkw], axis=0)
            gt = jnp.zeros((DH, FEAT + DH), f32)
            gfk = jnp.zeros((2 * WIN, FEAT), f32)
            gn = jnp.zeros((8, FEAT), f32)
            for h0 in range(0, per, per):
                part = slice(h0 * WIN, (h0 + per) * WIN)
                fq = cube(fq_scr[unit, part])
                den = jnp.sum(fq * cumb, axis=-1, keepdims=True)
                above = den > 1.0
                inv = 1.0 / jnp.where(above, den, 1.0)
                fqn = fq * inv
                fqb = plain(fqn).astype(bf16)
                far = mm(fqb, back, 1, 1)
                kin = cube(far[:, DH:])
                mixer = plain(jnp.where(lag_mask, kin, cube(p_scr[unit, part]))).astype(bf16)
                mix = mm(mixer, vw) + far[:, :DH]
                go = (mix - stacked(t_ref, g, b, h0, per).astype(f32)).astype(bf16)
                gp = mm(go, vw, 1, 1)
                gp_scr[unit, part] = gp
                gp = cube(gp)
                gin = plain(jnp.where(lag_mask, gp, 0.0)).astype(bf16)
                gf = cube(mm(jnp.concatenate([go, gin], axis=-1), back))
                slope = jnp.where(above, -jnp.sum(fqn * gf, axis=-1, keepdims=True), 0.0)
                gf_scr[unit, part] = plain((gf + slope * cumb) * inv)
                gker = plain(jnp.where(lag_mask, gp + slope, 0.0)).astype(bf16)
                gt = gt + mm(go, jnp.concatenate([fqb, mixer], axis=-1), 0, 0)
                gfk = gfk + mm(gker, fqb, 0, 0)
                gn = gn + jnp.sum(plain(fqn * slope).reshape(per * WIN // 8, 8, FEAT), axis=0)
            dv_acc[g, span] += gt[:, FEAT:].T
            later = bt_acc[...].astype(bf16)
            gfk = gfk[:WIN] + mm(vw[:WIN], later)
            gfk_acc[g, here] = gfk + jnp.sum(bn_acc[...], axis=0, keepdims=True)
            dv_acc[g, here] += mm(fkw[:WIN], later, 1, 1)
            bt_acc[...] += gt[:, :FEAT]
            bn_acc[...] += gn
            return inner

        lax.fori_loop(0, nb, block, 0, unroll=2)
        bt_out[g] = bt_acc[...].astype(bf16)
        bn_out[g] = bn_acc[...]
        hr_out[g, :, :FEAT] = gfk_acc[g, :WIN].astype(bf16)
        hr_out[g, :, FEAT:] = dv_acc[g, :WIN].astype(bf16)

        def send_back(lap, inner):
            for copy in back_copies(g, place, place - 1 - lap):
                copy.start()
            return inner

        lax.fori_loop(0, place, send_back, 0)

        @pl.when(place > 0)
        def _():
            return_copy(g, place - 1).start()

        return carry

    loads[5].wait()
    lax.fori_loop(0, kvl, group, 0)

    def logit_grads(unit, carry):
        for h0 in range(0, per, per):
            part = slice(h0 * WIN, (h0 + per) * WIN)
            fq = fq_scr[unit, part]
            gf = gf_scr[unit, part]
            dl = soft_pair_grad(fq[:, :DH], fq[:, DH:], gf[:, :DH], gf[:, DH:])
            dl_scr[unit, part] = dl
            gmq_acc[...] += mm(stacked(q_ref, unit // nb, unit % nb, h0, per), dl, 0, 0)
        return carry

    lax.fori_loop(0, kvl * nb, logit_grads, 0, unroll=2)

    def each_owner(first, last, visit):
        def one(c, carry):
            @pl.when(c != mine)
            def _():
                visit(c)

            return carry

        lax.fori_loop(first, last, one, 0, unroll=8)

    def part_copy(chunk):
        return remote(mg.at[chunk], mr.at[mine], mg_s, mg_r, peer(chunk))

    def total_copy(target):
        return remote(tot.at[mine], tot.at[mine], tot_s, tot_r, peer(target))

    def span_copy(count, send, recv):
        refs = mr.at[pl.ds(0, count)]
        return remote(refs, refs, send, recv, peer((mine + 1) % team))

    def scatter(which, part):
        half = chunks // 2
        for c in range(half):
            mg[which * half + c] = part[c * crows : (c + 1) * crows].astype(bf16)
        each_owner(which * half, which * half + half, lambda c: part_copy(c).start())

    scatter(0, gmq_acc[...])

    def query_grads(lap, carry):
        b = lap // kvl
        g = lap % kvl
        unit = g * nb + b
        here = pl.ds(b * WIN, WIN)
        span = pl.ds(b * WIN, 2 * WIN)
        for h0 in range(0, per, per):
            part = slice(h0 * WIN, (h0 + per) * WIN)
            probs = p_scr[unit, part]
            gp = gp_scr[unit, part]
            ds = (probs * (gp - jnp.sum(probs * gp, axis=-1, keepdims=True)) * scale).astype(bf16)
            gq = mm(
                jnp.concatenate([dl_scr[unit, part], ds], axis=-1),
                jnp.concatenate([kq[...], kx[g, span]], axis=0),
            ).astype(bf16)
            for h in range(per):
                gq_ref[here, pl.ds(pl.multiple_of((g * per + h0 + h) * DH, DH), DH)] = gq[
                    h * WIN : (h + 1) * WIN
                ]
            dk_acc[g, span] += mm(ds, stacked(q_ref, g, b, h0, per), 0, 0)
        return carry

    lax.fori_loop(0, kvl, query_grads, 0, unroll=kvl)
    for g in range(kvl):
        hk_out[g] = dk_acc[g, :WIN].astype(bf16)

        @pl.when(place > 0)
        def _():
            key_copy(g, place - 1).start()

    half_way = kvl * nb // 2
    lax.fori_loop(kvl, half_way, query_grads, 0, unroll=2)

    @pl.when(place == nseq - 1)
    def _():
        hr_in[...] = jnp.zeros_like(hr_in)
        hk_in[...] = jnp.zeros_like(hk_in)

    gmk_acc[...] = jnp.zeros_like(gmk_acc)
    for g in range(kvl):
        bt_acc[...] = jnp.zeros_like(bt_acc)
        bn_acc[...] = jnp.zeros_like(bn_acc)

        def take_back(source, carry):
            for copy in back_copies(g, source, source):
                copy.wait_recv()
            bt_acc[...] += bt_in[source, g].astype(f32)
            bn_acc[...] += bn_in[source, g]
            return carry

        lax.fori_loop(place + 2, nseq, take_back, 0)
        far = bt_acc[...].astype(bf16)
        far_norm = jnp.sum(bn_acc[...], axis=0, keepdims=True)

        @pl.when(place < nseq - 1)
        def _():
            take_back(place + 1, 0)
            return_copy(g, place + 1).wait_recv()

        near = bt_acc[...].astype(bf16)
        near_norm = jnp.sum(bn_acc[...], axis=0, keepdims=True)
        gfk = jnp.concatenate(
            [
                gfk_acc[g, WIN:] + mm(vx[g, WIN:rows], near) + near_norm,
                hr_in[g, :, :FEAT].astype(f32) + mm(vx[g, rows:], far) + far_norm,
            ],
            axis=0,
        )
        gv = jnp.concatenate(
            [
                dv_acc[g, WIN:rows] + mm(fkb[g, WIN:rows], near, 1, 1),
                dv_acc[g, rows:]
                + hr_in[g, :, FEAT:].astype(f32)
                + mm(fkb[g, rows:], far, 1, 1),
            ],
            axis=0,
        )
        dl = soft_pair_grad(
            fkx[g, WIN:, :DH], fkx[g, WIN:, DH:], gfk[:, :DH], gfk[:, DH:]
        )
        gk_acc[g] = mm(dl, mk, 1, 1)
        gv_ref[:, g * DH : (g + 1) * DH] = gv.astype(bf16)
        gmk_acc[...] += mm(kx[g, WIN:], dl, 0, 0)

    scatter(1, gmk_acc[...])
    lax.fori_loop(half_way, kvl * nb, query_grads, 0, unroll=2)

    for g in range(kvl):

        @pl.when(place < nseq - 1)
        def _():
            key_copy(g, place + 1).wait_recv()

        cols = slice(g * DH, (g + 1) * DH)
        gk_ref[:tail, cols] = (dk_acc[g, WIN:rows] + gk_acc[g, :tail]).astype(bf16)
        gk_ref[tail:, cols] = (
            dk_acc[g, rows:] + gk_acc[g, tail:] + hk_in[g].astype(f32)
        ).astype(bf16)

    def as_owner(act, otherwise=None):
        if chunks == team:
            act()
            return
        pl.when(mine < chunks)(act)
        if otherwise is not None:
            pl.when(mine >= chunks)(otherwise)

    def total():
        span_copy(team - 1, mg_s, mg_r).wait_recv()
        mr[mine] = mg[mine]
        part = mr[0].astype(f32)
        for d in range(1, team):
            part = part + mr[d].astype(f32)
        tot[mine] = part.astype(bf16)

        def give(d, carry):
            total_copy((mine + d) % team).start()
            return carry

        lax.fori_loop(1, team, give, 0, unroll=min(team - 1, 15))

    as_owner(total)
    as_owner(
        span_copy(chunks - 1, tot_s, tot_r).wait_recv,
        span_copy(chunks, tot_s, tot_r).wait_recv,
    )
    for c in range(chunks):
        gm_ref[c * crows : (c + 1) * crows] = tot[c].astype(f32)

    @pl.when(place < nseq - 1)
    def _():
        halo_copy(place + 1).wait_send()

    for g in range(kvl):

        @pl.when(place < nseq - 1)
        def _():
            for copy in state_copies(0, g, place, place + 1):
                copy.wait_send()

        def far_sent(target, carry):
            for copy in state_copies(1, g, place, target):
                copy.wait_send()
            return carry

        lax.fori_loop(place + 2, nseq, far_sent, 0)

        @pl.when(place > 0)
        def _():
            return_copy(g, place - 1).wait_send()
            key_copy(g, place - 1).wait_send()

        def back_sent(lap, carry):
            for copy in back_copies(g, place, place - 1 - lap):
                copy.wait_send()
            return carry

        lax.fori_loop(0, place, back_sent, 0)

    as_owner(
        span_copy(chunks - 1, mg_s, mg_r).wait_send,
        span_copy(chunks, mg_s, mg_r).wait_send,
    )
    as_owner(span_copy(team - 1, tot_s, tot_r).wait_send)


def hand_over(gq, gk, gv, gm, gq_out, gk_out, gv_out, gmq_out, gmk_out, put):
    writes = []
    for held, target in [(gq, gq_out), (gk, gk_out), (gv, gv_out), (gm.at[:DH], gmq_out), (gm.at[DH:], gmk_out)]:
        write = pltpu.make_async_copy(held, target, put.at[len(writes)])
        write.start()
        writes.append(write)
    for write in writes:
        write.wait()


def shards(nseq, nhead, queries, key_vecs, value_vecs, teacher_out, map_query, map_key):
    rows = queries.shape[0]
    kvl = key_vecs.shape[1] // DH
    per = QH // KVH
    nb = rows // WIN
    units = kvl * nb
    team = nseq * nhead
    chunks = min(team, 2 * DH // 16)
    crows = 2 * DH // chunks
    vm = pltpu.VMEM
    dma = pltpu.SemaphoreType.DMA
    scratch = [
        vm(queries.shape, bf16),
        vm(key_vecs.shape, bf16),
        vm(value_vecs.shape, bf16),
        vm(queries.shape, bf16),
        vm(map_query.shape, bf16),
        vm(map_key.shape, bf16),
        dma((6,)),
        vm((kvl, rows + WIN, DH), bf16),
        vm((kvl, rows + WIN, DH), bf16),
        vm((kvl, rows + WIN, FEAT), f32),
        vm((kvl, rows + WIN, FEAT), bf16),
        vm((kvl, rows, FEAT), f32),
        vm((kvl, nb - 1, DH, FEAT), f32),
        vm((kvl, nb, DH, FEAT), bf16),
        vm((DH, DH), bf16),
        vm((units, per * WIN, 2 * WIN), f32),
        vm((units, per * WIN, FEAT), f32),
        vm((units, per * WIN, 2 * WIN), f32),
        vm((units, per * WIN, FEAT), f32),
        vm((units, per * WIN, DH), bf16),
        vm((kvl, rows, FEAT), f32),
        vm((kvl, rows + WIN, DH), f32),
        vm((kvl, rows + WIN, DH), f32),
        vm((kvl, rows, DH), f32),
        vm((DH, FEAT), f32),
        vm((8, FEAT), f32),
        vm((DH, DH), f32),
        vm((DH, DH), f32),
        vm((2 * kvl, WIN, DH), bf16),
        vm((2 * kvl, WIN, DH), bf16),
        vm((2, kvl, DH, FEAT), bf16),
        vm((nseq, kvl, DH, FEAT), bf16),
        vm((2, kvl, 8, FEAT), f32),
        vm((nseq, kvl, 8, FEAT), f32),
        vm((kvl, DH, FEAT), bf16),
        vm((nseq, kvl, DH, FEAT), bf16),
        vm((kvl, 8, FEAT), f32),
        vm((nseq, kvl, 8, FEAT), f32),
        vm((kvl, WIN, FEAT + DH), bf16),
        vm((kvl, WIN, FEAT + DH), bf16),
        vm((kvl, WIN, DH), bf16),
        vm((kvl, WIN, DH), bf16),
        vm((chunks, crows, DH), bf16),
        vm((team, crows, DH), bf16),
        vm((chunks, crows, DH), bf16),
        dma, dma,
        dma((kvl, nseq)), dma((kvl, nseq)), dma((kvl, nseq)), dma((kvl, nseq)),
        dma((kvl, nseq)), dma((kvl, nseq)), dma((kvl, nseq)), dma((kvl, nseq)),
        dma((kvl,)), dma((kvl,)), dma((kvl,)), dma((kvl,)),
        dma, dma, dma, dma,
    ]
    whole = pl.BlockSpec(memory_space=pltpu.VMEM)
    anywhere = pl.BlockSpec(memory_space=pl.ANY)
    queries, key_vecs, value_vecs, teacher_out, map_query, map_key = (
        pltpu.with_memory_space_constraint(x, pltpu.HBM)
        for x in (queries, key_vecs, value_vecs, teacher_out, map_query, map_key)
    )
    results = pl.pallas_call(
        functools.partial(kernel, nseq, nhead, rows, kvl, per),
        out_shape=(
            vm(queries.shape, bf16),
            vm(key_vecs.shape, bf16),
            vm(value_vecs.shape, bf16),
            vm((2 * DH, DH), f32),
        ),
        in_specs=[anywhere] * 6,
        out_specs=[whole, whole, whole, whole],
        scratch_shapes=scratch,
        compiler_params=pltpu.CompilerParams(
            collective_id=0, has_side_effects=True, vmem_limit_bytes=40 * 1024 * 1024
        ),
        name="transfer_step",
    )(queries, key_vecs, value_vecs, teacher_out, map_query, map_key)
    return pl.pallas_call(
        hand_over,
        out_shape=(
            jax.ShapeDtypeStruct(queries.shape, bf16),
            jax.ShapeDtypeStruct(key_vecs.shape, bf16),
            jax.ShapeDtypeStruct(value_vecs.shape, bf16),
            jax.ShapeDtypeStruct((DH, DH), f32),
            jax.ShapeDtypeStruct((DH, DH), f32),
        ),
        in_specs=[whole] * 4,
        out_specs=[anywhere] * 5,
        scratch_shapes=[dma((5,))],
        compiler_params=pltpu.CompilerParams(vmem_limit_bytes=1024 * 1024),
        name="hand_over",
    )(*results)


def solution(mesh):
    in_specs = (
        P(("grp", "seq"), "head"),
        P(("grp", "seq"), "head"),
        P(("grp", "seq"), "head"),
        P(("grp", "seq"), "head"),
        P(),
        P(),
    )
    out_specs = (
        P(("grp", "seq"), "head"),
        P(("grp", "seq"), "head"),
        P(("grp", "seq"), "head"),
        P("grp", None),
        P("grp", None),
    )
    body = functools.partial(shards, mesh.shape["seq"], mesh.shape["head"])
    return jax.shard_map(body, mesh=mesh, in_specs=in_specs, out_specs=out_specs, check_vma=False)
```

```python
import functools

import jax
import jax.numpy as jnp
from jax import lax
from jax.experimental import pallas as pl
from jax.experimental.pallas import tpu as pltpu
from jax.sharding import PartitionSpec as P

QH = 64
KVH = 8
DH = 128
WIN = 64
FEAT = 256
LOG2E = 1.4426950408889634

f32 = jnp.float32
bf16 = jnp.bfloat16
MESH = pl.DeviceIdType.MESH


def mm(a, b, ca=1, cb=0, precision=None):
    return lax.dot_general(
        a, b, (((ca,), (cb,)), ((), ())), preferred_element_type=f32, precision=precision
    )


def soft_pair(logits):
    top = jnp.max(logits, axis=-1, keepdims=True)
    low = jnp.min(logits, axis=-1, keepdims=True)
    up = jnp.exp(logits - top)
    down = jnp.exp(low - logits)
    up = up * (1.0 / jnp.sum(up, axis=-1, keepdims=True))
    down = down * (1.0 / jnp.sum(down, axis=-1, keepdims=True))
    return up, down


def soft_pair_grad(up, down, ga, gb):
    part_up = up * (ga - jnp.sum(up * ga, axis=-1, keepdims=True))
    part_down = down * (gb - jnp.sum(down * gb, axis=-1, keepdims=True))
    return (part_up - part_down).astype(bf16)


def kernel(
    nseq, nhead, rows, kvl, per,
    q_hbm, k_hbm, v_hbm, t_hbm, mq_hbm, mk_hbm,
    gq_ref, gk_ref, gv_ref, gm_ref,
    q_ref, k_ref, v_ref, t_ref, mq_ref, mk_ref, in_s,
    kx, vx, fkx, fkb, cum, pre, stb, kq, ones, p_scr, fq_scr, gp_scr,
    fqb_scr, go_scr, inv_scr, slope_scr, dl_scr,
    gfk_acc, dv_acc, dk_acc, gk_acc, bt_acc, bn_acc, gmq_acc, gmk_acc,
    halo_out, halo_in, st_out, st_in, nm_out, nm_in,
    bt_out, bt_in, bn_out, bn_in, hr_out, hr_in, hk_out, hk_in, mg, mr, tot,
    halo_s, halo_r, st_s, st_r, nm_s, nm_r, bt_s, bt_r, bn_s, bn_r, hr_s, hr_r, hk_s, hk_r,
    mg_s, mg_r, tot_s, tot_r,
):
    nb = rows // WIN
    head_rows = per * WIN
    tail = rows - WIN
    chunks, _, _ = mg.shape
    crows = 2 * DH // chunks
    place = lax.axis_index("seq")
    mine = place * nhead + lax.axis_index("head")
    team = nseq * nhead
    scale = DH ** (-0.5)

    def remote(src, dst, send, recv, device):
        return pltpu.make_async_remote_copy(
            src_ref=src, dst_ref=dst, send_sem=send, recv_sem=recv,
            device_id=device, device_id_type=MESH,
        )

    barrier = pltpu.get_barrier_semaphore()

    def peer(n):
        return {"seq": n // nhead, "head": n % nhead}

    loads = [
        pltpu.make_async_copy(source, held, in_s.at[n])
        for n, (source, held) in enumerate(
            [(k_hbm, k_ref), (v_hbm, v_ref), (mk_hbm, mk_ref), (q_hbm, q_ref), (mq_hbm, mq_ref), (t_hbm, t_ref)]
        )
    ]
    for load in loads:
        load.start()
    def hail(d, carry):
        pl.semaphore_signal(barrier, inc=1, device_id=peer((mine + d) % team), device_id_type=MESH)
        return carry

    lax.fori_loop(1, team, hail, 0, unroll=min(team - 1, 15))

    for load in loads[:3]:
        load.wait()

    for g in range(kvl):
        cols = slice(g * DH, (g + 1) * DH)
        kx[g, WIN:] = k_ref[:, cols]
        vx[g, WIN:] = v_ref[:, cols]
        halo_out[g] = k_ref[tail:, cols]
        halo_out[kvl + g] = v_ref[tail:, cols]

    def halo_copy(target):
        return remote(halo_out, halo_in, halo_s, halo_r, {"seq": target})

    def state_copies(slot, g, source, target):
        return (
            remote(st_out.at[slot, g], st_in.at[source, g], st_s.at[g, target], st_r.at[g, source],
                   {"seq": target}),
            remote(nm_out.at[slot, g], nm_in.at[source, g], nm_s.at[g, target], nm_r.at[g, source],
                   {"seq": target}),
        )

    mk = mk_ref[...]
    for g in range(kvl):
        up, down = soft_pair(mm(kx[g, WIN:], mk))
        fk = jnp.concatenate([up, down], axis=-1)
        fkx[g, WIN:] = fk
        fkl = fk.astype(bf16)
        fkb[g, WIN:] = fkl
        early = mm(vx[g, WIN:rows], fkl[:tail], 0, 0)
        late = mm(vx[g, rows:], fkl[tail:], 0, 0)
        st_out[0, g] = early.astype(bf16)
        st_out[1, g] = (early + late).astype(bf16)
        n_early = jnp.sum(fk[:tail].reshape(tail // 8, 8, FEAT), axis=0)
        n_late = jnp.sum(fk[tail:].reshape(WIN // 8, 8, FEAT), axis=0)
        nm_out[0, g] = n_early
        nm_out[1, g] = n_early + n_late

    pl.semaphore_wait(barrier, team - 1)

    @pl.when(place < nseq - 1)
    def _():
        halo_copy(place + 1).start()

    def send_states(g):
        @pl.when(place < nseq - 1)
        def _():
            for copy in state_copies(0, g, place, place + 1):
                copy.start()

        def send_far(target, carry):
            for copy in state_copies(1, g, place, target):
                copy.start()
            return carry

        lax.fori_loop(place + 2, nseq, send_far, 0)

    send_states(0)

    ia = lax.broadcasted_iota(jnp.int32, (WIN, 2 * WIN), 0)
    ie = lax.broadcasted_iota(jnp.int32, (WIN, 2 * WIN), 1)
    lag_mask = (ie <= ia)[None]

    def stacked(ref, g, b, h0, hs):
        return jnp.concatenate(
            [
                ref[pl.ds(b * WIN, WIN), pl.ds(pl.multiple_of((g * per + h) * DH, DH), DH)]
                for h in range(h0, h0 + hs)
            ],
            axis=0,
        )

    def cube(x):
        return x.reshape(x.shape[0] // WIN, WIN, x.shape[-1])

    def plain(x):
        return x.reshape(x.shape[0] * WIN, x.shape[-1])

    def forward(lap, carry):
        b = (lap // kvl + 1) % nb
        g = lap % kvl
        unit = g * nb + b
        kw = kx[g, pl.ds(b * WIN, 2 * WIN)]
        first_key = jnp.where(place > 0, 0, WIN) - b * WIN
        seen = ((ie > ia) & (ie <= ia + WIN) & (ie >= first_key))[None]
        for h0 in range(0, per, per):
            part = slice(h0 * WIN, (h0 + per) * WIN)
            qs = stacked(q_ref, g, b, h0, per)
            both = mm(qs, jnp.concatenate([kq[...], kw], axis=0), 1, 1)
            logits = both[:, :DH] * LOG2E
            up = jnp.exp2(logits - jnp.max(logits, axis=-1, keepdims=True))
            down = jnp.exp2(jnp.min(logits, axis=-1, keepdims=True) - logits)
            pair = jnp.concatenate([up, down], axis=-1)
            high = pair.astype(bf16)
            rest = (pair - high.astype(f32)).astype(bf16)
            fq_scr[unit, part] = pair * (1.0 / (mm(high, ones[...]) + mm(rest, ones[...])))
            scores = jnp.where(seen, cube(both[:, DH:]) * (scale * LOG2E), -jnp.inf)
            weights = jnp.exp2(scores - jnp.max(scores, axis=-1, keepdims=True))
            weights = plain(weights).astype(bf16)
            p_scr[unit, part] = weights.astype(f32) * (1.0 / mm(weights, ones[:DH, :DH]))
        return carry

    loads[3].wait()
    loads[4].wait()
    kq[...] = mq_ref[...].T
    side = lax.broadcasted_iota(jnp.int32, (FEAT, FEAT), 0) < DH
    ones[...] = (side == (lax.broadcasted_iota(jnp.int32, (FEAT, FEAT), 1) < DH)).astype(bf16)
    lax.fori_loop(0, 2, forward, 0, unroll=2)
    for g in range(1, kvl):
        send_states(g)
    lax.fori_loop(2, kvl * (nb - 1), forward, 0, unroll=2)

    @pl.when(place > 0)
    def _():
        halo_copy(place - 1).wait_recv()

    @pl.when(place == 0)
    def _():
        halo_in[...] = jnp.zeros_like(halo_in)

    has_before = (place > 0).astype(f32)
    for g in range(kvl):
        kx[g, :WIN] = halo_in[g]
        vx[g, :WIN] = halo_in[kvl + g]
        up, down = soft_pair(mm(halo_in[g], mk))
        fk = jnp.concatenate([up, down], axis=-1) * has_before
        fkx[g, :WIN] = fk
        fkb[g, :WIN] = fk.astype(bf16)

    lax.fori_loop(kvl * (nb - 1), kvl * nb, forward, 0, unroll=kvl)

    ra = lax.broadcasted_iota(jnp.int32, (rows, rows), 0)
    re = lax.broadcasted_iota(jnp.int32, (rows, rows), 1)
    lower = (re <= ra).astype(bf16)
    for g in range(kvl):
        high = fkb[g, :rows]
        rest = (fkx[g, :rows] - high.astype(f32)).astype(bf16)
        cum[g] = mm(lower, high) + mm(lower, rest)
        for b in range(nb - 1):
            part = slice(b * WIN, (b + 1) * WIN)
            pre[g, b] = mm(vx[g, part], fkb[g, part], 0, 0)

    gmq_acc[...] = jnp.zeros_like(gmq_acc)
    dv_acc[...] = jnp.zeros_like(dv_acc)
    dk_acc[...] = jnp.zeros_like(dk_acc)

    def back_copies(g, source, target):
        return (
            remote(bt_out.at[g], bt_in.at[source, g], bt_s.at[g, target], bt_r.at[g, source],
                   {"seq": target}),
            remote(bn_out.at[g], bn_in.at[source, g], bn_s.at[g, target], bn_r.at[g, source],
                   {"seq": target}),
        )

    def return_copy(g, target):
        return remote(hr_out.at[g], hr_in.at[g], hr_s.at[g], hr_r.at[g], {"seq": target})

    def key_copy(g, target):
        return remote(hk_out.at[g], hk_in.at[g], hk_s.at[g], hk_r.at[g], {"seq": target})

    def group(g, carry):
        bt_acc[...] = jnp.zeros_like(bt_acc)
        bn_acc[...] = jnp.zeros_like(bn_acc)

        def take_state(source, inner):
            for copy in state_copies(0, g, source, source):
                copy.wait_recv()
            bt_acc[...] += st_in[source, g].astype(f32)
            bn_acc[...] += nm_in[source, g]
            return inner

        lax.fori_loop(0, place, take_state, 0)
        cum[g] = cum[g] + jnp.sum(bn_acc[...], axis=0, keepdims=True)
        running = bt_acc[...]
        for b in range(nb):
            stb[g, b] = running.astype(bf16)
            if b < nb - 1:
                running = running + pre[g, b]
        bt_acc[...] = jnp.zeros_like(bt_acc)
        bn_acc[...] = jnp.zeros_like(bn_acc)

        def block(lap, inner):
            b = nb - 1 - lap
            unit = g * nb + b
            here = pl.ds(b * WIN, WIN)
            span = pl.ds(b * WIN, 2 * WIN)
            cumb = cum[g, here][None]
            vw = vx[g, span]
            fkw = fkb[g, span]
            state = stb[g, b]
            back = jnp.concatenate([state, fkw], axis=0)
            fq = cube(fq_scr[unit])
            den = jnp.sum(fq * cumb, axis=-1, keepdims=True)
            above = den > 1.0
            inv = 1.0 / jnp.where(above, den, 1.0)
            fqn = fq * inv
            fqb = plain(fqn).astype(bf16)
            far = mm(fqb, back, 1, 1)
            kin = cube(far[:, DH:])
            mixer = plain(jnp.where(lag_mask, kin, cube(p_scr[unit]))).astype(bf16)
            mix = mm(mixer, vw) + far[:, :DH]
            go = (mix - stacked(t_ref, g, b, 0, per).astype(f32)).astype(bf16)
            gp = mm(go, vw, 1, 1)
            pull = cube(go.astype(f32) * far[:, :DH]) + jnp.where(lag_mask, kin * cube(gp), 0.0)
            slope = jnp.where(above, -jnp.sum(pull, axis=-1, keepdims=True), 0.0)
            fqb_scr[unit] = fqb
            go_scr[unit] = go
            gp_scr[unit] = gp
            inv_scr[unit] = plain(jnp.broadcast_to(inv, (per, WIN, DH)))
            slope_scr[unit] = plain(jnp.broadcast_to(slope, (per, WIN, DH)))
            gt = mm(go, jnp.concatenate([fqb, mixer], axis=-1), 0, 0)
            dv_acc[g, span] += gt[:, FEAT:].T
            later = bt_acc[...].astype(bf16)
            gfk_acc[g, here] = mm(vw[:WIN], later) + jnp.sum(bn_acc[...], axis=0, keepdims=True)
            dv_acc[g, here] += mm(fkw[:WIN], later, 1, 1)
            bt_acc[...] += gt[:, :FEAT]
            bn_acc[...] += jnp.sum(plain(fqn * slope).reshape(head_rows // 8, 8, FEAT), axis=0)
            return inner

        lax.fori_loop(0, nb, block, 0, unroll=2)
        bt_out[g] = bt_acc[...].astype(bf16)
        bn_out[g] = bn_acc[...]

        def send_back(lap, inner):
            for copy in back_copies(g, place, place - 1 - lap):
                copy.start()
            return inner

        lax.fori_loop(0, place, send_back, 0)
        return carry

    loads[5].wait()
    lax.fori_loop(0, kvl, group, 0)

    def logit_grads(lap, carry):
        b = lap // kvl
        g = lap % kvl
        unit = g * nb + b
        here = pl.ds(b * WIN, WIN)
        fq = fq_scr[unit]
        go = go_scr[unit]
        gp = cube(gp_scr[unit])
        inv = inv_scr[unit]
        slope = slope_scr[unit]
        gin = plain(jnp.where(lag_mask, gp, 0.0)).astype(bf16)
        back = jnp.concatenate([stb[g, b], fkb[g, pl.ds(b * WIN, 2 * WIN)]], axis=0)
        gf = mm(jnp.concatenate([go, gin], axis=-1), back)
        up_side = plain(cube(gf[:, :DH]) + cube(slope) * cum[g, here, :DH][None]) * inv
        down_side = plain(cube(gf[:, DH:]) + cube(slope) * cum[g, here, DH:][None]) * inv
        dl = soft_pair_grad(fq[:, :DH], fq[:, DH:], up_side, down_side)
        dl_scr[unit] = dl
        gmq_acc[...] += mm(stacked(q_ref, g, b, 0, per), dl, 0, 0)
        gker = plain(jnp.where(lag_mask, gp + cube(slope), 0.0)).astype(bf16)
        gfk_acc[g, here] += mm(gker, fqb_scr[unit], 0, 0)[:WIN]
        return carry

    lax.fori_loop(0, kvl, logit_grads, 0, unroll=kvl)
    for g in range(kvl):
        hr_out[g, :, :FEAT] = gfk_acc[g, :WIN].astype(bf16)
        hr_out[g, :, FEAT:] = dv_acc[g, :WIN].astype(bf16)

        @pl.when(place > 0)
        def _():
            return_copy(g, place - 1).start()

    lax.fori_loop(kvl, kvl * nb, logit_grads, 0, unroll=2)

    def each_owner(first, last, visit):
        def one(c, carry):
            @pl.when(c != mine)
            def _():
                visit(c)

            return carry

        lax.fori_loop(first, last, one, 0, unroll=8)

    def part_copy(chunk):
        return remote(mg.at[chunk], mr.at[mine], mg_s, mg_r, peer(chunk))

    def total_copy(target):
        return remote(tot.at[mine], tot.at[mine], tot_s, tot_r, peer(target))

    def span_copy(count, send, recv):
        refs = mr.at[pl.ds(0, count)]
        return remote(refs, refs, send, recv, peer((mine + 1) % team))

    def scatter(which, part):
        half = chunks // 2
        for c in range(half):
            mg[which * half + c] = part[c * crows : (c + 1) * crows].astype(bf16)
        each_owner(which * half, which * half + half, lambda c: part_copy(c).start())

    scatter(0, gmq_acc[...])

    def query_grads(lap, carry):
        b = lap // kvl
        g = lap % kvl
        unit = g * nb + b
        here = pl.ds(b * WIN, WIN)
        span = pl.ds(b * WIN, 2 * WIN)
        for h0 in range(0, per, per):
            part = slice(h0 * WIN, (h0 + per) * WIN)
            probs = p_scr[unit, part]
            gp = gp_scr[unit, part]
            ds = (probs * (gp - jnp.sum(probs * gp, axis=-1, keepdims=True)) * scale).astype(bf16)
            gq = mm(
                jnp.concatenate([dl_scr[unit, part], ds], axis=-1),
                jnp.concatenate([kq[...], kx[g, span]], axis=0),
            ).astype(bf16)
            for h in range(per):
                gq_ref[here, pl.ds(pl.multiple_of((g * per + h0 + h) * DH, DH), DH)] = gq[
                    h * WIN : (h + 1) * WIN
                ]
            dk_acc[g, span] += mm(ds, stacked(q_ref, g, b, h0, per), 0, 0)
        return carry

    lax.fori_loop(0, kvl, query_grads, 0, unroll=kvl)
    for g in range(kvl):
        hk_out[g] = dk_acc[g, :WIN].astype(bf16)

        @pl.when(place > 0)
        def _():
            key_copy(g, place - 1).start()

    half_way = kvl * nb // 2
    lax.fori_loop(kvl, half_way, query_grads, 0, unroll=2)

    @pl.when(place == nseq - 1)
    def _():
        hr_in[...] = jnp.zeros_like(hr_in)
        hk_in[...] = jnp.zeros_like(hk_in)

    gmk_acc[...] = jnp.zeros_like(gmk_acc)
    for g in range(kvl):
        bt_acc[...] = jnp.zeros_like(bt_acc)
        bn_acc[...] = jnp.zeros_like(bn_acc)

        def take_back(source, carry):
            for copy in back_copies(g, source, source):
                copy.wait_recv()
            bt_acc[...] += bt_in[source, g].astype(f32)
            bn_acc[...] += bn_in[source, g]
            return carry

        lax.fori_loop(place + 2, nseq, take_back, 0)
        far = bt_acc[...].astype(bf16)
        far_norm = jnp.sum(bn_acc[...], axis=0, keepdims=True)

        @pl.when(place < nseq - 1)
        def _():
            take_back(place + 1, 0)
            return_copy(g, place + 1).wait_recv()

        near = bt_acc[...].astype(bf16)
        near_norm = jnp.sum(bn_acc[...], axis=0, keepdims=True)
        gfk = jnp.concatenate(
            [
                gfk_acc[g, WIN:] + mm(vx[g, WIN:rows], near) + near_norm,
                hr_in[g, :, :FEAT].astype(f32) + mm(vx[g, rows:], far) + far_norm,
            ],
            axis=0,
        )
        gv = jnp.concatenate(
            [
                dv_acc[g, WIN:rows] + mm(fkb[g, WIN:rows], near, 1, 1),
                dv_acc[g, rows:]
                + hr_in[g, :, FEAT:].astype(f32)
                + mm(fkb[g, rows:], far, 1, 1),
            ],
            axis=0,
        )
        dl = soft_pair_grad(
            fkx[g, WIN:, :DH], fkx[g, WIN:, DH:], gfk[:, :DH], gfk[:, DH:]
        )
        gk_acc[g] = mm(dl, mk, 1, 1)
        gv_ref[:, g * DH : (g + 1) * DH] = gv.astype(bf16)
        gmk_acc[...] += mm(kx[g, WIN:], dl, 0, 0)

    scatter(1, gmk_acc[...])
    lax.fori_loop(half_way, kvl * nb, query_grads, 0, unroll=2)

    for g in range(kvl):

        @pl.when(place < nseq - 1)
        def _():
            key_copy(g, place + 1).wait_recv()

        cols = slice(g * DH, (g + 1) * DH)
        gk_ref[:tail, cols] = (dk_acc[g, WIN:rows] + gk_acc[g, :tail]).astype(bf16)
        gk_ref[tail:, cols] = (
            dk_acc[g, rows:] + gk_acc[g, tail:] + hk_in[g].astype(f32)
        ).astype(bf16)

    def as_owner(act, otherwise=None):
        if chunks == team:
            act()
            return
        pl.when(mine < chunks)(act)
        if otherwise is not None:
            pl.when(mine >= chunks)(otherwise)

    def total():
        span_copy(team - 1, mg_s, mg_r).wait_recv()
        mr[mine] = mg[mine]
        part = mr[0].astype(f32)
        for d in range(1, team):
            part = part + mr[d].astype(f32)
        tot[mine] = part.astype(bf16)

        def give(d, carry):
            total_copy((mine + d) % team).start()
            return carry

        lax.fori_loop(1, team, give, 0, unroll=min(team - 1, 15))

    as_owner(total)
    as_owner(
        span_copy(chunks - 1, tot_s, tot_r).wait_recv,
        span_copy(chunks, tot_s, tot_r).wait_recv,
    )
    for c in range(chunks):
        gm_ref[c * crows : (c + 1) * crows] = tot[c].astype(f32)

    @pl.when(place < nseq - 1)
    def _():
        halo_copy(place + 1).wait_send()

    for g in range(kvl):

        @pl.when(place < nseq - 1)
        def _():
            for copy in state_copies(0, g, place, place + 1):
                copy.wait_send()

        def far_sent(target, carry):
            for copy in state_copies(1, g, place, target):
                copy.wait_send()
            return carry

        lax.fori_loop(place + 2, nseq, far_sent, 0)

        @pl.when(place > 0)
        def _():
            return_copy(g, place - 1).wait_send()
            key_copy(g, place - 1).wait_send()

        def back_sent(lap, carry):
            for copy in back_copies(g, place, place - 1 - lap):
                copy.wait_send()
            return carry

        lax.fori_loop(0, place, back_sent, 0)

    as_owner(
        span_copy(chunks - 1, mg_s, mg_r).wait_send,
        span_copy(chunks, mg_s, mg_r).wait_send,
    )
    as_owner(span_copy(team - 1, tot_s, tot_r).wait_send)


def hand_over(gq, gk, gv, gm, gq_out, gk_out, gv_out, gmq_out, gmk_out, put):
    writes = []
    for held, target in [(gq, gq_out), (gk, gk_out), (gv, gv_out), (gm.at[:DH], gmq_out), (gm.at[DH:], gmk_out)]:
        write = pltpu.make_async_copy(held, target, put.at[len(writes)])
        write.start()
        writes.append(write)
    for write in writes:
        write.wait()


def shards(nseq, nhead, queries, key_vecs, value_vecs, teacher_out, map_query, map_key):
    rows = queries.shape[0]
    kvl = key_vecs.shape[1] // DH
    per = QH // KVH
    nb = rows // WIN
    units = kvl * nb
    team = nseq * nhead
    chunks = min(team, 2 * DH // 16)
    crows = 2 * DH // chunks
    vm = pltpu.VMEM
    dma = pltpu.SemaphoreType.DMA
    scratch = [
        vm(queries.shape, bf16),
        vm(key_vecs.shape, bf16),
        vm(value_vecs.shape, bf16),
        vm(queries.shape, bf16),
        vm(map_query.shape, bf16),
        vm(map_key.shape, bf16),
        dma((6,)),
        vm((kvl, rows + WIN, DH), bf16),
        vm((kvl, rows + WIN, DH), bf16),
        vm((kvl, rows + WIN, FEAT), f32),
        vm((kvl, rows + WIN, FEAT), bf16),
        vm((kvl, rows, FEAT), f32),
        vm((kvl, nb - 1, DH, FEAT), f32),
        vm((kvl, nb, DH, FEAT), bf16),
        vm((DH, DH), bf16),
        vm((FEAT, FEAT), bf16),
        vm((units, per * WIN, 2 * WIN), f32),
        vm((units, per * WIN, FEAT), f32),
        vm((units, per * WIN, 2 * WIN), f32),
        vm((units, per * WIN, FEAT), bf16),
        vm((units, per * WIN, DH), bf16),
        vm((units, per * WIN, DH), f32),
        vm((units, per * WIN, DH), f32),
        vm((units, per * WIN, DH), bf16),
        vm((kvl, rows, FEAT), f32),
        vm((kvl, rows + WIN, DH), f32),
        vm((kvl, rows + WIN, DH), f32),
        vm((kvl, rows, DH), f32),
        vm((DH, FEAT), f32),
        vm((8, FEAT), f32),
        vm((DH, DH), f32),
        vm((DH, DH), f32),
        vm((2 * kvl, WIN, DH), bf16),
        vm((2 * kvl, WIN, DH), bf16),
        vm((2, kvl, DH, FEAT), bf16),
        vm((nseq, kvl, DH, FEAT), bf16),
        vm((2, kvl, 8, FEAT), f32),
        vm((nseq, kvl, 8, FEAT), f32),
        vm((kvl, DH, FEAT), bf16),
        vm((nseq, kvl, DH, FEAT), bf16),
        vm((kvl, 8, FEAT), f32),
        vm((nseq, kvl, 8, FEAT), f32),
        vm((kvl, WIN, FEAT + DH), bf16),
        vm((kvl, WIN, FEAT + DH), bf16),
        vm((kvl, WIN, DH), bf16),
        vm((kvl, WIN, DH), bf16),
        vm((chunks, crows, DH), bf16),
        vm((team, crows, DH), bf16),
        vm((chunks, crows, DH), bf16),
        dma, dma,
        dma((kvl, nseq)), dma((kvl, nseq)), dma((kvl, nseq)), dma((kvl, nseq)),
        dma((kvl, nseq)), dma((kvl, nseq)), dma((kvl, nseq)), dma((kvl, nseq)),
        dma((kvl,)), dma((kvl,)), dma((kvl,)), dma((kvl,)),
        dma, dma, dma, dma,
    ]
    whole = pl.BlockSpec(memory_space=pltpu.VMEM)
    anywhere = pl.BlockSpec(memory_space=pl.ANY)
    queries, key_vecs, value_vecs, teacher_out, map_query, map_key = (
        pltpu.with_memory_space_constraint(x, pltpu.HBM)
        for x in (queries, key_vecs, value_vecs, teacher_out, map_query, map_key)
    )
    results = pl.pallas_call(
        functools.partial(kernel, nseq, nhead, rows, kvl, per),
        out_shape=(
            vm(queries.shape, bf16),
            vm(key_vecs.shape, bf16),
            vm(value_vecs.shape, bf16),
            vm((2 * DH, DH), f32),
        ),
        in_specs=[anywhere] * 6,
        out_specs=[whole, whole, whole, whole],
        scratch_shapes=scratch,
        compiler_params=pltpu.CompilerParams(
            collective_id=0, has_side_effects=True, vmem_limit_bytes=40 * 1024 * 1024
        ),
        name="transfer_step",
    )(queries, key_vecs, value_vecs, teacher_out, map_query, map_key)
    return pl.pallas_call(
        hand_over,
        out_shape=(
            jax.ShapeDtypeStruct(queries.shape, bf16),
            jax.ShapeDtypeStruct(key_vecs.shape, bf16),
            jax.ShapeDtypeStruct(value_vecs.shape, bf16),
            jax.ShapeDtypeStruct((DH, DH), f32),
            jax.ShapeDtypeStruct((DH, DH), f32),
        ),
        in_specs=[whole] * 4,
        out_specs=[anywhere] * 5,
        scratch_shapes=[dma((5,))],
        compiler_params=pltpu.CompilerParams(vmem_limit_bytes=1024 * 1024),
        name="hand_over",
    )(*results)


def solution(mesh):
    in_specs = (
        P(("grp", "seq"), "head"),
        P(("grp", "seq"), "head"),
        P(("grp", "seq"), "head"),
        P(("grp", "seq"), "head"),
        P(),
        P(),
    )
    out_specs = (
        P(("grp", "seq"), "head"),
        P(("grp", "seq"), "head"),
        P(("grp", "seq"), "head"),
        P("grp", None),
        P("grp", None),
    )
    body = functools.partial(shards, mesh.shape["seq"], mesh.shape["head"])
    return jax.shard_map(body, mesh=mesh, in_specs=in_specs, out_specs=out_specs, check_vma=False)
```

```python
import functools

import jax
import jax.numpy as jnp
from jax import lax
from jax.experimental import pallas as pl
from jax.experimental.pallas import tpu as pltpu
from jax.sharding import PartitionSpec as P

QH = 64
KVH = 8
DH = 128
WIN = 64
FEAT = 256
LOG2E = 1.4426950408889634

f32 = jnp.float32
bf16 = jnp.bfloat16
MESH = pl.DeviceIdType.MESH


def mm(a, b, ca=1, cb=0, precision=None):
    return lax.dot_general(
        a, b, (((ca,), (cb,)), ((), ())), preferred_element_type=f32, precision=precision
    )


def soft_pair(logits, ones):
    logits = logits * LOG2E
    up = jnp.exp2(logits - jnp.max(logits, axis=-1, keepdims=True))
    down = jnp.exp2(jnp.min(logits, axis=-1, keepdims=True) - logits)
    pair = jnp.concatenate([up, down], axis=-1)
    high = pair.astype(bf16)
    rest = (pair - high.astype(f32)).astype(bf16)
    return pair * (1.0 / (mm(high, ones) + mm(rest, ones)))


def soft_pair_grad(up, down, ga, gb):
    part_up = up * (ga - jnp.sum(up * ga, axis=-1, keepdims=True))
    part_down = down * (gb - jnp.sum(down * gb, axis=-1, keepdims=True))
    return (part_up - part_down).astype(bf16)


def kernel(
    nseq, nhead, rows, kvl, per,
    q_hbm, k_hbm, v_hbm, t_hbm, mq_hbm, mk_hbm,
    gq_ref, gk_ref, gv_ref, gm_ref,
    q_ref, k_ref, v_ref, t_ref, mq_ref, mk_ref, in_s,
    kx, vx, fkx, fkb, cum, pre, stb, kq, ones, p_scr, fq_scr, gp_scr,
    fqb_scr, go_scr, mix_scr, later_scr, latern_scr, inv_scr, slope_scr, dl_scr,
    gfk_acc, dv_acc, dk_acc, dk_scr, far_acc, farn_acc, nears, nearn, bt_acc, bn_acc, gmq_acc, gmk_acc,
    halo_out, halo_in, st_out, st_in, nm_out, nm_in,
    bt_out, bt_in, bn_out, bn_in, hr_out, hr_in, hk_out, hk_in, mg, mr, tot,
    halo_s, halo_r, st_s, st_r, nm_s, nm_r, bt_s, bt_r, bn_s, bn_r, hr_s, hr_r, hk_s, hk_r,
    mg_s, mg_r, tot_s, tot_r,
):
    nb = rows // WIN
    head_rows = per * WIN
    tail = rows - WIN
    chunks, _, _ = mg.shape
    crows = 2 * DH // chunks
    place = lax.axis_index("seq")
    mine = place * nhead + lax.axis_index("head")
    team = nseq * nhead
    scale = DH ** (-0.5)

    def remote(src, dst, send, recv, device):
        return pltpu.make_async_remote_copy(
            src_ref=src, dst_ref=dst, send_sem=send, recv_sem=recv,
            device_id=device, device_id_type=MESH,
        )

    barrier = pltpu.get_barrier_semaphore()

    def peer(n):
        return {"seq": n // nhead, "head": n % nhead}

    loads = [
        pltpu.make_async_copy(source, held, in_s.at[n])
        for n, (source, held) in enumerate(
            [(k_hbm, k_ref), (v_hbm, v_ref), (mk_hbm, mk_ref), (q_hbm, q_ref), (mq_hbm, mq_ref), (t_hbm, t_ref)]
        )
    ]
    for load in loads:
        load.start()
    def hail(d, carry):
        pl.semaphore_signal(barrier, inc=1, device_id=peer((mine + d) % team), device_id_type=MESH)
        return carry

    lax.fori_loop(1, team, hail, 0, unroll=min(team - 1, 15))

    for load in loads[:3]:
        load.wait()

    for g in range(kvl):
        cols = slice(g * DH, (g + 1) * DH)
        kx[g, WIN:] = k_ref[:, cols]
        vx[g, WIN:] = v_ref[:, cols]
        halo_out[g] = k_ref[tail:, cols]
        halo_out[kvl + g] = v_ref[tail:, cols]

    def halo_copy(target):
        return remote(halo_out, halo_in, halo_s, halo_r, {"seq": target})

    def state_copies(slot, g, source, target):
        return (
            remote(st_out.at[slot, g], st_in.at[source, g], st_s.at[g, target], st_r.at[g, source],
                   {"seq": target}),
            remote(nm_out.at[slot, g], nm_in.at[source, g], nm_s.at[g, target], nm_r.at[g, source],
                   {"seq": target}),
        )

    mk = mk_ref[...]
    side = lax.broadcasted_iota(jnp.int32, (FEAT, FEAT), 0) < DH
    ones[...] = (side == (lax.broadcasted_iota(jnp.int32, (FEAT, FEAT), 1) < DH)).astype(bf16)

    def key_features(keys):
        return soft_pair(mm(keys, mk), ones[...])

    for g in range(kvl):
        fk = key_features(kx[g, WIN:])
        fkx[g, WIN:] = fk
        fkl = fk.astype(bf16)
        fkb[g, WIN:] = fkl
        early = mm(vx[g, WIN:rows], fkl[:tail], 0, 0)
        late = mm(vx[g, rows:], fkl[tail:], 0, 0)
        st_out[0, g] = early.astype(bf16)
        st_out[1, g] = (early + late).astype(bf16)
        n_early = jnp.sum(fk[:tail].reshape(tail // 8, 8, FEAT), axis=0)
        n_late = jnp.sum(fk[tail:].reshape(WIN // 8, 8, FEAT), axis=0)
        nm_out[0, g] = n_early
        nm_out[1, g] = n_early + n_late

    pl.semaphore_wait(barrier, team - 1)

    @pl.when(place < nseq - 1)
    def _():
        halo_copy(place + 1).start()

    def send_states(g):
        @pl.when(place < nseq - 1)
        def _():
            for copy in state_copies(0, g, place, place + 1):
                copy.start()

        def send_far(target, carry):
            for copy in state_copies(1, g, place, target):
                copy.start()
            return carry

        lax.fori_loop(place + 2, nseq, send_far, 0)

    send_states(0)

    ia = lax.broadcasted_iota(jnp.int32, (WIN, 2 * WIN), 0)
    ie = lax.broadcasted_iota(jnp.int32, (WIN, 2 * WIN), 1)
    lag_mask = (ie <= ia)[None]

    def stacked(ref, g, b, h0, hs):
        return jnp.concatenate(
            [
                ref[pl.ds(b * WIN, WIN), pl.ds(pl.multiple_of((g * per + h) * DH, DH), DH)]
                for h in range(h0, h0 + hs)
            ],
            axis=0,
        )

    def cube(x):
        return x.reshape(x.shape[0] // WIN, WIN, x.shape[-1])

    def plain(x):
        return x.reshape(x.shape[0] * WIN, x.shape[-1])

    def forward(lap, carry):
        b = (lap // kvl + 1) % nb
        g = lap % kvl
        unit = g * nb + b
        kw = kx[g, pl.ds(b * WIN, 2 * WIN)]
        first_key = jnp.where(place > 0, 0, WIN) - b * WIN
        seen = ((ie > ia) & (ie <= ia + WIN) & (ie >= first_key))[None]
        for h0 in range(0, per, per):
            part = slice(h0 * WIN, (h0 + per) * WIN)
            qs = stacked(q_ref, g, b, h0, per)
            both = mm(qs, jnp.concatenate([kq[...], kw], axis=0), 1, 1)
            fq_scr[unit, part] = soft_pair(both[:, :DH], ones[...])
            scores = jnp.where(seen, cube(both[:, DH:]) * (scale * LOG2E), -jnp.inf)
            weights = jnp.exp2(scores - jnp.max(scores, axis=-1, keepdims=True))
            weights = plain(weights).astype(bf16)
            p_scr[unit, part] = weights.astype(f32) * (1.0 / mm(weights, ones[:DH, :DH]))
        return carry

    loads[3].wait()
    loads[4].wait()
    kq[...] = mq_ref[...].T
    lax.fori_loop(0, 2, forward, 0, unroll=2)
    for g in range(1, kvl):
        send_states(g)
    lax.fori_loop(2, kvl * (nb - 1), forward, 0, unroll=4)

    @pl.when(place > 0)
    def _():
        halo_copy(place - 1).wait_recv()

    @pl.when(place == 0)
    def _():
        halo_in[...] = jnp.zeros_like(halo_in)

    has_before = (place > 0).astype(f32)
    for g in range(kvl):
        kx[g, :WIN] = halo_in[g]
        vx[g, :WIN] = halo_in[kvl + g]
        fk = key_features(halo_in[g]) * has_before
        fkx[g, :WIN] = fk
        fkb[g, :WIN] = fk.astype(bf16)

    lax.fori_loop(kvl * (nb - 1), kvl * nb, forward, 0, unroll=kvl)

    ra = lax.broadcasted_iota(jnp.int32, (rows, rows), 0)
    re = lax.broadcasted_iota(jnp.int32, (rows, rows), 1)
    lower = (re <= ra).astype(bf16)
    for g in range(kvl):
        high = fkb[g, :rows]
        rest = (fkx[g, :rows] - high.astype(f32)).astype(bf16)
        cum[g] = mm(lower, high) + mm(lower, rest)
        for b in range(nb - 1):
            part = slice(b * WIN, (b + 1) * WIN)
            pre[g, b] = mm(vx[g, part], fkb[g, part], 0, 0)

    gmq_acc[...] = jnp.zeros_like(gmq_acc)
    dv_acc[...] = jnp.zeros_like(dv_acc)
    dk_acc[...] = jnp.zeros_like(dk_acc)

    def back_copies(g, source, target):
        return (
            remote(bt_out.at[g], bt_in.at[source, g], bt_s.at[g, target], bt_r.at[g, source],
                   {"seq": target}),
            remote(bn_out.at[g], bn_in.at[source, g], bn_s.at[g, target], bn_r.at[g, source],
                   {"seq": target}),
        )

    def return_copy(g, target):
        return remote(hr_out.at[g], hr_in.at[g], hr_s.at[g], hr_r.at[g], {"seq": target})

    def key_copy(g, target):
        return remote(hk_out.at[g], hk_in.at[g], hk_s.at[g], hk_r.at[g], {"seq": target})

    def group(g, carry):
        bt_acc[...] = jnp.zeros_like(bt_acc)
        bn_acc[...] = jnp.zeros_like(bn_acc)

        def take_state(source, inner):
            for copy in state_copies(0, g, source, source):
                copy.wait_recv()
            bt_acc[...] += st_in[source, g].astype(f32)
            bn_acc[...] += nm_in[source, g]
            return inner

        lax.fori_loop(0, place, take_state, 0)
        cum[g] = cum[g] + jnp.sum(bn_acc[...], axis=0, keepdims=True)
        running = bt_acc[...]
        for b in range(nb):
            stb[g, b] = running.astype(bf16)
            if b < nb - 1:
                running = running + pre[g, b]
        bt_acc[...] = jnp.zeros_like(bt_acc)
        bn_acc[...] = jnp.zeros_like(bn_acc)

        def block(lap, inner):
            b = nb - 1 - lap
            unit = g * nb + b
            here = pl.ds(b * WIN, WIN)
            span = pl.ds(b * WIN, 2 * WIN)
            cumb = cum[g, here][None]
            vw = vx[g, span]
            fkw = fkb[g, span]
            state = stb[g, b]
            back = jnp.concatenate([state, fkw], axis=0)
            fq = cube(fq_scr[unit])
            den = jnp.sum(fq * cumb, axis=-1, keepdims=True)
            above = den > 1.0
            inv = 1.0 / jnp.where(above, den, 1.0)
            fqn = fq * inv
            fqb = plain(fqn).astype(bf16)
            far = mm(fqb, back, 1, 1)
            kin = cube(far[:, DH:])
            mixer = plain(jnp.where(lag_mask, kin, cube(p_scr[unit]))).astype(bf16)
            mix = mm(mixer, vw) + far[:, :DH]
            go = (mix - stacked(t_ref, g, b, 0, per).astype(f32)).astype(bf16)
            gp = mm(go, vw, 1, 1)
            pull = cube(go.astype(f32) * far[:, :DH]) + jnp.where(lag_mask, kin * cube(gp), 0.0)
            slope = jnp.where(above, -jnp.sum(pull, axis=-1, keepdims=True), 0.0)
            fqb_scr[unit] = fqb
            go_scr[unit] = go
            gp_scr[unit] = gp
            inv_scr[unit] = plain(jnp.broadcast_to(inv, (per, WIN, DH)))
            slope_scr[unit] = plain(jnp.broadcast_to(slope, (per, WIN, DH)))
            mix_scr[unit] = mixer
            gt = mm(go, fqb, 0, 0)
            later_scr[unit] = bt_acc[...].astype(bf16)
            latern_scr[unit] = bn_acc[...]
            bt_acc[...] += gt
            bn_acc[...] += jnp.sum(plain(fqn * slope).reshape(head_rows // 8, 8, FEAT), axis=0)
            return inner

        lax.fori_loop(0, nb, block, 0, unroll=4)
        bt_out[g] = bt_acc[...].astype(bf16)
        bn_out[g] = bn_acc[...]

        def send_back(lap, inner):
            for copy in back_copies(g, place, place - 1 - lap):
                copy.start()
            return inner

        lax.fori_loop(0, place, send_back, 0)
        return carry

    loads[5].wait()
    lax.fori_loop(0, kvl, group, 0)

    def logit_grads(lap, carry):
        b = lap // kvl
        g = lap % kvl
        unit = g * nb + b
        here = pl.ds(b * WIN, WIN)
        fq = fq_scr[unit]
        go = go_scr[unit]
        gp = cube(gp_scr[unit])
        inv = inv_scr[unit]
        slope = slope_scr[unit]
        gin = plain(jnp.where(lag_mask, gp, 0.0)).astype(bf16)
        back = jnp.concatenate([stb[g, b], fkb[g, pl.ds(b * WIN, 2 * WIN)]], axis=0)
        gf = mm(jnp.concatenate([go, gin], axis=-1), back)
        up_side = plain(cube(gf[:, :DH]) + cube(slope) * cum[g, here, :DH][None]) * inv
        down_side = plain(cube(gf[:, DH:]) + cube(slope) * cum[g, here, DH:][None]) * inv
        dl = soft_pair_grad(fq[:, :DH], fq[:, DH:], up_side, down_side)
        dl_scr[unit] = dl
        gmq_acc[...] += mm(stacked(q_ref, g, b, 0, per), dl, 0, 0)
        gker = plain(jnp.where(lag_mask, gp + cube(slope), 0.0)).astype(bf16)
        later = later_scr[unit]
        gfk_acc[g, here] = (
            mm(gker, fqb_scr[unit], 0, 0)[:WIN]
            + mm(vx[g, here], later)
            + jnp.sum(latern_scr[unit], axis=0, keepdims=True)
        )
        gt = mm(go, mix_scr[unit], 0, 0)
        dv_acc[g, pl.ds(b * WIN, 2 * WIN)] += gt.T
        dv_acc[g, here] += mm(fkb[g, here], later, 1, 1)
        return carry

    lax.fori_loop(0, kvl, logit_grads, 0, unroll=kvl)
    for g in range(kvl):
        hr_out[g, :, :FEAT] = gfk_acc[g, :WIN].astype(bf16)
        hr_out[g, :, FEAT:] = dv_acc[g, :WIN].astype(bf16)

        @pl.when(place > 0)
        def _():
            return_copy(g, place - 1).start()

    lax.fori_loop(kvl, kvl * nb, logit_grads, 0, unroll=2)

    def each_owner(first, last, visit):
        def one(c, carry):
            @pl.when(c != mine)
            def _():
                visit(c)

            return carry

        lax.fori_loop(first, last, one, 0, unroll=8)

    def part_copy(chunk):
        return remote(mg.at[chunk], mr.at[mine], mg_s, mg_r, peer(chunk))

    def total_copy(target):
        return remote(tot.at[mine], tot.at[mine], tot_s, tot_r, peer(target))

    def span_copy(count, send, recv):
        refs = mr.at[pl.ds(0, count)]
        return remote(refs, refs, send, recv, peer((mine + 1) % team))

    def scatter(which, part):
        half = chunks // 2
        for c in range(half):
            mg[which * half + c] = part[c * crows : (c + 1) * crows].astype(bf16)
        each_owner(which * half, which * half + half, lambda c: part_copy(c).start())

    scatter(0, gmq_acc[...])

    def query_grads(lap, carry):
        b = lap // kvl
        g = lap % kvl
        unit = g * nb + b
        here = pl.ds(b * WIN, WIN)
        span = pl.ds(b * WIN, 2 * WIN)
        for h0 in range(0, per, per):
            part = slice(h0 * WIN, (h0 + per) * WIN)
            probs = p_scr[unit, part]
            gp = gp_scr[unit, part]
            ds = (probs * (gp - jnp.sum(probs * gp, axis=-1, keepdims=True)) * scale).astype(bf16)
            gq = mm(
                jnp.concatenate([dl_scr[unit, part], ds], axis=-1),
                jnp.concatenate([kq[...], kx[g, span]], axis=0),
            ).astype(bf16)
            for h in range(per):
                gq_ref[here, pl.ds(pl.multiple_of((g * per + h0 + h) * DH, DH), DH)] = gq[
                    h * WIN : (h + 1) * WIN
                ]
            dk_acc[g, span] += mm(ds, stacked(q_ref, g, b, h0, per), 0, 0)
        return carry

    lax.fori_loop(0, kvl, query_grads, 0, unroll=kvl)
    for g in range(kvl):
        hk_out[g] = dk_acc[g, :WIN].astype(bf16)

        @pl.when(place > 0)
        def _():
            key_copy(g, place - 1).start()

    half_way = kvl * nb // 2
    lax.fori_loop(kvl, half_way, query_grads, 0, unroll=2)

    @pl.when(place == nseq - 1)
    def _():
        hr_in[...] = jnp.zeros_like(hr_in)
        hk_in[...] = jnp.zeros_like(hk_in)

    for g in range(kvl):

        def take_back(source, carry):
            for copy in back_copies(g, source, source):
                copy.wait_recv()
            far_acc[g] += bt_in[source, g].astype(f32)
            farn_acc[g] += bn_in[source, g]
            return carry

        far_acc[g] = jnp.zeros((DH, FEAT), f32)
        farn_acc[g] = jnp.zeros((8, FEAT), f32)
        lax.fori_loop(place + 2, nseq, take_back, 0)
        nears[kvl + g] = far_acc[g].astype(bf16)
        nearn[kvl + g] = farn_acc[g]

        @pl.when(place < nseq - 1)
        def _():
            take_back(place + 1, 0)
            return_copy(g, place + 1).wait_recv()

    gmk = jnp.zeros((DH, DH), f32)
    for g in range(kvl):
        near = far_acc[g].astype(bf16)
        nears[g] = near
        gfk = jnp.concatenate(
            [
                gfk_acc[g, WIN:]
                + mm(vx[g, WIN:rows], near)
                + jnp.sum(farn_acc[g], axis=0, keepdims=True),
                hr_in[g, :, :FEAT].astype(f32)
                + mm(vx[g, rows:], nears[kvl + g])
                + jnp.sum(nearn[kvl + g], axis=0, keepdims=True),
            ],
            axis=0,
        )
        dl = soft_pair_grad(
            fkx[g, WIN:, :DH], fkx[g, WIN:, DH:], gfk[:, :DH], gfk[:, DH:]
        )
        dk_scr[g] = dl
        gmk = gmk + mm(kx[g, WIN:], dl, 0, 0)
    gmk_acc[...] = gmk

    scatter(1, gmk_acc[...])
    lax.fori_loop(half_way, kvl * nb, query_grads, 0, unroll=2)

    for g in range(kvl):

        @pl.when(place < nseq - 1)
        def _():
            key_copy(g, place + 1).wait_recv()

        cols = slice(g * DH, (g + 1) * DH)
        gv = jnp.concatenate(
            [
                dv_acc[g, WIN:rows] + mm(fkb[g, WIN:rows], nears[g], 1, 1),
                dv_acc[g, rows:]
                + hr_in[g, :, FEAT:].astype(f32)
                + mm(fkb[g, rows:], nears[kvl + g], 1, 1),
            ],
            axis=0,
        )
        gv_ref[:, cols] = gv.astype(bf16)
        gkl = mm(dk_scr[g], mk, 1, 1)
        gk_ref[:tail, cols] = (dk_acc[g, WIN:rows] + gkl[:tail]).astype(bf16)
        gk_ref[tail:, cols] = (
            dk_acc[g, rows:] + gkl[tail:] + hk_in[g].astype(f32)
        ).astype(bf16)

    def as_owner(act, otherwise=None):
        if chunks == team:
            act()
            return
        pl.when(mine < chunks)(act)
        if otherwise is not None:
            pl.when(mine >= chunks)(otherwise)

    def total():
        span_copy(team - 1, mg_s, mg_r).wait_recv()
        mr[mine] = mg[mine]
        part = mr[0].astype(f32)
        for d in range(1, team):
            part = part + mr[d].astype(f32)
        tot[mine] = part.astype(bf16)

        def give(d, carry):
            total_copy((mine + d) % team).start()
            return carry

        lax.fori_loop(1, team, give, 0, unroll=min(team - 1, 15))

    as_owner(total)
    @pl.when(place < nseq - 1)
    def _():
        halo_copy(place + 1).wait_send()

    for g in range(kvl):

        @pl.when(place < nseq - 1)
        def _():
            for copy in state_copies(0, g, place, place + 1):
                copy.wait_send()

        def far_sent(target, carry):
            for copy in state_copies(1, g, place, target):
                copy.wait_send()
            return carry

        lax.fori_loop(place + 2, nseq, far_sent, 0)

        @pl.when(place > 0)
        def _():
            return_copy(g, place - 1).wait_send()
            key_copy(g, place - 1).wait_send()

        def back_sent(lap, carry):
            for copy in back_copies(g, place, place - 1 - lap):
                copy.wait_send()
            return carry

        lax.fori_loop(0, place, back_sent, 0)

    as_owner(
        span_copy(chunks - 1, mg_s, mg_r).wait_send,
        span_copy(chunks, mg_s, mg_r).wait_send,
    )
    as_owner(
        span_copy(chunks - 1, tot_s, tot_r).wait_recv,
        span_copy(chunks, tot_s, tot_r).wait_recv,
    )
    for c in range(chunks):
        gm_ref[c * crows : (c + 1) * crows] = tot[c].astype(f32)

    as_owner(span_copy(team - 1, tot_s, tot_r).wait_send)


def hand_over(gq, gk, gv, gm, gq_out, gk_out, gv_out, gmq_out, gmk_out, put):
    writes = []
    for held, target in [(gq, gq_out), (gk, gk_out), (gv, gv_out), (gm.at[:DH], gmq_out), (gm.at[DH:], gmk_out)]:
        write = pltpu.make_async_copy(held, target, put.at[len(writes)])
        write.start()
        writes.append(write)
    for write in writes:
        write.wait()


def shards(nseq, nhead, queries, key_vecs, value_vecs, teacher_out, map_query, map_key):
    rows = queries.shape[0]
    kvl = key_vecs.shape[1] // DH
    per = QH // KVH
    nb = rows // WIN
    units = kvl * nb
    team = nseq * nhead
    chunks = min(team, 2 * DH // 16)
    crows = 2 * DH // chunks
    vm = pltpu.VMEM
    dma = pltpu.SemaphoreType.DMA
    scratch = [
        vm(queries.shape, bf16),
        vm(key_vecs.shape, bf16),
        vm(value_vecs.shape, bf16),
        vm(queries.shape, bf16),
        vm(map_query.shape, bf16),
        vm(map_key.shape, bf16),
        dma((6,)),
        vm((kvl, rows + WIN, DH), bf16),
        vm((kvl, rows + WIN, DH), bf16),
        vm((kvl, rows + WIN, FEAT), f32),
        vm((kvl, rows + WIN, FEAT), bf16),
        vm((kvl, rows, FEAT), f32),
        vm((kvl, nb - 1, DH, FEAT), f32),
        vm((kvl, nb, DH, FEAT), bf16),
        vm((DH, DH), bf16),
        vm((FEAT, FEAT), bf16),
        vm((units, per * WIN, 2 * WIN), f32),
        vm((units, per * WIN, FEAT), f32),
        vm((units, per * WIN, 2 * WIN), f32),
        vm((units, per * WIN, FEAT), bf16),
        vm((units, per * WIN, DH), bf16),
        vm((units, per * WIN, DH), bf16),
        vm((units, DH, FEAT), bf16),
        vm((units, 8, FEAT), f32),
        vm((units, per * WIN, DH), f32),
        vm((units, per * WIN, DH), f32),
        vm((units, per * WIN, DH), bf16),
        vm((kvl, rows, FEAT), f32),
        vm((kvl, rows + WIN, DH), f32),
        vm((kvl, rows + WIN, DH), f32),
        vm((kvl, rows, DH), bf16),
        vm((kvl, DH, FEAT), f32),
        vm((kvl, 8, FEAT), f32),
        vm((2 * kvl, DH, FEAT), bf16),
        vm((2 * kvl, 8, FEAT), f32),
        vm((DH, FEAT), f32),
        vm((8, FEAT), f32),
        vm((DH, DH), f32),
        vm((DH, DH), f32),
        vm((2 * kvl, WIN, DH), bf16),
        vm((2 * kvl, WIN, DH), bf16),
        vm((2, kvl, DH, FEAT), bf16),
        vm((nseq, kvl, DH, FEAT), bf16),
        vm((2, kvl, 8, FEAT), f32),
        vm((nseq, kvl, 8, FEAT), f32),
        vm((kvl, DH, FEAT), bf16),
        vm((nseq, kvl, DH, FEAT), bf16),
        vm((kvl, 8, FEAT), f32),
        vm((nseq, kvl, 8, FEAT), f32),
        vm((kvl, WIN, FEAT + DH), bf16),
        vm((kvl, WIN, FEAT + DH), bf16),
        vm((kvl, WIN, DH), bf16),
        vm((kvl, WIN, DH), bf16),
        vm((chunks, crows, DH), bf16),
        vm((team, crows, DH), bf16),
        vm((chunks, crows, DH), bf16),
        dma, dma,
        dma((kvl, nseq)), dma((kvl, nseq)), dma((kvl, nseq)), dma((kvl, nseq)),
        dma((kvl, nseq)), dma((kvl, nseq)), dma((kvl, nseq)), dma((kvl, nseq)),
        dma((kvl,)), dma((kvl,)), dma((kvl,)), dma((kvl,)),
        dma, dma, dma, dma,
    ]
    whole = pl.BlockSpec(memory_space=pltpu.VMEM)
    anywhere = pl.BlockSpec(memory_space=pl.ANY)
    queries, key_vecs, value_vecs, teacher_out, map_query, map_key = (
        pltpu.with_memory_space_constraint(x, pltpu.HBM)
        for x in (queries, key_vecs, value_vecs, teacher_out, map_query, map_key)
    )
    results = pl.pallas_call(
        functools.partial(kernel, nseq, nhead, rows, kvl, per),
        out_shape=(
            vm(queries.shape, bf16),
            vm(key_vecs.shape, bf16),
            vm(value_vecs.shape, bf16),
            vm((2 * DH, DH), f32),
        ),
        in_specs=[anywhere] * 6,
        out_specs=[whole, whole, whole, whole],
        scratch_shapes=scratch,
        compiler_params=pltpu.CompilerParams(
            collective_id=0, has_side_effects=True, vmem_limit_bytes=40 * 1024 * 1024
        ),
        name="transfer_step",
    )(queries, key_vecs, value_vecs, teacher_out, map_query, map_key)
    return pl.pallas_call(
        hand_over,
        out_shape=(
            jax.ShapeDtypeStruct(queries.shape, bf16),
            jax.ShapeDtypeStruct(key_vecs.shape, bf16),
            jax.ShapeDtypeStruct(value_vecs.shape, bf16),
            jax.ShapeDtypeStruct((DH, DH), f32),
            jax.ShapeDtypeStruct((DH, DH), f32),
        ),
        in_specs=[whole] * 4,
        out_specs=[anywhere] * 5,
        scratch_shapes=[dma((5,))],
        compiler_params=pltpu.CompilerParams(vmem_limit_bytes=1024 * 1024),
        name="hand_over",
    )(*results)


def solution(mesh):
    in_specs = (
        P(("grp", "seq"), "head"),
        P(("grp", "seq"), "head"),
        P(("grp", "seq"), "head"),
        P(("grp", "seq"), "head"),
        P(),
        P(),
    )
    out_specs = (
        P(("grp", "seq"), "head"),
        P(("grp", "seq"), "head"),
        P(("grp", "seq"), "head"),
        P("grp", None),
        P("grp", None),
    )
    body = functools.partial(shards, mesh.shape["seq"], mesh.shape["head"])
    return jax.shard_map(body, mesh=mesh, in_specs=in_specs, out_specs=out_specs, check_vma=False)
```

```python
import functools

import jax
import jax.numpy as jnp
from jax import lax
from jax.experimental import pallas as pl
from jax.experimental.pallas import tpu as pltpu
from jax.sharding import PartitionSpec as P

QH = 64
KVH = 8
DH = 128
WIN = 64
FEAT = 256
LOG2E = 1.4426950408889634

f32 = jnp.float32
bf16 = jnp.bfloat16
MESH = pl.DeviceIdType.MESH


def mm(a, b, ca=1, cb=0, precision=None):
    return lax.dot_general(
        a, b, (((ca,), (cb,)), ((), ())), preferred_element_type=f32, precision=precision
    )


def soft_pair(logits, ones):
    logits = logits * LOG2E
    up = jnp.exp2(logits - jnp.max(logits, axis=-1, keepdims=True))
    down = jnp.exp2(jnp.min(logits, axis=-1, keepdims=True) - logits)
    pair = jnp.concatenate([up, down], axis=-1)
    high = pair.astype(bf16)
    rest = (pair - high.astype(f32)).astype(bf16)
    return pair * (1.0 / (mm(high, ones) + mm(rest, ones)))


def norm_rows(partial):
    total = jnp.sum(partial, axis=0, keepdims=True)
    row = lax.broadcasted_iota(jnp.int32, (16, total.shape[1]), 0)
    out = jnp.zeros((16, total.shape[1]), f32)
    for n in range(3):
        piece = total.astype(bf16).astype(f32)
        out = jnp.where(row == n, piece, out)
        total = total - piece
    return out.astype(bf16)


def rows_norm(rows):
    rows = rows.astype(f32)
    return rows[:8] + rows[8:]


def soft_pair_grad(up, down, ga, gb):
    part_up = up * (ga - jnp.sum(up * ga, axis=-1, keepdims=True))
    part_down = down * (gb - jnp.sum(down * gb, axis=-1, keepdims=True))
    return (part_up - part_down).astype(bf16)


def kernel(
    nseq, nhead, rows, kvl, per,
    q_hbm, k_hbm, v_hbm, t_hbm, mq_hbm, mk_hbm,
    gq_ref, gk_ref, gv_ref, gm_ref,
    q_ref, k_ref, v_ref, t_ref, mq_ref, mk_ref, in_s,
    kx, vx, fkx, fkb, cum, pre, stb, kq, ones, p_scr, fq_scr, gp_scr,
    fqb_scr, go_scr, mix_scr, later_scr, latern_scr, inv_scr, slope_scr, dl_scr,
    gfk_acc, dv_acc, dk_acc, dk_scr, far_acc, farn_acc, nears, nearn, bt_acc, bn_acc, gmq_acc, gmk_acc,
    halo_out, halo_in, st_out, st_in, bt_out, bt_in, hr_out, hr_in, hk_out, hk_in, mg, mr, tot,
    halo_s, halo_r, st_s, st_r, bt_s, bt_r, hr_s, hr_r, hk_s, hk_r,
    mg_s, mg_r, tot_s, tot_r,
):
    nb = rows // WIN
    head_rows = per * WIN
    tail = rows - WIN
    chunks, _, _ = mg.shape
    crows = 2 * DH // chunks
    place = lax.axis_index("seq")
    lane = lax.axis_index("head")
    mine = place * nhead + lane
    team = nseq * nhead
    scale = DH ** (-0.5)

    def remote(src, dst, send, recv, device):
        return pltpu.make_async_remote_copy(
            src_ref=src, dst_ref=dst, send_sem=send, recv_sem=recv,
            device_id=device, device_id_type=MESH,
        )

    barrier = pltpu.get_barrier_semaphore()

    def peer(n):
        return {"seq": n // nhead, "head": n % nhead}

    loads = [
        pltpu.make_async_copy(source, held, in_s.at[n])
        for n, (source, held) in enumerate(
            [(k_hbm, k_ref), (v_hbm, v_ref), (mk_hbm, mk_ref), (q_hbm, q_ref), (mq_hbm, mq_ref), (t_hbm, t_ref)]
        )
    ]
    for load in loads:
        load.start()
    def each_peer(visit):
        for dh in range(nhead):
            h = (lane + dh) % nhead
            for ds in range(nseq):
                if ds or dh:
                    visit({"seq": (place + ds) % nseq, "head": h})

    each_peer(
        lambda device: pl.semaphore_signal(barrier, inc=1, device_id=device, device_id_type=MESH)
    )

    for load in loads[:3]:
        load.wait()

    for g in range(kvl):
        cols = slice(g * DH, (g + 1) * DH)
        kx[g, WIN:] = k_ref[:, cols]
        vx[g, WIN:] = v_ref[:, cols]
        halo_out[g] = k_ref[tail:, cols]
        halo_out[kvl + g] = v_ref[tail:, cols]

    def halo_copy(target):
        return remote(halo_out, halo_in, halo_s, halo_r, {"seq": target})

    def state_copies(slot, g, source, target):
        return (
            remote(st_out.at[slot, g], st_in.at[source, g], st_s.at[g, target], st_r.at[g, source],
                   {"seq": target}),
        )

    mk = mk_ref[...]
    side = lax.broadcasted_iota(jnp.int32, (FEAT, FEAT), 0) < DH
    ones[...] = (side == (lax.broadcasted_iota(jnp.int32, (FEAT, FEAT), 1) < DH)).astype(bf16)

    def key_features(keys):
        return soft_pair(mm(keys, mk), ones[...])

    for g in range(kvl):
        fk = key_features(kx[g, WIN:])
        fkx[g, WIN:] = fk
        fkl = fk.astype(bf16)
        fkb[g, WIN:] = fkl
        early = mm(vx[g, WIN:rows], fkl[:tail], 0, 0)
        late = mm(vx[g, rows:], fkl[tail:], 0, 0)
        st_out[0, g, :DH] = early.astype(bf16)
        st_out[1, g, :DH] = (early + late).astype(bf16)
        n_early = jnp.sum(fk[:tail].reshape(tail // 8, 8, FEAT), axis=0)
        n_late = jnp.sum(fk[tail:].reshape(WIN // 8, 8, FEAT), axis=0)
        st_out[0, g, DH:] = norm_rows(n_early)
        st_out[1, g, DH:] = norm_rows(n_early + n_late)

    pl.semaphore_wait(barrier, team - 1)

    @pl.when(place < nseq - 1)
    def _():
        halo_copy(place + 1).start()

    def send_states(g):
        @pl.when(place < nseq - 1)
        def _():
            for copy in state_copies(0, g, place, place + 1):
                copy.start()

        def send_far(target, carry):
            for copy in state_copies(1, g, place, target):
                copy.start()
            return carry

        lax.fori_loop(place + 2, nseq, send_far, 0)

    send_states(0)

    ia = lax.broadcasted_iota(jnp.int32, (WIN, 2 * WIN), 0)
    ie = lax.broadcasted_iota(jnp.int32, (WIN, 2 * WIN), 1)
    lag_mask = (ie <= ia)[None]

    def stacked(ref, g, b, h0, hs):
        return jnp.concatenate(
            [
                ref[pl.ds(b * WIN, WIN), pl.ds(pl.multiple_of((g * per + h) * DH, DH), DH)]
                for h in range(h0, h0 + hs)
            ],
            axis=0,
        )

    def cube(x):
        return x.reshape(x.shape[0] // WIN, WIN, x.shape[-1])

    def plain(x):
        return x.reshape(x.shape[0] * WIN, x.shape[-1])

    def forward(lap, carry):
        b = (lap // kvl + 1) % nb
        g = lap % kvl
        unit = g * nb + b
        kw = kx[g, pl.ds(b * WIN, 2 * WIN)]
        first_key = jnp.where(place > 0, 0, WIN) - b * WIN
        seen = ((ie > ia) & (ie <= ia + WIN) & (ie >= first_key))[None]
        for h0 in range(0, per, per):
            part = slice(h0 * WIN, (h0 + per) * WIN)
            qs = stacked(q_ref, g, b, h0, per)
            both = mm(qs, jnp.concatenate([kq[...], kw], axis=0), 1, 1)
            fq_scr[unit, part] = soft_pair(both[:, :DH], ones[...])
            scores = jnp.where(seen, cube(both[:, DH:]) * (scale * LOG2E), -jnp.inf)
            weights = jnp.exp2(scores - jnp.max(scores, axis=-1, keepdims=True))
            weights = plain(weights).astype(bf16)
            probs = weights.astype(f32) * (1.0 / mm(weights, ones[:DH, :DH]))
            p_scr[unit, part] = probs
            mix = mm(probs.astype(bf16), vx[g, pl.ds(b * WIN, 2 * WIN)])
            gp_scr[unit, part] = mix - stacked(t_ref, g, b, 0, per).astype(f32)
        return carry

    loads[3].wait()
    loads[4].wait()
    loads[5].wait()
    kq[...] = mq_ref[...].T
    lax.fori_loop(0, 2, forward, 0, unroll=2)
    for g in range(1, kvl):
        send_states(g)
    lax.fori_loop(2, kvl * (nb - 1), forward, 0, unroll=4)

    @pl.when(place > 0)
    def _():
        halo_copy(place - 1).wait_recv()

    @pl.when(place == 0)
    def _():
        halo_in[...] = jnp.zeros_like(halo_in)

    has_before = (place > 0).astype(f32)
    for g in range(kvl):
        kx[g, :WIN] = halo_in[g]
        vx[g, :WIN] = halo_in[kvl + g]
        fk = key_features(halo_in[g]) * has_before
        fkx[g, :WIN] = fk
        fkb[g, :WIN] = fk.astype(bf16)

    lax.fori_loop(kvl * (nb - 1), kvl * nb, forward, 0, unroll=kvl)

    ra = lax.broadcasted_iota(jnp.int32, (rows, rows), 0)
    re = lax.broadcasted_iota(jnp.int32, (rows, rows), 1)
    lower = (re <= ra).astype(bf16)
    for g in range(kvl):
        high = fkb[g, :rows]
        rest = (fkx[g, :rows] - high.astype(f32)).astype(bf16)
        cum[g] = mm(lower, high) + mm(lower, rest)
        for b in range(nb - 1):
            part = slice(b * WIN, (b + 1) * WIN)
            pre[g, b] = mm(vx[g, part], fkb[g, part], 0, 0)

    gmq_acc[...] = jnp.zeros_like(gmq_acc)
    dv_acc[...] = jnp.zeros_like(dv_acc)
    dk_acc[...] = jnp.zeros_like(dk_acc)

    def back_copies(g, source, target):
        return (
            remote(bt_out.at[g], bt_in.at[source, g], bt_s.at[g, target], bt_r.at[g, source],
                   {"seq": target}),
        )

    def return_copy(g, target):
        return remote(hr_out.at[g], hr_in.at[g], hr_s.at[g], hr_r.at[g], {"seq": target})

    def key_copy(g, target):
        return remote(hk_out.at[g], hk_in.at[g], hk_s.at[g], hk_r.at[g], {"seq": target})

    def group(g, carry):
        bt_acc[...] = jnp.zeros_like(bt_acc)
        bn_acc[...] = jnp.zeros_like(bn_acc)

        def take_state(source, inner):
            for copy in state_copies(0, g, source, source):
                copy.wait_recv()
            bt_acc[...] += st_in[source, g, :DH].astype(f32)
            bn_acc[...] += rows_norm(st_in[source, g, DH:])
            return inner

        lax.fori_loop(0, place, take_state, 0)
        cum[g] = cum[g] + jnp.sum(bn_acc[...], axis=0, keepdims=True)
        running = bt_acc[...]
        for b in range(nb):
            stb[g, b] = running.astype(bf16)
            if b < nb - 1:
                running = running + pre[g, b]
        bt_acc[...] = jnp.zeros_like(bt_acc)
        bn_acc[...] = jnp.zeros_like(bn_acc)

        def block(lap, inner):
            b = nb - 1 - lap
            unit = g * nb + b
            here = pl.ds(b * WIN, WIN)
            span = pl.ds(b * WIN, 2 * WIN)
            cumb = cum[g, here][None]
            vw = vx[g, span]
            fkw = fkb[g, span]
            state = stb[g, b]
            back = jnp.concatenate([state, fkw], axis=0)
            fq = cube(fq_scr[unit])
            den = jnp.sum(fq * cumb, axis=-1, keepdims=True)
            above = den > 1.0
            inv = 1.0 / jnp.where(above, den, 1.0)
            fqn = fq * inv
            fqb = plain(fqn).astype(bf16)
            far = mm(fqb, back, 1, 1)
            lag = plain(jnp.where(lag_mask, cube(far[:, DH:]), 0.0)).astype(bf16)
            lin = mm(lag, vw) + far[:, :DH]
            go = (gp_scr[unit] + lin).astype(bf16)
            pull = cube(go.astype(f32) * lin)
            slope = jnp.where(above, -jnp.sum(pull, axis=-1, keepdims=True), 0.0)
            fqb_scr[unit] = fqb
            go_scr[unit] = go
            inv_scr[unit] = plain(jnp.broadcast_to(inv, (per, WIN, DH)))
            slope_scr[unit] = plain(jnp.broadcast_to(slope, (per, WIN, DH)))
            mix_scr[unit] = lag
            gt = mm(go, fqb, 0, 0)
            later_scr[unit] = bt_acc[...].astype(bf16)
            latern_scr[unit] = bn_acc[...]
            bt_acc[...] += gt
            bn_acc[...] += jnp.sum(plain(fqn * slope).reshape(head_rows // 8, 8, FEAT), axis=0)
            return inner

        lax.fori_loop(0, nb, block, 0, unroll=4)
        bt_out[g, :DH] = bt_acc[...].astype(bf16)
        bt_out[g, DH:] = norm_rows(bn_acc[...])

        def send_back(lap, inner):
            for copy in back_copies(g, place, place - 1 - lap):
                copy.start()
            return inner

        lax.fori_loop(0, place, send_back, 0)
        return carry

    lax.fori_loop(0, kvl, group, 0)

    def logit_grads(lap, carry):
        b = lap // kvl
        g = lap % kvl
        unit = g * nb + b
        here = pl.ds(b * WIN, WIN)
        fq = fq_scr[unit]
        go = go_scr[unit]
        gp = mm(go, vx[g, pl.ds(b * WIN, 2 * WIN)], 1, 1)
        gp_scr[unit] = gp
        gp = cube(gp)
        inv = inv_scr[unit]
        slope = slope_scr[unit]
        gin = plain(jnp.where(lag_mask, gp, 0.0)).astype(bf16)
        back = jnp.concatenate([stb[g, b], fkb[g, pl.ds(b * WIN, 2 * WIN)]], axis=0)
        gf = mm(jnp.concatenate([go, gin], axis=-1), back)
        up_side = plain(cube(gf[:, :DH]) + cube(slope) * cum[g, here, :DH][None]) * inv
        down_side = plain(cube(gf[:, DH:]) + cube(slope) * cum[g, here, DH:][None]) * inv
        dl = soft_pair_grad(fq[:, :DH], fq[:, DH:], up_side, down_side)
        dl_scr[unit] = dl
        gmq_acc[...] += mm(stacked(q_ref, g, b, 0, per), dl, 0, 0)
        gker = plain(jnp.where(lag_mask, gp + cube(slope), 0.0)).astype(bf16)
        later = later_scr[unit]
        gfk_acc[g, here] = (
            mm(gker, fqb_scr[unit], 0, 0)[:WIN]
            + mm(vx[g, here], later)
            + jnp.sum(latern_scr[unit], axis=0, keepdims=True)
        )
        return carry

    lax.fori_loop(0, kvl, logit_grads, 0, unroll=kvl)
    for g in range(kvl):
        hr_out[g] = gfk_acc[g, :WIN].astype(bf16)

        @pl.when(place > 0)
        def _():
            return_copy(g, place - 1).start()

    lax.fori_loop(kvl, kvl * nb, logit_grads, 0, unroll=2)

    def each_owner(first, last, visit):
        def one(c, carry):
            @pl.when(c != mine)
            def _():
                visit(c)

            return carry

        lax.fori_loop(first, last, one, 0, unroll=8)

    def part_copy(chunk):
        return remote(mg.at[chunk], mr.at[mine], mg_s, mg_r, peer(chunk))

    def total_copy(target):
        return remote(tot.at[mine], tot.at[mine], tot_s, tot_r, target)

    def span_copy(count, send, recv):
        refs = mr.at[pl.ds(0, count)]
        return remote(refs, refs, send, recv, peer((mine + 1) % team))

    def scatter(which, part):
        half = chunks // 2
        for c in range(half):
            mg[which * half + c] = part[c * crows : (c + 1) * crows].astype(bf16)
        each_owner(which * half, which * half + half, lambda c: part_copy(c).start())

    scatter(0, gmq_acc[...])

    def query_grads(lap, carry):
        b = lap // kvl
        g = lap % kvl
        unit = g * nb + b
        here = pl.ds(b * WIN, WIN)
        span = pl.ds(b * WIN, 2 * WIN)
        for h0 in range(0, per, per):
            part = slice(h0 * WIN, (h0 + per) * WIN)
            probs = p_scr[unit, part]
            gp = gp_scr[unit, part]
            ds = (probs * (gp - jnp.sum(probs * gp, axis=-1, keepdims=True)) * scale).astype(bf16)
            gq = mm(
                jnp.concatenate([dl_scr[unit, part], ds], axis=-1),
                jnp.concatenate([kq[...], kx[g, span]], axis=0),
            ).astype(bf16)
            for h in range(per):
                gq_ref[here, pl.ds(pl.multiple_of((g * per + h0 + h) * DH, DH), DH)] = gq[
                    h * WIN : (h + 1) * WIN
                ]
            dk_acc[g, span] += mm(ds, stacked(q_ref, g, b, h0, per), 0, 0)
            mixer = (probs + mix_scr[unit].astype(f32)).astype(bf16)
            dv_acc[g, span] += mm(mixer, go_scr[unit], 0, 0)
            dv_acc[g, here] += mm(fkb[g, here], later_scr[unit], 1, 1)
        return carry

    @pl.when(place == nseq - 1)
    def _():
        hr_in[...] = jnp.zeros_like(hr_in)
        hk_in[...] = jnp.zeros_like(hk_in)

    for g in range(kvl):

        def take_back(source, carry):
            for copy in back_copies(g, source, source):
                copy.wait_recv()
            far_acc[g] += bt_in[source, g, :DH].astype(f32)
            farn_acc[g] += rows_norm(bt_in[source, g, DH:])
            return carry

        far_acc[g] = jnp.zeros((DH, FEAT), f32)
        farn_acc[g] = jnp.zeros((8, FEAT), f32)
        lax.fori_loop(place + 2, nseq, take_back, 0)
        nears[kvl + g] = far_acc[g].astype(bf16)
        nearn[kvl + g] = farn_acc[g]

        @pl.when(place < nseq - 1)
        def _():
            take_back(place + 1, 0)
            return_copy(g, place + 1).wait_recv()

    gmk = jnp.zeros((DH, DH), f32)
    for g in range(kvl):
        near = far_acc[g].astype(bf16)
        nears[g] = near
        gfk = jnp.concatenate(
            [
                gfk_acc[g, WIN:]
                + mm(vx[g, WIN:rows], near)
                + jnp.sum(farn_acc[g], axis=0, keepdims=True),
                hr_in[g].astype(f32)
                + mm(vx[g, rows:], nears[kvl + g])
                + jnp.sum(nearn[kvl + g], axis=0, keepdims=True),
            ],
            axis=0,
        )
        dl = soft_pair_grad(
            fkx[g, WIN:, :DH], fkx[g, WIN:, DH:], gfk[:, :DH], gfk[:, DH:]
        )
        dk_scr[g] = dl
        gmk = gmk + mm(kx[g, WIN:], dl, 0, 0)
    gmk_acc[...] = gmk

    scatter(1, gmk_acc[...])
    lax.fori_loop(0, kvl, query_grads, 0, unroll=kvl)
    for g in range(kvl):
        hk_out[g, :, :DH] = dk_acc[g, :WIN].astype(bf16)
        hk_out[g, :, DH:] = dv_acc[g, :WIN].astype(bf16)

        @pl.when(place > 0)
        def _():
            key_copy(g, place - 1).start()


    lax.fori_loop(kvl, kvl * nb, query_grads, 0, unroll=2)

    for g in range(kvl):

        @pl.when(place < nseq - 1)
        def _():
            key_copy(g, place + 1).wait_recv()

        cols = slice(g * DH, (g + 1) * DH)
        gv = jnp.concatenate(
            [
                dv_acc[g, WIN:rows] + mm(fkb[g, WIN:rows], nears[g], 1, 1),
                dv_acc[g, rows:]
                + hk_in[g, :, DH:].astype(f32)
                + mm(fkb[g, rows:], nears[kvl + g], 1, 1),
            ],
            axis=0,
        )
        gv_ref[:, cols] = gv.astype(bf16)
        gkl = mm(dk_scr[g], mk, 1, 1)
        gk_ref[:tail, cols] = (dk_acc[g, WIN:rows] + gkl[:tail]).astype(bf16)
        gk_ref[tail:, cols] = (
            dk_acc[g, rows:] + gkl[tail:] + hk_in[g, :, :DH].astype(f32)
        ).astype(bf16)

    def as_owner(act, otherwise=None):
        if chunks == team:
            act()
            return
        pl.when(mine < chunks)(act)
        if otherwise is not None:
            pl.when(mine >= chunks)(otherwise)

    def total():
        span_copy(team - 1, mg_s, mg_r).wait_recv()
        mr[mine] = mg[mine]
        part = mr[0].astype(f32)
        for d in range(1, team):
            part = part + mr[d].astype(f32)
        tot[mine] = part.astype(bf16)

        each_peer(lambda device: total_copy(device).start())

    as_owner(total)
    @pl.when(place < nseq - 1)
    def _():
        halo_copy(place + 1).wait_send()

    for g in range(kvl):

        @pl.when(place < nseq - 1)
        def _():
            for copy in state_copies(0, g, place, place + 1):
                copy.wait_send()

        def far_sent(target, carry):
            for copy in state_copies(1, g, place, target):
                copy.wait_send()
            return carry

        lax.fori_loop(place + 2, nseq, far_sent, 0)

        @pl.when(place > 0)
        def _():
            return_copy(g, place - 1).wait_send()
            key_copy(g, place - 1).wait_send()

        def back_sent(lap, carry):
            for copy in back_copies(g, place, place - 1 - lap):
                copy.wait_send()
            return carry

        lax.fori_loop(0, place, back_sent, 0)

    as_owner(
        span_copy(chunks - 1, mg_s, mg_r).wait_send,
        span_copy(chunks, mg_s, mg_r).wait_send,
    )
    as_owner(
        span_copy(chunks - 1, tot_s, tot_r).wait_recv,
        span_copy(chunks, tot_s, tot_r).wait_recv,
    )
    for c in range(chunks):
        gm_ref[c * crows : (c + 1) * crows] = tot[c].astype(f32)

    as_owner(span_copy(team - 1, tot_s, tot_r).wait_send)


def hand_over(gq, gk, gv, gm, gq_out, gk_out, gv_out, gmq_out, gmk_out, put):
    writes = []
    for held, target in [(gq, gq_out), (gk, gk_out), (gv, gv_out), (gm.at[:DH], gmq_out), (gm.at[DH:], gmk_out)]:
        write = pltpu.make_async_copy(held, target, put.at[len(writes)])
        write.start()
        writes.append(write)
    for write in writes:
        write.wait()


def shards(nseq, nhead, queries, key_vecs, value_vecs, teacher_out, map_query, map_key):
    rows = queries.shape[0]
    kvl = key_vecs.shape[1] // DH
    per = QH // KVH
    nb = rows // WIN
    units = kvl * nb
    team = nseq * nhead
    chunks = min(team, 2 * DH // 16)
    crows = 2 * DH // chunks
    vm = pltpu.VMEM
    dma = pltpu.SemaphoreType.DMA
    scratch = [
        vm(queries.shape, bf16),
        vm(key_vecs.shape, bf16),
        vm(value_vecs.shape, bf16),
        vm(queries.shape, bf16),
        vm(map_query.shape, bf16),
        vm(map_key.shape, bf16),
        dma((6,)),
        vm((kvl, rows + WIN, DH), bf16),
        vm((kvl, rows + WIN, DH), bf16),
        vm((kvl, rows + WIN, FEAT), f32),
        vm((kvl, rows + WIN, FEAT), bf16),
        vm((kvl, rows, FEAT), f32),
        vm((kvl, nb - 1, DH, FEAT), f32),
        vm((kvl, nb, DH, FEAT), bf16),
        vm((DH, DH), bf16),
        vm((FEAT, FEAT), bf16),
        vm((units, per * WIN, 2 * WIN), f32),
        vm((units, per * WIN, FEAT), f32),
        vm((units, per * WIN, 2 * WIN), f32),
        vm((units, per * WIN, FEAT), bf16),
        vm((units, per * WIN, DH), bf16),
        vm((units, per * WIN, DH), bf16),
        vm((units, DH, FEAT), bf16),
        vm((units, 8, FEAT), f32),
        vm((units, per * WIN, DH), f32),
        vm((units, per * WIN, DH), f32),
        vm((units, per * WIN, DH), bf16),
        vm((kvl, rows, FEAT), f32),
        vm((kvl, rows + WIN, DH), f32),
        vm((kvl, rows + WIN, DH), f32),
        vm((kvl, rows, DH), bf16),
        vm((kvl, DH, FEAT), f32),
        vm((kvl, 8, FEAT), f32),
        vm((2 * kvl, DH, FEAT), bf16),
        vm((2 * kvl, 8, FEAT), f32),
        vm((DH, FEAT), f32),
        vm((8, FEAT), f32),
        vm((DH, DH), f32),
        vm((DH, DH), f32),
        vm((2 * kvl, WIN, DH), bf16),
        vm((2 * kvl, WIN, DH), bf16),
        vm((2, kvl, DH + 16, FEAT), bf16),
        vm((nseq, kvl, DH + 16, FEAT), bf16),
        vm((kvl, DH + 16, FEAT), bf16),
        vm((nseq, kvl, DH + 16, FEAT), bf16),
        vm((kvl, WIN, FEAT), bf16),
        vm((kvl, WIN, FEAT), bf16),
        vm((kvl, WIN, 2 * DH), bf16),
        vm((kvl, WIN, 2 * DH), bf16),
        vm((chunks, crows, DH), bf16),
        vm((team, crows, DH), bf16),
        vm((chunks, crows, DH), bf16),
        dma, dma,
        dma((kvl, nseq)), dma((kvl, nseq)), dma((kvl, nseq)), dma((kvl, nseq)),
        dma((kvl,)), dma((kvl,)), dma((kvl,)), dma((kvl,)),
        dma, dma, dma, dma,
    ]
    whole = pl.BlockSpec(memory_space=pltpu.VMEM)
    anywhere = pl.BlockSpec(memory_space=pl.ANY)
    queries, key_vecs, value_vecs, teacher_out, map_query, map_key = (
        pltpu.with_memory_space_constraint(x, pltpu.HBM)
        for x in (queries, key_vecs, value_vecs, teacher_out, map_query, map_key)
    )
    results = pl.pallas_call(
        functools.partial(kernel, nseq, nhead, rows, kvl, per),
        out_shape=(
            vm(queries.shape, bf16),
            vm(key_vecs.shape, bf16),
            vm(value_vecs.shape, bf16),
            vm((2 * DH, DH), f32),
        ),
        in_specs=[anywhere] * 6,
        out_specs=[whole, whole, whole, whole],
        scratch_shapes=scratch,
        compiler_params=pltpu.CompilerParams(
            collective_id=0, has_side_effects=True, vmem_limit_bytes=40 * 1024 * 1024
        ),
        name="transfer_step",
    )(queries, key_vecs, value_vecs, teacher_out, map_query, map_key)
    return pl.pallas_call(
        hand_over,
        out_shape=(
            jax.ShapeDtypeStruct(queries.shape, bf16),
            jax.ShapeDtypeStruct(key_vecs.shape, bf16),
            jax.ShapeDtypeStruct(value_vecs.shape, bf16),
            jax.ShapeDtypeStruct((DH, DH), f32),
            jax.ShapeDtypeStruct((DH, DH), f32),
        ),
        in_specs=[whole] * 4,
        out_specs=[anywhere] * 5,
        scratch_shapes=[dma((5,))],
        compiler_params=pltpu.CompilerParams(vmem_limit_bytes=1024 * 1024),
        name="hand_over",
    )(*results)


def solution(mesh):
    in_specs = (
        P(("grp", "seq"), "head"),
        P(("grp", "seq"), "head"),
        P(("grp", "seq"), "head"),
        P(("grp", "seq"), "head"),
        P(),
        P(),
    )
    out_specs = (
        P(("grp", "seq"), "head"),
        P(("grp", "seq"), "head"),
        P(("grp", "seq"), "head"),
        P("grp", None),
        P("grp", None),
    )
    body = functools.partial(shards, mesh.shape["seq"], mesh.shape["head"])
    return jax.shard_map(body, mesh=mesh, in_specs=in_specs, out_specs=out_specs, check_vma=False)
```

```python
import functools

import jax
import jax.numpy as jnp
from jax import lax
from jax.experimental import pallas as pl
from jax.experimental.pallas import tpu as pltpu
from jax.sharding import PartitionSpec as P

QH = 64
KVH = 8
DH = 128
WIN = 64
FEAT = 256
LOG2E = 1.4426950408889634

f32 = jnp.float32
bf16 = jnp.bfloat16
MESH = pl.DeviceIdType.MESH


def mm(a, b, ca=1, cb=0, precision=None):
    return lax.dot_general(
        a, b, (((ca,), (cb,)), ((), ())), preferred_element_type=f32, precision=precision
    )


def soft_pair(logits, ones):
    logits = logits * LOG2E
    up = jnp.exp2(logits - jnp.max(logits, axis=-1, keepdims=True))
    down = jnp.exp2(jnp.min(logits, axis=-1, keepdims=True) - logits)
    pair = jnp.concatenate([up, down], axis=-1)
    high = pair.astype(bf16)
    rest = (pair - high.astype(f32)).astype(bf16)
    return pair * (1.0 / (mm(high, ones) + mm(rest, ones)))


def norm_rows(partial):
    total = jnp.sum(partial, axis=0, keepdims=True)
    row = lax.broadcasted_iota(jnp.int32, (16, total.shape[1]), 0)
    out = jnp.zeros((16, total.shape[1]), f32)
    for n in range(3):
        piece = total.astype(bf16).astype(f32)
        out = jnp.where(row == n, piece, out)
        total = total - piece
    return out.astype(bf16)


def rows_norm(rows):
    rows = rows.astype(f32)
    return rows[:8] + rows[8:]


def soft_pair_grad(up, down, ga, gb):
    part_up = up * (ga - jnp.sum(up * ga, axis=-1, keepdims=True))
    part_down = down * (gb - jnp.sum(down * gb, axis=-1, keepdims=True))
    return (part_up - part_down).astype(bf16)


def kernel(
    nseq, nhead, rows, kvl, per,
    q_hbm, k_hbm, v_hbm, t_hbm, mq_hbm, mk_hbm,
    gq_ref, gk_ref, gv_ref, gm_ref,
    q_ref, k_ref, v_ref, t_ref, mq_ref, mk_ref, in_s,
    kx, vx, fkx, fkb, cum, pre, stb, kq, ones, p_scr, fq_scr, gp_scr,
    fqb_scr, go_scr, mix_scr, later_scr, latern_scr, inv_scr, slope_scr, dl_scr,
    gfk_acc, dv_acc, dk_acc, dk_scr, far_acc, farn_acc, nears, nearn, bt_acc, bn_acc, gmq_acc, gmk_acc,
    halo_out, halo_in, st_out, st_in, bt_out, bt_in, hr_out, hr_in, hk_out, hk_in, mg, mr, tot,
    halo_s, halo_r, st_s, st_r, bt_s, bt_r, hr_s, hr_r, hk_s, hk_r,
    mg_s, mg_r, tot_s, tot_r,
):
    nb = rows // WIN
    head_rows = per * WIN
    tail = rows - WIN
    chunks, _, _ = mg.shape
    crows = 2 * DH // chunks
    place = lax.axis_index("seq")
    lane = lax.axis_index("head")
    mine = place * nhead + lane
    team = nseq * nhead
    scale = DH ** (-0.5)

    def remote(src, dst, send, recv, device):
        return pltpu.make_async_remote_copy(
            src_ref=src, dst_ref=dst, send_sem=send, recv_sem=recv,
            device_id=device, device_id_type=MESH,
        )

    barrier = pltpu.get_barrier_semaphore()

    def peer(n):
        return {"seq": n // nhead, "head": n % nhead}

    loads = [
        pltpu.make_async_copy(source, held, in_s.at[n])
        for n, (source, held) in enumerate(
            [(k_hbm, k_ref), (v_hbm, v_ref), (mk_hbm, mk_ref), (q_hbm, q_ref), (mq_hbm, mq_ref), (t_hbm, t_ref)]
        )
    ]
    for load in loads:
        load.start()
    def each_peer(visit):
        for dh in range(nhead):
            h = (lane + dh) % nhead
            for ds in range(nseq):
                if ds or dh:
                    visit({"seq": (place + ds) % nseq, "head": h})

    each_peer(
        lambda device: pl.semaphore_signal(barrier, inc=1, device_id=device, device_id_type=MESH)
    )

    for load in loads[:3]:
        load.wait()

    for g in range(kvl):
        cols = slice(g * DH, (g + 1) * DH)
        kx[g, WIN:] = k_ref[:, cols]
        vx[g, WIN:] = v_ref[:, cols]
        halo_out[g] = k_ref[tail:, cols]
        halo_out[kvl + g] = v_ref[tail:, cols]

    def halo_copy(target):
        return remote(halo_out, halo_in, halo_s, halo_r, {"seq": target})

    def state_copies(slot, g, source, target):
        return (
            remote(st_out.at[slot, g], st_in.at[source, g], st_s.at[g, target], st_r.at[g, source],
                   {"seq": target}),
        )

    mk = mk_ref[...]
    side = lax.broadcasted_iota(jnp.int32, (FEAT, FEAT), 0) < DH
    ones[...] = (side == (lax.broadcasted_iota(jnp.int32, (FEAT, FEAT), 1) < DH)).astype(bf16)

    def key_features(keys):
        return soft_pair(mm(keys, mk), ones[...])

    for g in range(kvl):
        fk = key_features(kx[g, WIN:])
        fkx[g, WIN:] = fk
        fkl = fk.astype(bf16)
        fkb[g, WIN:] = fkl
        early = mm(vx[g, WIN:rows], fkl[:tail], 0, 0)
        late = mm(vx[g, rows:], fkl[tail:], 0, 0)
        st_out[0, g, :DH] = early.astype(bf16)
        st_out[1, g, :DH] = (early + late).astype(bf16)
        n_early = jnp.sum(fk[:tail].reshape(tail // 8, 8, FEAT), axis=0)
        n_late = jnp.sum(fk[tail:].reshape(WIN // 8, 8, FEAT), axis=0)
        st_out[0, g, DH:] = norm_rows(n_early)
        st_out[1, g, DH:] = norm_rows(n_early + n_late)

    pl.semaphore_wait(barrier, team - 1)

    @pl.when(place < nseq - 1)
    def _():
        halo_copy(place + 1).start()

    def send_states(g):
        @pl.when(place < nseq - 1)
        def _():
            for copy in state_copies(0, g, place, place + 1):
                copy.start()

        def send_far(target, carry):
            for copy in state_copies(1, g, place, target):
                copy.start()
            return carry

        lax.fori_loop(place + 2, nseq, send_far, 0)

    for g in range(kvl):
        send_states(g)

    ia = lax.broadcasted_iota(jnp.int32, (WIN, 2 * WIN), 0)
    ie = lax.broadcasted_iota(jnp.int32, (WIN, 2 * WIN), 1)
    lag_mask = (ie <= ia)[None]

    def stacked(ref, g, b, h0, hs):
        return jnp.concatenate(
            [
                ref[pl.ds(b * WIN, WIN), pl.ds(pl.multiple_of((g * per + h) * DH, DH), DH)]
                for h in range(h0, h0 + hs)
            ],
            axis=0,
        )

    def cube(x):
        return x.reshape(x.shape[0] // WIN, WIN, x.shape[-1])

    def plain(x):
        return x.reshape(x.shape[0] * WIN, x.shape[-1])

    def forward(lap, carry):
        b = (lap // kvl + 1) % nb
        g = lap % kvl
        unit = g * nb + b
        kw = kx[g, pl.ds(b * WIN, 2 * WIN)]
        first_key = jnp.where(place > 0, 0, WIN) - b * WIN
        seen = ((ie > ia) & (ie <= ia + WIN) & (ie >= first_key))[None]
        for h0 in range(0, per, per):
            part = slice(h0 * WIN, (h0 + per) * WIN)
            qs = stacked(q_ref, g, b, h0, per)
            both = mm(qs, jnp.concatenate([kq[...], kw], axis=0), 1, 1)
            fq_scr[unit, part] = soft_pair(both[:, :DH], ones[...])
            scores = jnp.where(seen, cube(both[:, DH:]) * (scale * LOG2E), -jnp.inf)
            weights = jnp.exp2(scores - jnp.max(scores, axis=-1, keepdims=True))
            weights = plain(weights).astype(bf16)
            probs = weights.astype(f32) * (1.0 / mm(weights, ones[:DH, :DH]))
            p_scr[unit, part] = probs
            mix = mm(probs.astype(bf16), vx[g, pl.ds(b * WIN, 2 * WIN)])
            gp_scr[unit, part] = mix - stacked(t_ref, g, b, 0, per).astype(f32)
        return carry

    loads[3].wait()
    loads[4].wait()
    loads[5].wait()
    kq[...] = mq_ref[...].T
    lax.fori_loop(0, kvl * (nb - 1), forward, 0, unroll=3)

    @pl.when(place > 0)
    def _():
        halo_copy(place - 1).wait_recv()

    @pl.when(place == 0)
    def _():
        halo_in[...] = jnp.zeros_like(halo_in)

    has_before = (place > 0).astype(f32)
    for g in range(kvl):
        kx[g, :WIN] = halo_in[g]
        vx[g, :WIN] = halo_in[kvl + g]
        fk = key_features(halo_in[g]) * has_before
        fkx[g, :WIN] = fk
        fkb[g, :WIN] = fk.astype(bf16)

    lax.fori_loop(kvl * (nb - 1), kvl * nb, forward, 0, unroll=kvl)

    ra = lax.broadcasted_iota(jnp.int32, (rows, rows), 0)
    re = lax.broadcasted_iota(jnp.int32, (rows, rows), 1)
    lower = (re <= ra).astype(bf16)
    for g in range(kvl):
        high = fkb[g, :rows]
        rest = (fkx[g, :rows] - high.astype(f32)).astype(bf16)
        cum[g] = mm(lower, high) + mm(lower, rest)
        for b in range(nb - 1):
            part = slice(b * WIN, (b + 1) * WIN)
            pre[g, b] = mm(vx[g, part], fkb[g, part], 0, 0)

    gmq_acc[...] = jnp.zeros_like(gmq_acc)
    dv_acc[...] = jnp.zeros_like(dv_acc)
    dk_acc[...] = jnp.zeros_like(dk_acc)

    def back_copies(g, source, target):
        return (
            remote(bt_out.at[g], bt_in.at[source, g], bt_s.at[g, target], bt_r.at[g, source],
                   {"seq": target}),
        )

    def return_copy(g, target):
        return remote(hr_out.at[g], hr_in.at[g], hr_s.at[g], hr_r.at[g], {"seq": target})

    def key_copy(g, target):
        return remote(hk_out.at[g], hk_in.at[g], hk_s.at[g], hk_r.at[g], {"seq": target})

    def group(g, carry):
        bt_acc[...] = jnp.zeros_like(bt_acc)
        bn_acc[...] = jnp.zeros_like(bn_acc)

        def take_state(source, inner):
            for copy in state_copies(0, g, source, source):
                copy.wait_recv()
            bt_acc[...] += st_in[source, g, :DH].astype(f32)
            bn_acc[...] += rows_norm(st_in[source, g, DH:])
            return inner

        lax.fori_loop(0, place, take_state, 0)
        cum[g] = cum[g] + jnp.sum(bn_acc[...], axis=0, keepdims=True)
        running = bt_acc[...]
        for b in range(nb):
            stb[g, b] = running.astype(bf16)
            if b < nb - 1:
                running = running + pre[g, b]
        bt_acc[...] = jnp.zeros_like(bt_acc)
        bn_acc[...] = jnp.zeros_like(bn_acc)

        def block(lap, inner):
            b = nb - 1 - lap
            unit = g * nb + b
            here = pl.ds(b * WIN, WIN)
            span = pl.ds(b * WIN, 2 * WIN)
            cumb = cum[g, here][None]
            vw = vx[g, span]
            fkw = fkb[g, span]
            state = stb[g, b]
            back = jnp.concatenate([state, fkw], axis=0)
            fq = cube(fq_scr[unit])
            den = jnp.sum(fq * cumb, axis=-1, keepdims=True)
            above = den > 1.0
            inv = 1.0 / jnp.where(above, den, 1.0)
            fqn = fq * inv
            fqb = plain(fqn).astype(bf16)
            far = mm(fqb, back, 1, 1)
            lag = plain(jnp.where(lag_mask, cube(far[:, DH:]), 0.0)).astype(bf16)
            lin = mm(lag, vw) + far[:, :DH]
            go = (gp_scr[unit] + lin).astype(bf16)
            pull = cube(go.astype(f32) * lin)
            slope = jnp.where(above, -jnp.sum(pull, axis=-1, keepdims=True), 0.0)
            fqb_scr[unit] = fqb
            go_scr[unit] = go
            inv_scr[unit] = plain(jnp.broadcast_to(inv, (per, WIN, DH)))
            slope_scr[unit] = plain(jnp.broadcast_to(slope, (per, WIN, DH)))
            mix_scr[unit] = lag
            gt = mm(go, fqb, 0, 0)
            later_scr[unit] = bt_acc[...].astype(bf16)
            latern_scr[unit] = bn_acc[...]
            bt_acc[...] += gt
            bn_acc[...] += jnp.sum(plain(fqn * slope).reshape(head_rows // 8, 8, FEAT), axis=0)
            return inner

        lax.fori_loop(0, nb, block, 0, unroll=4)
        bt_out[g, :DH] = bt_acc[...].astype(bf16)
        bt_out[g, DH:] = norm_rows(bn_acc[...])

        def send_back(lap, inner):
            for copy in back_copies(g, place, place - 1 - lap):
                copy.start()
            return inner

        lax.fori_loop(0, place, send_back, 0)
        return carry

    lax.fori_loop(0, kvl, group, 0)

    def logit_grads(lap, carry):
        b = lap // kvl
        g = lap % kvl
        unit = g * nb + b
        here = pl.ds(b * WIN, WIN)
        fq = fq_scr[unit]
        go = go_scr[unit]
        gp = mm(go, vx[g, pl.ds(b * WIN, 2 * WIN)], 1, 1)
        gp_scr[unit] = gp
        gp = cube(gp)
        inv = inv_scr[unit]
        slope = slope_scr[unit]
        gin = plain(jnp.where(lag_mask, gp, 0.0)).astype(bf16)
        back = jnp.concatenate([stb[g, b], fkb[g, pl.ds(b * WIN, 2 * WIN)]], axis=0)
        gf = mm(jnp.concatenate([go, gin], axis=-1), back)
        up_side = plain(cube(gf[:, :DH]) + cube(slope) * cum[g, here, :DH][None]) * inv
        down_side = plain(cube(gf[:, DH:]) + cube(slope) * cum[g, here, DH:][None]) * inv
        dl = soft_pair_grad(fq[:, :DH], fq[:, DH:], up_side, down_side)
        dl_scr[unit] = dl
        gmq_acc[...] += mm(stacked(q_ref, g, b, 0, per), dl, 0, 0)
        gker = plain(jnp.where(lag_mask, gp + cube(slope), 0.0)).astype(bf16)
        later = later_scr[unit]
        gfk_acc[g, here] = (
            mm(gker, fqb_scr[unit], 0, 0)[:WIN]
            + mm(vx[g, here], later)
            + jnp.sum(latern_scr[unit], axis=0, keepdims=True)
        )
        return carry

    lax.fori_loop(0, kvl, logit_grads, 0, unroll=kvl)
    for g in range(kvl):
        hr_out[g] = gfk_acc[g, :WIN].astype(bf16)

        @pl.when(place > 0)
        def _():
            return_copy(g, place - 1).start()

    lax.fori_loop(kvl, kvl * nb, logit_grads, 0, unroll=2)

    def each_owner(first, last, visit):
        def one(c, carry):
            @pl.when(c != mine)
            def _():
                visit(c)

            return carry

        lax.fori_loop(first, last, one, 0, unroll=8)

    def part_copy(chunk):
        return remote(mg.at[chunk], mr.at[mine], mg_s, mg_r, peer(chunk))

    def total_copy(target):
        return remote(tot.at[mine], tot.at[mine], tot_s, tot_r, target)

    def span_copy(count, send, recv):
        refs = mr.at[pl.ds(0, count)]
        return remote(refs, refs, send, recv, peer((mine + 1) % team))

    def scatter(which, part):
        half = chunks // 2
        for c in range(half):
            mg[which * half + c] = part[c * crows : (c + 1) * crows].astype(bf16)
        each_owner(which * half, which * half + half, lambda c: part_copy(c).start())

    scatter(0, gmq_acc[...])

    def query_grads(lap, carry):
        b = lap // kvl
        g = lap % kvl
        unit = g * nb + b
        here = pl.ds(b * WIN, WIN)
        span = pl.ds(b * WIN, 2 * WIN)
        for h0 in range(0, per, per):
            part = slice(h0 * WIN, (h0 + per) * WIN)
            probs = p_scr[unit, part]
            gp = gp_scr[unit, part]
            ds = (probs * (gp - jnp.sum(probs * gp, axis=-1, keepdims=True)) * scale).astype(bf16)
            gq = mm(
                jnp.concatenate([dl_scr[unit, part], ds], axis=-1),
                jnp.concatenate([kq[...], kx[g, span]], axis=0),
            ).astype(bf16)
            for h in range(per):
                gq_ref[here, pl.ds(pl.multiple_of((g * per + h0 + h) * DH, DH), DH)] = gq[
                    h * WIN : (h + 1) * WIN
                ]
            dk_acc[g, span] += mm(ds, stacked(q_ref, g, b, h0, per), 0, 0)
            mixer = (probs + mix_scr[unit].astype(f32)).astype(bf16)
            dv_acc[g, span] += mm(mixer, go_scr[unit], 0, 0)
            dv_acc[g, here] += mm(fkb[g, here], later_scr[unit], 1, 1)
        return carry

    @pl.when(place == nseq - 1)
    def _():
        hr_in[...] = jnp.zeros_like(hr_in)
        hk_in[...] = jnp.zeros_like(hk_in)

    for g in range(kvl):

        def take_back(source, carry):
            for copy in back_copies(g, source, source):
                copy.wait_recv()
            far_acc[g] += bt_in[source, g, :DH].astype(f32)
            farn_acc[g] += rows_norm(bt_in[source, g, DH:])
            return carry

        far_acc[g] = jnp.zeros((DH, FEAT), f32)
        farn_acc[g] = jnp.zeros((8, FEAT), f32)
        lax.fori_loop(place + 2, nseq, take_back, 0)
        nears[kvl + g] = far_acc[g].astype(bf16)
        nearn[kvl + g] = farn_acc[g]

        @pl.when(place < nseq - 1)
        def _():
            take_back(place + 1, 0)
            return_copy(g, place + 1).wait_recv()

    gmk = jnp.zeros((DH, DH), f32)
    for g in range(kvl):
        near = far_acc[g].astype(bf16)
        nears[g] = near
        gfk = jnp.concatenate(
            [
                gfk_acc[g, WIN:]
                + mm(vx[g, WIN:rows], near)
                + jnp.sum(farn_acc[g], axis=0, keepdims=True),
                hr_in[g].astype(f32)
                + mm(vx[g, rows:], nears[kvl + g])
                + jnp.sum(nearn[kvl + g], axis=0, keepdims=True),
            ],
            axis=0,
        )
        dl = soft_pair_grad(
            fkx[g, WIN:, :DH], fkx[g, WIN:, DH:], gfk[:, :DH], gfk[:, DH:]
        )
        dk_scr[g] = dl
        gmk = gmk + mm(kx[g, WIN:], dl, 0, 0)
    gmk_acc[...] = gmk

    scatter(1, gmk_acc[...])
    lax.fori_loop(0, kvl, query_grads, 0, unroll=kvl)
    for g in range(kvl):
        hk_out[g, :, :DH] = dk_acc[g, :WIN].astype(bf16)
        hk_out[g, :, DH:] = dv_acc[g, :WIN].astype(bf16)

        @pl.when(place > 0)
        def _():
            key_copy(g, place - 1).start()


    lax.fori_loop(kvl, kvl * nb, query_grads, 0, unroll=2)

    for g in range(kvl):

        @pl.when(place < nseq - 1)
        def _():
            key_copy(g, place + 1).wait_recv()

        cols = slice(g * DH, (g + 1) * DH)
        gv = jnp.concatenate(
            [
                dv_acc[g, WIN:rows] + mm(fkb[g, WIN:rows], nears[g], 1, 1),
                dv_acc[g, rows:]
                + hk_in[g, :, DH:].astype(f32)
                + mm(fkb[g, rows:], nears[kvl + g], 1, 1),
            ],
            axis=0,
        )
        gv_ref[:, cols] = gv.astype(bf16)
        gkl = mm(dk_scr[g], mk, 1, 1)
        gk_ref[:tail, cols] = (dk_acc[g, WIN:rows] + gkl[:tail]).astype(bf16)
        gk_ref[tail:, cols] = (
            dk_acc[g, rows:] + gkl[tail:] + hk_in[g, :, :DH].astype(f32)
        ).astype(bf16)

    def as_owner(act, otherwise=None):
        if chunks == team:
            act()
            return
        pl.when(mine < chunks)(act)
        if otherwise is not None:
            pl.when(mine >= chunks)(otherwise)

    def total():
        span_copy(team - 1, mg_s, mg_r).wait_recv()
        mr[mine] = mg[mine]
        part = mr[0].astype(f32)
        for d in range(1, team):
            part = part + mr[d].astype(f32)
        tot[mine] = part.astype(bf16)

        each_peer(lambda device: total_copy(device).start())

    as_owner(total)
    @pl.when(place < nseq - 1)
    def _():
        halo_copy(place + 1).wait_send()

    for g in range(kvl):

        @pl.when(place < nseq - 1)
        def _():
            for copy in state_copies(0, g, place, place + 1):
                copy.wait_send()

        def far_sent(target, carry):
            for copy in state_copies(1, g, place, target):
                copy.wait_send()
            return carry

        lax.fori_loop(place + 2, nseq, far_sent, 0)

        @pl.when(place > 0)
        def _():
            return_copy(g, place - 1).wait_send()
            key_copy(g, place - 1).wait_send()

        def back_sent(lap, carry):
            for copy in back_copies(g, place, place - 1 - lap):
                copy.wait_send()
            return carry

        lax.fori_loop(0, place, back_sent, 0)

    as_owner(
        span_copy(chunks - 1, mg_s, mg_r).wait_send,
        span_copy(chunks, mg_s, mg_r).wait_send,
    )
    as_owner(
        span_copy(chunks - 1, tot_s, tot_r).wait_recv,
        span_copy(chunks, tot_s, tot_r).wait_recv,
    )
    for c in range(chunks):
        gm_ref[c * crows : (c + 1) * crows] = tot[c].astype(f32)

    as_owner(span_copy(team - 1, tot_s, tot_r).wait_send)


def hand_over(gq, gk, gv, gm, gq_out, gk_out, gv_out, gmq_out, gmk_out, put):
    writes = []
    for held, target in [(gq, gq_out), (gk, gk_out), (gv, gv_out), (gm.at[:DH], gmq_out), (gm.at[DH:], gmk_out)]:
        write = pltpu.make_async_copy(held, target, put.at[len(writes)])
        write.start()
        writes.append(write)
    for write in writes:
        write.wait()


def shards(nseq, nhead, queries, key_vecs, value_vecs, teacher_out, map_query, map_key):
    rows = queries.shape[0]
    kvl = key_vecs.shape[1] // DH
    per = QH // KVH
    nb = rows // WIN
    units = kvl * nb
    team = nseq * nhead
    chunks = min(team, 2 * DH // 16)
    crows = 2 * DH // chunks
    vm = pltpu.VMEM
    dma = pltpu.SemaphoreType.DMA
    scratch = [
        vm(queries.shape, bf16),
        vm(key_vecs.shape, bf16),
        vm(value_vecs.shape, bf16),
        vm(queries.shape, bf16),
        vm(map_query.shape, bf16),
        vm(map_key.shape, bf16),
        dma((6,)),
        vm((kvl, rows + WIN, DH), bf16),
        vm((kvl, rows + WIN, DH), bf16),
        vm((kvl, rows + WIN, FEAT), f32),
        vm((kvl, rows + WIN, FEAT), bf16),
        vm((kvl, rows, FEAT), f32),
        vm((kvl, nb - 1, DH, FEAT), f32),
        vm((kvl, nb, DH, FEAT), bf16),
        vm((DH, DH), bf16),
        vm((FEAT, FEAT), bf16),
        vm((units, per * WIN, 2 * WIN), f32),
        vm((units, per * WIN, FEAT), f32),
        vm((units, per * WIN, 2 * WIN), f32),
        vm((units, per * WIN, FEAT), bf16),
        vm((units, per * WIN, DH), bf16),
        vm((units, per * WIN, DH), bf16),
        vm((units, DH, FEAT), bf16),
        vm((units, 8, FEAT), f32),
        vm((units, per * WIN, DH), f32),
        vm((units, per * WIN, DH), f32),
        vm((units, per * WIN, DH), bf16),
        vm((kvl, rows, FEAT), f32),
        vm((kvl, rows + WIN, DH), f32),
        vm((kvl, rows + WIN, DH), f32),
        vm((kvl, rows, DH), bf16),
        vm((kvl, DH, FEAT), f32),
        vm((kvl, 8, FEAT), f32),
        vm((2 * kvl, DH, FEAT), bf16),
        vm((2 * kvl, 8, FEAT), f32),
        vm((DH, FEAT), f32),
        vm((8, FEAT), f32),
        vm((DH, DH), f32),
        vm((DH, DH), f32),
        vm((2 * kvl, WIN, DH), bf16),
        vm((2 * kvl, WIN, DH), bf16),
        vm((2, kvl, DH + 16, FEAT), bf16),
        vm((nseq, kvl, DH + 16, FEAT), bf16),
        vm((kvl, DH + 16, FEAT), bf16),
        vm((nseq, kvl, DH + 16, FEAT), bf16),
        vm((kvl, WIN, FEAT), bf16),
        vm((kvl, WIN, FEAT), bf16),
        vm((kvl, WIN, 2 * DH), bf16),
        vm((kvl, WIN, 2 * DH), bf16),
        vm((chunks, crows, DH), bf16),
        vm((team, crows, DH), bf16),
        vm((chunks, crows, DH), bf16),
        dma, dma,
        dma((kvl, nseq)), dma((kvl, nseq)), dma((kvl, nseq)), dma((kvl, nseq)),
        dma((kvl,)), dma((kvl,)), dma((kvl,)), dma((kvl,)),
        dma, dma, dma, dma,
    ]
    whole = pl.BlockSpec(memory_space=pltpu.VMEM)
    anywhere = pl.BlockSpec(memory_space=pl.ANY)
    queries, key_vecs, value_vecs, teacher_out, map_query, map_key = (
        pltpu.with_memory_space_constraint(x, pltpu.HBM)
        for x in (queries, key_vecs, value_vecs, teacher_out, map_query, map_key)
    )
    results = pl.pallas_call(
        functools.partial(kernel, nseq, nhead, rows, kvl, per),
        out_shape=(
            vm(queries.shape, bf16),
            vm(key_vecs.shape, bf16),
            vm(value_vecs.shape, bf16),
            vm((2 * DH, DH), f32),
        ),
        in_specs=[anywhere] * 6,
        out_specs=[whole, whole, whole, whole],
        scratch_shapes=scratch,
        compiler_params=pltpu.CompilerParams(
            collective_id=0, has_side_effects=True, vmem_limit_bytes=40 * 1024 * 1024
        ),
        name="transfer_step",
    )(queries, key_vecs, value_vecs, teacher_out, map_query, map_key)
    return pl.pallas_call(
        hand_over,
        out_shape=(
            jax.ShapeDtypeStruct(queries.shape, bf16),
            jax.ShapeDtypeStruct(key_vecs.shape, bf16),
            jax.ShapeDtypeStruct(value_vecs.shape, bf16),
            jax.ShapeDtypeStruct((DH, DH), f32),
            jax.ShapeDtypeStruct((DH, DH), f32),
        ),
        in_specs=[whole] * 4,
        out_specs=[anywhere] * 5,
        scratch_shapes=[dma((5,))],
        compiler_params=pltpu.CompilerParams(vmem_limit_bytes=1024 * 1024),
        name="hand_over",
    )(*results)


def solution(mesh):
    in_specs = (
        P(("grp", "seq"), "head"),
        P(("grp", "seq"), "head"),
        P(("grp", "seq"), "head"),
        P(("grp", "seq"), "head"),
        P(),
        P(),
    )
    out_specs = (
        P(("grp", "seq"), "head"),
        P(("grp", "seq"), "head"),
        P(("grp", "seq"), "head"),
        P("grp", None),
        P("grp", None),
    )
    body = functools.partial(shards, mesh.shape["seq"], mesh.shape["head"])
    return jax.shard_map(body, mesh=mesh, in_specs=in_specs, out_specs=out_specs, check_vma=False)
```
